32 devices in a mesh: batch: 4 (over y, x), filt: 8 (over z, core).
Axes of the slice: x: 2, y: 2, z: 4, core: 2. Of those that a mesh axis runs over, the one named last changes fastest.
Arguments:
- images: bfloat16 [768, 3072], P(('batch', 'filt')), may hold values from -6 to 6
- labels: int32 [768], P(('batch', 'filt')), may hold values from 0 to 9
- partner: int32 [768], P(('batch', 'filt')), may hold values from 0 to 767, as said below
- valid_mask: int32 [768], P(('batch', 'filt')), may hold values from 0 to 1, as said below
- group_sizes: int32 [4, 8], replicated, may hold values from 1 to 185, as said below
- stem_weight: float32 [16, 27], replicated, may hold values from -1.25 to 1.25
- bridge_weight: float32 [640, 16], P('filt'), may hold values from -1.5 to 1.5
- conv_weight: float32 [2, 640, 9, 640], P(None, 'filt'), may hold values from -0.078125 to 0.078125
- norm_params: float32 [6, 640], P(None, 'filt'), may hold values from 0.5 to 1.5
- head_weight: float32 [10, 640], P(None, 'filt'), may hold values from -1 to 1
- head_bias: float32 [10], replicated, may hold values from -3 to 3
- stem_first: float32 [16, 27], replicated, may hold values from -4.7683716e-06 to 4.7683716e-06
- stem_second: float32 [16, 27], replicated, may hold values from 1.2540817e-12 to 2.002716e-11
- bridge_first: float32 [640, 16], P('filt'), may hold values from -9.536743e-07 to 9.536743e-07
- bridge_second: float32 [640, 16], P('filt'), may hold values from 5.016327e-14 to 8.010864e-13
- conv_first: float32 [2, 640, 9, 640], P(None, 'filt'), may hold values from -2.3841858e-06 to 2.3841858e-06
- conv_second: float32 [2, 640, 9, 640], P(None, 'filt'), may hold values from 3.5671658e-13 to 5.6966146e-12
- norm_first: float32 [6, 640], P(None, 'filt'), may hold values from -7.6293945e-06 to 7.6293945e-06
- norm_second: float32 [6, 640], P(None, 'filt'), may hold values from 3.2104493e-12 to 5.126953e-11
- head_first: float32 [10, 640], P(None, 'filt'), may hold values from -7.6293945e-06 to 7.6293945e-06
- head_second: float32 [10, 640], P(None, 'filt'), may hold values from 3.2104493e-12 to 5.126953e-11
- bias_first: float32 [10], replicated, may hold values from -2.2888184e-05 to 2.2888184e-05
- bias_second: float32 [10], replicated, may hold values from 3.5671657e-11 to 5.696615e-10
Outputs:
- stem_weight_new: float32 [16, 27], replicated
- stem_first_new: float32 [16, 27], replicated
- stem_second_new: float32 [16, 27], replicated
- bridge_weight_new: float32 [640, 16], P('filt')
- bridge_first_new: float32 [640, 16], P('filt')
- bridge_second_new: float32 [640, 16], P('filt')
- conv_weight_new: float32 [2, 640, 9, 640], P(None, 'filt')
- conv_first_new: float32 [2, 640, 9, 640], P(None, 'filt')
- conv_second_new: float32 [2, 640, 9, 640], P(None, 'filt')
- norm_params_new: float32 [6, 640], P(None, 'filt')
- norm_first_new: float32 [6, 640], P(None, 'filt')
- norm_second_new: float32 [6, 640], P(None, 'filt')
- head_weight_new: float32 [10, 640], P(None, 'filt')
- head_first_new: float32 [10, 640], P(None, 'filt')
- head_second_new: float32 [10, 640], P(None, 'filt')
- head_bias_new: float32 [10], replicated
- bias_first_new: float32 [10], replicated
- bias_second_new: float32 [10], replicated
- grad_norm: float32 [], replicated
- loss: float32 [], replicated
The draws below stay inside these ranges and needn't reach their ends.
Inputs may be any that keep to these rules, and one draw needn't show every extreme that they name: `group_sizes`: row b lists the sizes of the 8 groups of batch shard b, laid one after another from the shard's first slot; a shard's sizes sum to at most 192, and in one shard exactly. `valid_mask`: slots after a shard's groups hold 0; the first slot of every group holds 1, and so does image 768 - 1. `partner`: each entry is the index of an image whose valid_mask is 1.
All inputs are finite; a program needn't handle non-finite values.
Results may differ from the reference program's by a relative error of at most 0.008.
The reference program's roundings to bfloat16 on the way count: a program that leaves them out, or rounds other values in their place, can miss the bound.
Values may be sent and summed in bfloat16 or wider, within the bound.
A program may use at most 256 MiB of HBM per device.

```python
import math
import jax
import jax.numpy as jnp
from jax import lax

C = 640
STEM = 16
CLASSES = 10
IMG_DEV = 24
GROUPS = 8
STEP = 8
IMAGES = 768
N_BATCH = 4
N_FILT = 8


def shard_plan(key):
    base_key = jax.random.fold_in(key, 4242)
    key_list = jax.random.split(base_key, 5)
    capacity = IMG_DEV * N_FILT
    shard_index = jnp.arange(N_BATCH)
    shard_totals = capacity // 2 + jax.random.randint(key_list[1], (N_BATCH,), 0, capacity // 2 + 1)
    shard_totals = jnp.where(shard_index == N_BATCH - 1, capacity, shard_totals)
    group_powers = jnp.left_shift(jnp.int32(1), jax.random.randint(key_list[2], (N_BATCH, GROUPS), 0, 6))
    spare_slots = shard_totals - GROUPS
    sizes_drawn = 1 + spare_slots[:, None] * group_powers // jnp.sum(group_powers, axis=1, keepdims=True)
    sizes_drawn = sizes_drawn.at[:, GROUPS - 1].add(shard_totals - jnp.sum(sizes_drawn, axis=1))
    forced_row = jnp.where(jnp.arange(GROUPS) == 0, capacity - GROUPS + 1, 1)
    sizes_drawn = jnp.where(shard_index[:, None] == N_BATCH - 1, forced_row[None, :], sizes_drawn)
    group_ends = jnp.cumsum(sizes_drawn, axis=1)
    group_starts = group_ends - sizes_drawn
    slot_index = jnp.arange(capacity)
    group_head = jnp.any(slot_index[None, :, None] == group_starts[:, None, :], axis=2)
    random_kept = jax.random.randint(key_list[3], (N_BATCH, capacity), 0, 8) > 0
    inside = slot_index[None, :] < shard_totals[:, None]
    valid_drawn = (inside & (group_head | random_kept)).astype(jnp.int32)
    return (sizes_drawn.astype(jnp.int32), valid_drawn.reshape(-1), key_list[4])


def draw_group_sizes(key, part):
    return shard_plan(key)[0]


def draw_valid_mask(key, part):
    return shard_plan(key)[1]


def draw_partner(key, part):
    plan_parts = shard_plan(key)
    valid_drawn = plan_parts[1]
    order = jnp.argsort(1 - valid_drawn, stable=True)
    living = jnp.sum(valid_drawn)
    picks = jax.random.randint(plan_parts[2], (IMAGES,), 0, living)
    chosen = order[picks].astype(jnp.int32)
    return chosen.at[0].set(0).at[1].set(IMAGES - 1)


def plant(array, key, smallest, high):
    dims = array.shape
    spot = [jax.random.randint(jax.random.fold_in(key, axis), (), 0, dims[axis]) for axis in range(len(dims))]
    array = array.at[tuple(spot)].set(smallest)
    longest = dims.index(max(dims))
    spot[longest] = (spot[longest] + 1) % dims[longest]
    return array.at[tuple(spot)].set(high)


def steps_of(own_key, shape, cuts, smallest, largest):
    def one(dim, parts):
        steps = jax.random.uniform(jax.random.fold_in(jax.random.fold_in(own_key, 6), dim), (parts,), jnp.float32, smallest / len(cuts), largest / len(cuts))
        return jnp.repeat(jnp.exp(steps), shape[dim] // parts).reshape((-1,) + (1,) * (len(shape) - dim - 1))

    factor_of = one(*cuts[0])
    for cut in cuts[1:]:
        factor_of = factor_of * one(*cut)
    return factor_of


def gaussian(key, dims, scale, bound, cuts=(), kind=jnp.bfloat16):
    values = scale * jax.random.normal(key, dims, jnp.float32)
    if cuts:
        values = values * steps_of(key, dims, cuts, -0.22, 0.18)
    return jnp.clip(values, -bound, bound).astype(kind)


def setup_inputs(seed: int = 0) -> dict:
    streams_of = jax.random.split(jax.random.key(seed), 24)
    return {
        "images": gaussian(streams_of[0], (IMAGES, 3072), 1.0, 6.0, ((0, 32),)),
        "labels": plant(jax.random.randint(streams_of[1], (IMAGES,), 0, CLASSES), jax.random.fold_in(streams_of[1], 1), 0, CLASSES - 1).astype(jnp.int32),
        "partner": draw_partner(jax.random.fold_in(streams_of[23], 71), 0),
        "valid_mask": draw_valid_mask(jax.random.fold_in(streams_of[23], 71), 0),
        "group_sizes": draw_group_sizes(jax.random.fold_in(streams_of[23], 71), 0),
        "stem_weight": gaussian(streams_of[5], (STEM, 27), 27 ** -0.5, 1.25, (), jnp.float32),
        "bridge_weight": gaussian(streams_of[6], (C, STEM), STEM ** -0.5, 1.5, ((0, 8),), jnp.float32),
        "conv_weight": gaussian(streams_of[7], (2, C, 9, C), (9 * C) ** -0.5, 0.078125, ((1, 8),), jnp.float32),
        "norm_params": jnp.clip(1.0 + 0.1 * jax.random.normal(streams_of[8], (6, C), jnp.float32), 0.5, 1.5),
        "head_weight": gaussian(streams_of[9], (CLASSES, C), (C // 16) ** -0.5, 1.0, ((1, 8),), jnp.float32),
        "head_bias": gaussian(streams_of[10], (CLASSES,), 0.5, 3.0, (), jnp.float32),
        "stem_first": gaussian(streams_of[11], (STEM, 27), (0.111 * 0.3 * (18 * C * C) ** -0.5 / 16), 4.76837158203125e-06, (), jnp.float32),
        "stem_second": jnp.clip(jnp.exp(jax.random.uniform(streams_of[12], (STEM, 27), jnp.float32, math.log(1.2540816909240027e-12), math.log(2.0027160485547313e-11))), 1.2540816909240027e-12, 2.0027160485547313e-11),
        "bridge_first": gaussian(streams_of[13], (C, STEM), (0.111 * 0.03 * (18 * C * C) ** -0.5 / 8), 9.5367431640625e-07, ((0, 8),), jnp.float32),
        "bridge_second": jnp.clip(jnp.exp(math.log(8.010864107482751e-13) - 2.7706857 * jax.random.uniform(streams_of[14], (C, STEM), jnp.float32) ** steps_of(streams_of[14], (C, STEM), ((0, 8),), -0.2, 0.2)), 5.016326980536445e-14, 8.010864107482751e-13),
        "conv_first": gaussian(streams_of[15], (2, C, 9, C), (0.111 * 0.01 * (18 * C * C) ** -0.5), 2.384185791015625e-06, ((1, 8),), jnp.float32),
        "conv_second": jnp.clip(jnp.exp(math.log(5.696614620992468e-12) - 2.77068577 * jax.random.uniform(streams_of[16], (2, C, 9, C), jnp.float32) ** steps_of(streams_of[16], (2, C, 9, C), ((1, 8),), -0.2, 0.2)), 3.5671658227091896e-13, 5.696614620992468e-12),
        "norm_first": gaussian(streams_of[17], (6, C), (0.111 * 0.03 * (18 * C * C) ** -0.5), 7.62939453125e-06, ((1, 8),), jnp.float32),
        "norm_second": jnp.clip(jnp.exp(math.log(5.126953028788961e-11) - 2.7706857 * jax.random.uniform(streams_of[18], (6, C), jnp.float32) ** steps_of(streams_of[18], (6, C), ((1, 8),), -0.2, 0.2)), 3.210449267543325e-12, 5.126953028788961e-11),
        "head_first": gaussian(streams_of[19], (CLASSES, C), (0.111 * 0.03 * (18 * C * C) ** -0.5), 7.62939453125e-06, ((1, 8),), jnp.float32),
        "head_second": jnp.clip(jnp.exp(math.log(5.126953028788961e-11) - 2.7706857 * jax.random.uniform(streams_of[20], (CLASSES, C), jnp.float32) ** steps_of(streams_of[20], (CLASSES, C), ((1, 8),), -0.2, 0.2)), 3.210449267543325e-12, 5.126953028788961e-11),
        "bias_first": gaussian(streams_of[21], (CLASSES,), (0.111 * 0.1 * (18 * C * C) ** -0.5), 2.288818359375e-05, (), jnp.float32),
        "bias_second": jnp.clip(jnp.exp(jax.random.uniform(streams_of[22], (CLASSES,), jnp.float32, math.log(3.567165660078864e-11), math.log(5.69661484650652e-10))), 3.567165660078864e-11, 5.69661484650652e-10),
    }


@jax.custom_vjp
def low(v):
    return lax.optimization_barrier(v.astype(jnp.bfloat16)).astype(jnp.float32)

@jax.custom_vjp
def low_back(v):
    return v

def low_keep(v):
    return (low(v), None)

def low_pass(kept, output_gradient):
    return (output_gradient,)

def back_keep(v):
    return (v, None)

def back_low(kept, output_gradient):
    return (low(output_gradient),)
low.defvjp(low_keep, low_pass)
low_back.defvjp(back_keep, back_low)
highest = lax.Precision.HIGHEST
beta_one = 0.9
beta_two = 0.95
adam_eps = 1e-08
norm_epsilon = 1e-05
clip_norm = 0.01
own_share = 0.7

def make_patches(images):
    number = images.shape[0]
    grid = images.reshape(number, 3, 32, 32)
    padded = jnp.pad(grid, ((0, 0), (0, 0), (1, 1), (1, 1)))
    pieces = [padded[:, :, row_off:row_off + 29:4, col_off:col_off + 29:4] for row_off in range(3) for col_off in range(3)]
    stacked = jnp.stack(pieces, axis=2)
    return jnp.transpose(stacked, (1, 2, 0, 3, 4)).reshape(27, number * 64)

def shifted(feature_field):
    width, rows = feature_field.shape
    grid = feature_field.reshape(width, rows // 64, 8, 8)
    padded = jnp.pad(grid, ((0, 0), (0, 0), (1, 1), (1, 1)))
    pieces = [padded[:, :, row_off:row_off + 8, col_off:col_off + 8] for row_off in range(3) for col_off in range(3)]
    return jnp.stack(pieces, axis=0).reshape(9, width, rows)

def image_weights(valid_mask, group_sizes):
    shards, groups = group_sizes.shape
    capacity = valid_mask.shape[0] // shards
    group_ends = jnp.cumsum(group_sizes, axis=1)
    slot_index = jnp.arange(capacity, dtype=jnp.int32)
    member = lax.optimization_barrier(jnp.sum((slot_index[None, :, None] >= group_ends[:, None, :]).astype(jnp.int32), axis=2))
    member = jnp.minimum(member, groups - 1)
    chosen = (member[:, :, None] == jnp.arange(groups, dtype=jnp.int32)[None, None, :]).astype(jnp.float32)
    sizes_each = lax.optimization_barrier(jnp.sum(chosen * group_sizes[:, None, :].astype(jnp.float32), axis=2))
    return valid_mask.astype(jnp.float32) / sizes_each.reshape(-1)

def norm_relu(feature_field, norm_gain, norm_shift, row_validity_mask, valid_count):
    batch_mean = lax.optimization_barrier(jnp.sum(feature_field * row_validity_mask, axis=1)) / valid_count
    centered_input = feature_field - batch_mean[:, None]
    batch_variance = lax.optimization_barrier(jnp.sum(centered_input * centered_input * row_validity_mask, axis=1)) / valid_count
    normalized_input = centered_input * lax.rsqrt(batch_variance + norm_epsilon)[:, None]
    return jnp.maximum(norm_gain[:, None] * normalized_input + norm_shift[:, None], 0.0)

def conv(feature_field, weight):
    return jnp.einsum('otc,tcr->or', weight, shifted(feature_field), precision=highest)

def forward(params, patch, row_validity_mask, valid_count, image_weight, total, target):
    stem_weight, bridge_weight, conv_weight, norm_params, head_weight, head_bias = params
    stem = low(low_back(jnp.dot(low(stem_weight), patch, precision=highest)))
    base = low_back(jnp.dot(low(bridge_weight), stem, precision=highest))
    first = low(norm_relu(base, norm_params[0], norm_params[1], row_validity_mask, valid_count))
    inner = low_back(conv(first, low(conv_weight[0])))
    second = low(norm_relu(inner, norm_params[2], norm_params[3], row_validity_mask, valid_count))
    branch = low_back(conv(second, low(conv_weight[1])))
    final = norm_relu(base + branch, norm_params[4], norm_params[5], row_validity_mask, valid_count)
    pooled = low(lax.optimization_barrier(jnp.mean(final.reshape(final.shape[0], -1, 64), axis=2)))
    logits = low_back(jnp.dot(low(head_weight), pooled, precision=highest) + head_bias[:, None])
    moved = logits - lax.optimization_barrier(jnp.max(logits, axis=0, keepdims=True))
    logp = moved - jnp.log(lax.optimization_barrier(jnp.sum(jnp.exp(moved), axis=0, keepdims=True)))
    return -jnp.sum(image_weight * lax.optimization_barrier(jnp.sum(target * logp, axis=0))) / total

def adam_step(weight, output_gradient, first, second, rate, shrink, factor):
    clipped = output_gradient * factor
    first = beta_one * first + (1.0 - beta_one) * clipped
    second = beta_two * second + (1.0 - beta_two) * clipped * clipped
    ahead = first / (1.0 - beta_one ** STEP)
    behind = second / (1.0 - beta_two ** STEP)
    return (weight - rate * (ahead / (jnp.sqrt(behind) + adam_eps) + shrink * weight), first, second)

def reference(images, labels, partner, valid_mask, group_sizes, stem_weight, bridge_weight, conv_weight, norm_params, head_weight, head_bias, stem_first, stem_second, bridge_first, bridge_second, conv_first, conv_second, norm_first, norm_second, head_first, head_second, bias_first, bias_second):
    patch = make_patches(images).astype(jnp.float32)
    image_weight = image_weights(valid_mask, group_sizes)
    total = jnp.sum(image_weight)
    valid_count = 64.0 * jnp.sum(valid_mask.astype(jnp.float32))
    row_validity_mask = jnp.repeat(valid_mask.astype(jnp.float32), 64)
    classes = jnp.arange(head_bias.shape[0], dtype=jnp.int32)
    partner_labels = labels[partner]
    target = own_share * (labels[None, :] == classes[:, None]).astype(jnp.float32) + (1.0 - own_share) * (partner_labels[None, :] == classes[:, None]).astype(jnp.float32)
    params = (stem_weight, bridge_weight, conv_weight, norm_params, head_weight, head_bias)

    def objective(*weights):
        return forward(weights, patch, row_validity_mask, valid_count, image_weight, total, target)
    loss, pullback = jax.vjp(objective, *params)
    grads = pullback(jnp.ones_like(loss))
    grad_norm = jnp.sqrt(sum((jnp.sum(output_gradient * output_gradient) for output_gradient in grads)))
    factor = clip_norm / jnp.maximum(grad_norm, clip_norm)
    stem_new = adam_step(stem_weight, grads[0], stem_first, stem_second, 0.5, 0.05, factor)
    bridge_new = adam_step(bridge_weight, grads[1], bridge_first, bridge_second, 0.6, 0.05, factor)
    conv_new = adam_step(conv_weight, grads[2], conv_first, conv_second, 0.033, 0.05, factor)
    norm_new = adam_step(norm_params, grads[3], norm_first, norm_second, 0.5, 0.0, factor)
    head_new = adam_step(head_weight, grads[4], head_first, head_second, 0.1, 0.05, factor)
    bias_new = adam_step(head_bias, grads[5], bias_first, bias_second, 0.5, 0.0, factor)
    return (stem_new[0], stem_new[1], stem_new[2], bridge_new[0], bridge_new[1], bridge_new[2], conv_new[0], conv_new[1], conv_new[2], norm_new[0], norm_new[1], norm_new[2], head_new[0], head_new[1], head_new[2], bias_new[0], bias_new[1], bias_new[2], grad_norm, loss)
```

```python
import jax
import jax.numpy as jnp
from jax import lax
from jax.experimental import pallas as pl
from jax.experimental.pallas import tpu as pltpu
from jax.sharding import PartitionSpec as P

STEP = 8

beta_one = 0.9
beta_two = 0.95
adam_eps = 1e-08
norm_epsilon = 1e-05
clip_norm = 0.01
own_share = 0.7

MESH = pl.DeviceIdType.MESH
bf16 = jnp.bfloat16
f32 = jnp.float32
LINE = bf16
NB, NF, NZ, NDEV, NCHIP = 4, 8, 4, 32, 16
C, IMG, ROWS = 640, 24, 1536
BLK = 8 * IMG
AC = (((1,), (1,)), ((), ()))
CC = (((0,), (0,)), ((), ()))


def iota(shape, dim):
    return lax.broadcasted_iota(jnp.int32, shape, dim)


def wide(row5):
    return jnp.concatenate([row5[k : k + 1, :] for k in range(5)], axis=1)


def column(row, n):
    eye = iota((n, n), 0) == iota((n, n), 1)
    return jnp.sum(jnp.where(eye, jnp.broadcast_to(row, (n, n)), 0.0), axis=1, keepdims=True)


class Place:
    def __init__(self):
        self.b = lax.axis_index("batch")
        self.f = lax.axis_index("filt")
        self.z = self.f // 2
        self.c = lax.rem(self.f, 2)
        self.me = self.b * NF + self.f
        self.chip = self.b * NZ + self.z
        self.xn = self.b + 1 - 2 * lax.rem(self.b, 2)
        self.yn = lax.rem(self.b + 2, NB)
        self.dn = (NB - 1) - self.b
        self.sib = self.f + 1 - 2 * self.c


def remote(src, dst, ssem, rsem, b, f):
    return pltpu.make_async_remote_copy(
        src_ref=src, dst_ref=dst, send_sem=ssem, recv_sem=rsem, device_id=(b, f), device_id_type=MESH
    )


def greet(p):
    sem = pltpu.get_barrier_semaphore()

    def hello(i, carry):
        to = lax.rem(p.me + i, NDEV)
        pl.semaphore_signal(
            sem, inc=1, device_id=(to // NF, lax.rem(to, NF)), device_id_type=MESH
        )
        return carry

    lax.fori_loop(1, NDEV, hello, 0)


def met():
    pl.semaphore_wait(pltpu.get_barrier_semaphore(), NDEV - 1)


class Exchange:
    def __init__(self, p, slots, sibs, ssem, rsem, psem, qsem):
        self.p, self.slots, self.sibs = p, slots, sibs
        self.ssem, self.rsem, self.psem, self.qsem = ssem, rsem, psem, qsem

    def mine(self, e):
        return self.slots.at[e, self.p.chip]

    def send(self, e):
        p = self.p
        mine = self.mine(e)

        def one(i, carry):
            to = lax.rem(p.chip + i, NCHIP)
            remote(
                mine, mine, self.ssem.at[e], self.rsem.at[e], to // NZ, 2 * lax.rem(to, NZ) + p.c
            ).start()
            return carry

        lax.fori_loop(1, NCHIP, one, 0)

    def wait(self, e):
        p = self.p
        rest = self.slots.at[e, 0 : NCHIP - 1]
        remote(rest, rest, self.ssem.at[e], self.rsem.at[e], p.b, p.sib).wait()

    def swap(self, e, value):
        p = self.p
        self.sibs[e, 0] = value
        copy = remote(
            self.sibs.at[e, 0], self.sibs.at[e, 1], self.psem.at[e], self.qsem.at[e], p.b, p.sib
        )
        copy.start()
        copy.wait()
        return self.sibs[e, 1]

    def total(self, e):
        self.wait(e)
        own = jnp.sum(self.slots[e], axis=0)
        return own + self.swap(e, own)


def put_row(slot, row, value):
    for k in range(5):
        slot[row + k : row + k + 1, :] = value[:, 128 * k : 128 * k + 128]


def put_spare(slot, value):
    for k, row in enumerate((5, 6, 7, 13, 14)):
        slot[row : row + 1, :] = value[:, 128 * k : 128 * k + 128]


def spare(rows):
    return wide(jnp.concatenate([rows[5:8], rows[13:15]], axis=0))


def local_stats(src, mask, count, slot):
    def total(j, acc):
        x = src[pl.ds(pl.multiple_of(j * BLK, BLK), BLK), :]
        m = jnp.concatenate([mask[...]] * 5, axis=1)
        return acc + jnp.sum((x * m).reshape(BLK // 8, 8, C), axis=0)

    acc = lax.fori_loop(0, 8, total, jnp.zeros((8, C), f32))
    own_sum = jnp.sum(acc, axis=0, keepdims=True)
    own_mean = own_sum / jnp.maximum(count, 1.0)

    def squares(j, acc):
        x = src[pl.ds(pl.multiple_of(j * BLK, BLK), BLK), :]
        m = jnp.concatenate([mask[...]] * 5, axis=1)
        d = x - own_mean
        return acc + jnp.sum((d * d * m).reshape(BLK // 8, 8, C), axis=0)

    acc = lax.fori_loop(0, 8, squares, jnp.zeros((8, C), f32))
    put_row(slot, 0, own_sum)
    put_row(slot, 8, jnp.sum(acc, axis=0, keepdims=True))


def joint_stats(ex, e):
    ex.wait(e)
    every = ex.slots[e]
    n = ex.slots[0, :, 5:6, :]
    sums = every[:, 0:5, :]
    n_own, s_own = jnp.sum(n, axis=0), jnp.sum(sums, axis=0)
    m_own = s_own / jnp.maximum(n_own, 1.0)
    off = sums / jnp.maximum(n, 1.0) - m_own[None]
    q_own = jnp.sum(every[:, 8:13, :] + n * off * off, axis=0)
    rest = jnp.sum(every[:, 5:8, :], axis=0)
    more = jnp.sum(every[:, 13:16, :], axis=0)
    got = ex.swap(e, jnp.concatenate([s_own, rest, q_own, more], axis=0))
    n_sib = ex.sibs[0, 1, 5:6, :]
    s_sib, q_sib = got[0:5], got[8:13]
    count = n_own + n_sib
    mean = (s_own + s_sib) / count
    a, b = m_own - mean, s_sib / jnp.maximum(n_sib, 1.0) - mean
    spread = ((q_own + q_sib) + (n_own * a * a + n_sib * b * b)) / count
    return wide(mean), wide(lax.rsqrt(spread + norm_epsilon)), spare(got + jnp.concatenate([s_own, rest, q_own, more], axis=0))


def spread_rows(S, j, x):
    at = pl.ds(pl.multiple_of((j + 1) * BLK, BLK), BLK)
    gap = jnp.zeros((IMG, C), f32)
    S[0, at, :] = jnp.concatenate([gap, x[: BLK - IMG]], axis=0).astype(bf16)
    S[1, at, :] = x.astype(bf16)
    S[2, at, :] = jnp.concatenate([x[IMG:], gap], axis=0).astype(bf16)


def conv_rows(S, W, k, r0, M):
    acc = None
    for u in range(3):
        lhs = jnp.concatenate([S[u, pl.ds(r0 + v * BLK, M), :] for v in range(3)], axis=1)
        rhs = jnp.concatenate(
            [
                jnp.concatenate(
                    [W[k, u, z, c, v * 80 : v * 80 + 80, :] for z in range(NZ) for c in range(2)], axis=0
                )
                for v in range(3)
            ],
            axis=1,
        )
        d = lax.dot_general(lhs, rhs, AC, preferred_element_type=f32)
        acc = d if acc is None else acc + d
    return acc


class Gather:
    def __init__(self, p, W, zs, zr, xs, xr, ds, dr):
        self.p, self.W = p, W
        self.zs, self.zr, self.xs, self.xr, self.ds, self.dr = zs, zr, xs, xr, ds, dr

    def part(self, s, z, b, row, n):
        return self.W.at[
            s // 3, lax.rem(s, 3), z, self.p.c, pl.ds(pl.multiple_of(b * 64 + row, 32), n), :
        ]

    def zcopy(self, s, i):
        p = self.p
        mine = self.part(s, p.z, p.b, 0, 64)
        to = lax.rem(p.z + i, NZ)
        return remote(mine, mine, self.zs.at[s, i], self.zr.at[s, i], p.b, 2 * to + p.c)

    def zsend(self, s):
        for i in (2, 1, 3):
            self.zcopy(s, i).start()

    def xcopy(self, s, i, d):
        p = self.p
        z = lax.rem(p.z + NZ - i, NZ)
        b, row, n, to = ((p.b, 0, 64, p.xn), (p.b, 0, 64, p.yn), (p.xn, 0, 32, p.yn), (p.yn, 32, 32, p.xn))[d]
        part = self.part(s, z, b, row, n)
        at = 3 * d + i - 1
        return remote(part, part, self.xs.at[s, at], self.xr.at[s, at], to, p.f)

    def relay(self, s):
        for i in range(1, NZ):
            self.zcopy(s, i).wait_recv()
            self.xcopy(s, i, 0).start()
            self.xcopy(s, i, 1).start()

    def turn(self, s):
        for i in range(1, NZ):
            self.xcopy(s, i, 0).wait_recv()
            self.xcopy(s, i, 2).start()
            self.xcopy(s, i, 1).wait_recv()
            self.xcopy(s, i, 3).start()

    def dcopy(self, s):
        p = self.p
        mine = self.W.at[s // 3, lax.rem(s, 3), :, p.c]
        return remote(mine, mine, self.ds.at[s], self.dr.at[s], p.b, p.sib)

    def across(self, s):
        for i in range(1, NZ):
            self.xcopy(s, i, 2).wait_recv()
            self.xcopy(s, i, 3).wait_recv()
        self.dcopy(s).start()

    def arrive(self, s):
        self.dcopy(s).wait_recv()

    def drain(self, s):
        for i in range(1, NZ):
            self.zcopy(s, i).wait_send()
            for d in range(4):
                self.xcopy(s, i, d).wait_send()
        self.dcopy(s).wait_send()


class Scatter:
    def __init__(self, p, W, RX, RZ, G, Q, GF, sems):
        self.p, self.W, self.RX, self.RZ, self.G, self.Q, self.GF = p, W, RX, RZ, G, Q, GF
        (self.bs, self.br, self.cs, self.cr, self.es, self.er) = sems

    def held(self, e, q, half):
        return self.G.at[e % 3, :, pl.ds(pl.multiple_of(q * 64 + 32 * half, 32), 32), :]

    def room(self, e, i):
        at = pl.ds(128 * (i % 2), 128)
        if e < 3:
            ref = self.RX.at[e, i // 2, at, :]
        else:
            ref = self.W.at[1, e % 3, i // 4, (i // 2) % 2, at, :]
        return ref

    def hop(self, e, i):
        p = self.p
        q, half, to = (
            (p.dn, 0, p.xn), (p.dn, 1, p.yn), (p.xn, 0, p.xn), (p.yn, 1, p.yn), (p.yn, 0, p.yn), (p.xn, 1, p.xn),
        )[i]
        return remote(
            self.held(e, q, half), self.room(e, i).reshape(NZ, 32, C), self.bs.at[e, i], self.br.at[e, i], to, p.f
        )

    def begin(self, e):
        for i in range(4):
            self.hop(e, i).start()

    def mid(self, e):
        p = self.p
        for i, q, half in ((0, p.yn, 0), (1, p.xn, 1)):
            self.hop(e, i).wait_recv()
            mine = self.held(e, q, half)
            got = self.room(e, i)[...].reshape(NZ, 32, C).astype(f32)
            mine[...] = (mine[...].astype(f32) + got).astype(bf16)
            self.hop(e, 4 + i).start()

    def out3(self, e, i):
        p = self.p
        to = lax.rem(p.z + i, NZ)
        return remote(
            self.Q.at[e % 3, to], self.RZ.at[e, i - 1], self.cs.at[e, i - 1], self.cr.at[e, i - 1], p.b, 2 * to + p.c
        )

    def out4(self, e, d):
        p = self.p
        to = (p.xn, p.yn, p.dn)[d]
        mine = self.GF.at[1 - e // 3, e % 3, pl.ds(pl.multiple_of(p.b * 64, 64), 64), :]
        return remote(mine, mine, self.es.at[e, d], self.er.at[e, d], to, p.f)

    def along(self, e):
        p = self.p
        for i in range(2, 6):
            self.hop(e, i).wait_recv()
        for half, ways in ((0, (2, 4)), (1, (3, 5))):
            acc = self.held(e, p.b, half)[...].astype(f32)
            for i in ways:
                acc = acc + self.room(e, i)[...].reshape(NZ, 32, C).astype(f32)
            self.Q[e % 3, :, 32 * half : 32 * half + 32, :] = acc.astype(self.Q.dtype)
        for i in (2, 1, 3):
            self.out3(e, i).start()

    def final(self, e, lost):
        p = self.p
        for i in range(1, NZ):
            self.out3(e, i).wait_recv()
        acc = self.Q[e % 3, p.z].astype(f32)
        for i in range(1, NZ):
            acc = acc + self.RZ[e, i - 1].astype(f32)
        acc = acc + lost
        low = acc.astype(bf16)
        self.GF[1 - e // 3, e % 3, pl.ds(pl.multiple_of(p.b * 64, 64), 64), :] = low
        for d in (2, 0, 1):
            self.out4(e, d).start()
        low = low.astype(f32)
        return jnp.sum((low * low).reshape(8, 8, C), axis=0)

    def clear(self, e):
        for i in range(6):
            self.hop(e, i).wait_send()
        for i in range(1, NZ):
            self.out3(e, i).wait_send()

    def end(self, e):
        for d in range(3):
            self.out4(e, d).wait()


def conv_back_rows(S, W, k, r0, M):
    acc = None
    for u in range(3):
        lhs = jnp.concatenate([S[2 - u, pl.ds(r0 + (2 - v) * BLK, M), :] for v in range(3)], axis=1)
        rhs = jnp.concatenate(
            [
                W[k, u, z, c, v * 80 : v * 80 + 80, :]
                for v in range(3)
                for z in range(NZ)
                for c in range(2)
            ],
            axis=0,
        )
        d = jnp.dot(lhs, rhs, preferred_element_type=f32)
        acc = d if acc is None else acc + d
    return acc


def filter_grad(p, S, S2, dyT, dyS, DS, mu, G, e):
    u = e % 3
    if u == 0:
        ones = jnp.ones((ROWS, 128), bf16)
        own = jnp.concatenate([dyT[z, p.c] for z in range(NZ)], axis=0)
        sib = jnp.concatenate([dyS[z] for z in range(NZ)], axis=0)
        DS[...] = jnp.dot(own, ones, preferred_element_type=f32) + jnp.dot(
            sib, ones, preferred_element_type=f32
        )

    def tap(v, carry):
        at = pl.ds(pl.multiple_of(v * BLK, BLK), ROWS)
        own = jnp.concatenate([dyT[z, p.c] for z in range(NZ)], axis=0)
        sib = jnp.concatenate([dyS[z] for z in range(NZ)], axis=0)
        d = jnp.dot(own, S[u, at, :], preferred_element_type=f32)
        d = d + jnp.dot(sib, S2[u, at, :], preferred_element_type=f32)
        d = d - jnp.concatenate([DS[...]] * 5, axis=1) * mu
        for z in range(NZ):
            G[u, z, pl.ds(pl.multiple_of(v * 80, 16), 80), :] = d[80 * z : 80 * z + 80].astype(bf16)
        return carry

    lax.fori_loop(0, 3, tap, 0)


def step_kernel(
    images, labels, partner, valid, sizes, stem_w, bridge_t, conv_w, norm, head, bias,
    GF, bh_o, small_o, norm_o, misc_o,
    W, S, S2, dyT, dyS, DS, inner, block, dfl, RX, RZ, G, Q, slots, sibs, lab, gath, par, mask, AB, stem, dstem, pad,
    xs_, xr_, ps_, pr_, lbs, lbr, gs, gr, zs, zr, xs, xr, ds, dr, ls,
    bs, br, cs, cr, es, er, ts, tr, us, ur, free, fs, fr, hs, hr, js, jr, ms, mr,
):
    p = Place()
    ex = Exchange(p, slots, sibs, xs_, xr_, ps_, pr_)
    ga = Gather(p, W, zs, zr, xs, xr, ds, dr)
    sc = Scatter(p, W, RX, RZ, G, Q, GF, (bs, br, cs, cr, es, er))
    greet(p)
    load = pltpu.make_async_copy(conv_w.reshape(1440, C), block.at[pl.ds(0, 1440)], ls.at[0])
    load.start()
    mine = gath.at[p.f]
    mine[...] = jnp.zeros((40, 128), f32)
    mine[0:16, 0:80] = bridge_t[...]
    mine[16:22, 0:80] = norm[...]
    mine[24:34, 0:80] = head[...]
    def small(i):
        to = lax.rem(p.f + i, NF)
        return remote(mine, mine, gs, gr, p.b, to)

    def cast(s):
        k, u = s // 3, s % 3
        for v in range(3):
            t = 9 * k + 3 * u + v
            W[k, u, p.z, p.c, 80 * v : 80 * v + 80, :] = block[80 * t : 80 * t + 80, :].astype(bf16)
        W[k, u, p.z, p.c, 240:256, :] = jnp.zeros((16, C), bf16)

    load.wait()
    cast(0)
    met()
    for i in range(1, NF):
        small(i).start()
    ga.zsend(0)
    for s in range(1, 6):
        cast(s)
        if s < 3:
            ga.zsend(s)
    img = pltpu.roll(images[...].astype(f32), 32, 1)
    lane = iota((IMG, 128), 1)
    for c in range(3):
        for i in range(8):
            a = img[:, 1024 * c + 128 * i : 1024 * c + 128 * i + 128]
            if i == 0:
                a = jnp.where(lane < 32, 0.0, a)
            AB[IMG * i : IMG * i + IMG, 128 * c : 128 * c + 128] = a
    tile_c = jnp.bitwise_and(iota((16, 128), 1), 15) == iota((16, 128), 0)
    wc = lax.dot_general(
        stem_w[...].astype(bf16), tile_c.astype(bf16), CC, preferred_element_type=f32
    )
    fold_r = (jnp.bitwise_and(iota((256, 27), 0), 31) == iota((256, 27), 1)).astype(bf16)
    own_j = iota((256, 128), 0) // 32 == iota((256, 128), 1) // 16
    bd = jnp.dot(fold_r, wc.astype(bf16), preferred_element_type=f32)
    bd = jnp.where(own_j, bd, 0.0).astype(bf16)
    l, r = iota((128, 256), 0), iota((128, 256), 1)
    v = jnp.bitwise_and(l, 31) - 4 * (r // 32) + 1

    def hits(c):
        want = 9 * c + 3 * (l // 32) + v
        hit = (l < 96) & (v >= 0) & (v < 3) & (want == jnp.bitwise_and(r, 31))
        return hit.astype(f32)

    acc = None
    for c in range(3):
        t = jnp.dot(hits(c).astype(bf16), bd, preferred_element_type=f32).astype(bf16)
        d = jnp.dot(
            AB[:, 128 * c : 128 * c + 128].astype(bf16), t, preferred_element_type=f32
        )
        acc = d if acc is None else acc + d
    stem[...] = acc.astype(bf16).astype(f32)
    ok = column(valid[...].astype(f32), IMG)
    q = p.f * IMG + iota((IMG, 1), 0)
    member = jnp.zeros((IMG, 1), jnp.int32)
    end = jnp.int32(0)
    for g in range(8):
        end = end + sizes[p.b, g]
        member = member + (q >= end).astype(jnp.int32)
    member = jnp.minimum(member, 7)
    size = jnp.zeros((IMG, 1), f32)
    for g in range(8):
        size = size + jnp.where(member == g, sizes[p.b, g].astype(f32), 0.0)
    weight = ok / size
    mask[...] = jnp.concatenate([jnp.broadcast_to(ok, (IMG, 128))] * 8, axis=0)
    count = 64.0 * jnp.sum(ok)
    own_row = labels[...].astype(f32)
    slot = ex.mine(0)
    slot[5:6, :] = jnp.full((1, 128), count, f32)
    slot[6:7, :] = jnp.concatenate([own_row, jnp.zeros((1, 104), f32)], axis=1)
    slot[7:8, :] = jnp.full((1, 128), jnp.sum(weight), f32)
    edge = jnp.zeros((BLK, C), bf16)
    for u in range(3):
        S[u, 0:BLK, :] = edge
        S[u, 9 * BLK : 10 * BLK, :] = edge
        for z in range(NZ):
            G[u, z, 240:256, :] = jnp.zeros((16, C), bf16)
    rest = gath.at[0 : NF - 1]
    remote(rest, rest, gs, gr, p.b, p.sib).wait()
    lane = iota((40, 128), 1)
    for k in range(5):
        acc = jnp.zeros((40, 128), f32)
        for f in range(NF):
            lo, hi = max(80 * f, 128 * k), min(80 * f + 80, 128 * k + 128)
            if lo < hi:
                turned = pltpu.roll(gath[f], (80 * f - 128 * k) % 128, 1)
                acc = jnp.where((lane >= lo - 128 * k) & (lane < hi - 128 * k), turned, acc)
        par[:, 128 * k : 128 * k + 128] = acc
    bridge8 = jnp.concatenate([par[0:16, :].astype(bf16)] * 8, axis=0)

    def rows(j):
        return pl.ds(pl.multiple_of(j * BLK, BLK), BLK)

    def base_rows(j):
        pick = iota((BLK, 128), 1) // 16 == j
        x = jnp.where(pick, stem[...], 0.0).astype(bf16)
        return jnp.dot(x, bridge8, preferred_element_type=f32)

    def base_block(j, carry):
        inner[rows(j), :] = base_rows(j)
        return carry

    lax.fori_loop(0, 8, base_block, 0)
    local_stats(inner, mask, count, ex.mine(0))
    ex.send(0)
    ga.relay(0)
    ga.relay(1)
    ga.turn(0)

    def inner_rows(j):
        return inner[rows(j), :]

    def block_rows(j):
        return block[rows(j), :]

    def dfl_rows(j):
        return dfl[rows(j), :]

    def gain(k):
        return par[16 + 2 * k : 17 + 2 * k, :]

    def shift(k):
        return par[17 + 2 * k : 18 + 2 * k, :]

    def normed(src, stats, k):
        mean, scale = stats[:2]

        def one(j, acc):
            hat = (src(j) - mean) * scale
            out = jnp.maximum(gain(k) * hat + shift(k), 0.0)
            spread_rows(S, j, out)
            m = jnp.concatenate([mask[...]] * 5, axis=1)
            return acc + jnp.sum((out * m).reshape(BLK // 8, 8, C), axis=0)

        acc = lax.fori_loop(0, 8, one, jnp.zeros((8, C), f32))
        return jnp.sum(acc, axis=0, keepdims=True)

    stats0 = joint_stats(ex, 0)
    labs = remote(lab.at[0], lab.at[1], lbs, lbr, p.b, p.sib)
    lab[0] = slots[0, :, 6, :]
    labs.start()
    put_spare(ex.mine(1), normed(inner_rows, stats0, 0))
    for s in range(3, 6):
        ga.zsend(s)
    ga.relay(2)
    ga.turn(1)
    ga.across(0)
    ga.turn(2)
    ga.relay(3)
    ga.across(1)
    ga.across(2)
    ga.relay(4)
    for s in range(3):
        ga.arrive(s)

    def conv0(it, carry):
        r0 = pl.multiple_of(it * 384, 384)
        inner[pl.ds(r0, 384), :] = conv_rows(S, W, 0, r0, 384)

        @pl.when(it == 0)
        def _():
            ga.relay(5)

        @pl.when(it == 1)
        def _():
            ga.turn(3)
            ga.turn(4)

        @pl.when(it == 3)
        def _():
            ga.turn(5)
            ga.across(3)

        return carry

    lax.fori_loop(0, 4, conv0, 0)
    local_stats(inner, mask, count, ex.mine(1))
    ex.send(1)
    ga.across(4)
    stats1 = joint_stats(ex, 1)
    put_spare(ex.mine(2), normed(inner_rows, stats1, 1))
    ga.across(5)
    for s in range(3, 6):
        ga.arrive(s)

    def share(u):
        return remote(S.at[u], S2.at[u], ts.at[u], tr.at[u], p.b, p.sib)

    for u in range(3):
        share(u).start()

    def conv1(it, carry):
        r0 = pl.multiple_of(it * 384, 384)
        at = pl.ds(r0, 384)
        low = jnp.concatenate([base_rows(2 * it), base_rows(2 * it + 1)], axis=0)
        block[at, :] = low + conv_rows(S, W, 1, r0, 384)
        return carry

    lax.fori_loop(0, 4, conv1, 0)
    local_stats(block, mask, count, ex.mine(2))
    ex.send(2)
    for s in range(6):
        ga.drain(s)
    lane = iota((IMG, 16), 1)
    label = column(own_row, IMG)
    mate = column(partner[...].astype(f32), IMG)
    home = jnp.floor((mate + 0.5) / 24.0)
    chip = jnp.floor((home + 0.5) / 2.0)
    at_chip = (iota((IMG, NCHIP), 1).astype(f32) == chip).astype(bf16)
    labs.wait()
    own_side = jnp.dot(at_chip, lab[0].astype(bf16), preferred_element_type=f32)
    sib_side = jnp.dot(at_chip, lab[1].astype(bf16), preferred_element_type=f32)
    there = jnp.where(home - 2.0 * chip == p.c.astype(f32), own_side, sib_side)
    spot = iota((IMG, 128), 1).astype(f32) == mate - 24.0 * home
    mate_label = jnp.sum(jnp.where(spot, there, 0.0), axis=1, keepdims=True)
    lane_f = lane.astype(f32)
    target = own_share * (lane_f == label).astype(f32) + (1.0 - own_share) * (
        lane_f == mate_label
    ).astype(f32)
    live = lane < 10
    head16 = par[24:40, :].astype(bf16)
    pad[...] = jnp.zeros((8, 128), f32)
    pad[0:1, 0:10] = bias[...]
    sides = sibs[0, 0] + sibs[0, 1]
    total = jnp.sum(sides[7:8, 0:1])
    valid_count = jnp.sum(sides[5:6, 0:1])
    stats2 = joint_stats(ex, 2)
    mu0, mu1 = stats1[2] / valid_count, stats2[2] / valid_count

    def pool(j, acc):
        hat = (block_rows(j) - stats2[0]) * stats2[1]
        out = jnp.maximum(gain(2) * hat + shift(2), 0.0)
        return acc + jnp.sum(out.reshape(8, IMG, C), axis=0)

    pooled = lax.fori_loop(0, 8, pool, jnp.zeros((IMG, C), f32)) / 64.0
    pooled = pooled.astype(bf16)
    logits = lax.dot_general(pooled, head16, AC, preferred_element_type=f32) + pad[0:1, 0:16]
    top = jnp.max(jnp.where(live, logits, -3e38), axis=1, keepdims=True)
    moved = jnp.where(live, logits - top, 0.0)
    size_sum = jnp.sum(jnp.where(live, jnp.exp(moved), 0.0), axis=1, keepdims=True)
    logp = moved - jnp.log(size_sum)
    loss_part = -jnp.sum(
        weight * jnp.sum(jnp.where(live, target * logp, 0.0), axis=1, keepdims=True)
    )
    d_logits = jnp.where(live, (jnp.exp(logp) - target) * (weight / total), 0.0).astype(bf16)
    g_bias = jnp.sum(d_logits.astype(f32), axis=0, keepdims=True)
    par[24:40, :] = lax.dot_general(d_logits, pooled, CC, preferred_element_type=f32)
    d_pooled = jnp.dot(d_logits, head16, preferred_element_type=f32)
    d_out24 = d_pooled / 64.0

    def zhat(src, j, stats):
        return (src(j) - stats[0]) * stats[1]

    def passed(hat, k, d_out):
        return jnp.where(gain(k) * hat + shift(k) > 0.0, d_out, 0.0)

    def grad_sums(src, stats, k, d_of, e):
        def one(j, acc):
            hat = zhat(src, j, stats)
            got = passed(hat, k, d_of(j))
            return (
                acc[0] + jnp.sum(got.reshape(BLK // 8, 8, C), axis=0),
                acc[1] + jnp.sum((got * hat).reshape(BLK // 8, 8, C), axis=0),
            )

        zero = jnp.zeros((8, C), f32)
        acc = lax.fori_loop(0, 8, one, (zero, zero))
        put_row(ex.mine(e), 0, jnp.sum(acc[0], axis=0, keepdims=True))
        put_row(ex.mine(e), 8, jnp.sum(acc[1], axis=0, keepdims=True))

    def grad_rows(src, stats, k, d_of, sums, j):
        hat = zhat(src, j, stats)
        m = jnp.concatenate([mask[...]] * 5, axis=1)
        got = passed(hat, k, d_of(j))
        return (gain(k) * stats[1]) * (got - m * (sums[0] + hat * sums[1]) / valid_count)

    def head_rows(j):
        return jnp.concatenate([d_out24] * 8, axis=0)

    def turn(src):
        for it in range(4):
            x = src[384 * it : 384 * it + 384, :].T.astype(bf16)
            for f in range(NF):
                dyT[f // 2, f % 2, :, 384 * it : 384 * it + 384] = x[80 * f : 80 * f + 80]

    trade = remote(dyT.at[:, 1 - p.c], dyS, us, ur, p.b, p.sib)

    grad_sums(block_rows, stats2, 2, head_rows, 3)
    slot = ex.mine(3)
    slot[5:6, :] = jnp.full((1, 128), loss_part, f32)
    slot[6:7, :] = jnp.concatenate([g_bias, jnp.zeros((1, 112), f32)], axis=1)
    ex.send(3)
    tot3 = ex.total(3)
    sums2 = wide(tot3[0:5]), wide(tot3[8:13])

    def low_sums(dst, src, stats, k, d_of, sums):
        def one(j, acc):
            d = grad_rows(src, stats, k, d_of, sums, j)
            dst[rows(j), :] = d
            return acc + jnp.sum(d.astype(bf16).astype(f32).reshape(BLK // 8, 8, C), axis=0)

        acc = lax.fori_loop(0, 8, one, jnp.zeros((8, C), f32))
        return jnp.sum(acc, axis=0, keepdims=True)

    def lost(dy_sums, mu):
        at = 64 * p.b + iota((64, C), 0)
        o = at - 80 * ((at >= 80).astype(jnp.int32) + (at >= 160).astype(jnp.int32))
        hit = (iota((64, C), 1) == 80 * p.f + o) & (at < 240)
        return jnp.sum(jnp.where(hit, dy_sums, 0.0), axis=1, keepdims=True) * mu

    put_spare(ex.mine(4), low_sums(block, block_rows, stats2, 2, head_rows, sums2))
    turn(block)
    trade.start()
    for u in range(3):
        share(u).wait()
    trade.wait()
    filter_grad(p, S, S2, dyT, dyS, DS, mu1, G, 0)
    sc.begin(0)
    filter_grad(p, S, S2, dyT, dyS, DS, mu1, G, 1)
    sc.begin(1)
    filter_grad(p, S, S2, dyT, dyS, DS, mu1, G, 2)
    sc.begin(2)
    sc.mid(0)
    pl.semaphore_signal(free, inc=1, device_id=(p.b, p.sib), device_id_type=MESH)

    def spread(src):
        def one(j, carry):
            spread_rows(S, j, src[rows(j), :])
            return carry

        lax.fori_loop(0, 8, one, 0)

    spread(block)

    def back_conv1(it, carry):
        r0 = pl.multiple_of(it * 384, 384)
        dfl[pl.ds(r0, 384), :] = conv_back_rows(S, W, 1, r0, 384)

        @pl.when(it == 1)
        def _():
            sc.mid(1)

        @pl.when(it == 3)
        def _():
            sc.mid(2)

        return carry

    lax.fori_loop(0, 4, back_conv1, 0)
    grad_sums(inner_rows, stats1, 1, dfl_rows, 4)
    ex.send(4)
    normed(base_rows, stats0, 0)
    pl.semaphore_wait(free, 1)
    for u in range(3):
        share(u).start()
    sc.along(0)
    tot4 = ex.total(4)
    sums1 = wide(tot4[0:5]), wide(tot4[8:13])
    lost1 = lost(spare(tot4), mu1)
    put_spare(ex.mine(5), low_sums(dfl, inner_rows, stats1, 1, dfl_rows, sums1))
    turn(dfl)
    trade.start()
    sc.along(1)
    sc.along(2)
    sc.clear(0)
    share(0).wait()
    trade.wait()
    filter_grad(p, S, S2, dyT, dyS, DS, mu0, G, 3)
    sc.begin(3)
    squares = sc.final(0, lost1)
    sc.clear(1)
    share(1).wait()
    filter_grad(p, S, S2, dyT, dyS, DS, mu0, G, 4)
    sc.begin(4)
    squares = squares + sc.final(1, lost1)
    sc.clear(2)
    share(2).wait()
    filter_grad(p, S, S2, dyT, dyS, DS, mu0, G, 5)
    sc.begin(5)
    squares = squares + sc.final(2, lost1)
    sc.mid(3)
    spread(dfl)

    def back_conv0(it, carry):
        r0 = pl.multiple_of(it * 384, 384)
        inner[pl.ds(r0, 384), :] = conv_back_rows(S, W, 0, r0, 384)

        @pl.when(it == 2)
        def _():
            sc.mid(4)

        return carry

    lax.fori_loop(0, 4, back_conv0, 0)

    grad_sums(base_rows, stats0, 0, inner_rows, 5)
    ex.send(5)
    sc.mid(5)
    sc.along(3)
    sc.along(4)
    tot5 = ex.total(5)
    lost0 = lost(spare(tot5), mu0)
    sums0 = wide(tot5[0:5]), wide(tot5[8:13])
    grid16 = dfl.at[512:640]
    grid16[...] = jnp.zeros((128, C), f32)
    dstem[...] = jnp.zeros((BLK, 128), f32)

    def back0(j, carry):
        d = block[rows(j), :] + grad_rows(base_rows, stats0, 0, inner_rows, sums0, j)
        d = d.astype(bf16)
        pick = iota((BLK, 128), 1) // 16 == j
        x = jnp.where(pick, stem[...], 0.0).astype(bf16)
        grid16[...] += lax.dot_general(x, d, CC, preferred_element_type=f32)
        y = lax.dot_general(d, bridge8, AC, preferred_element_type=f32)
        dstem[...] += jnp.where(pick, y, 0.0)
        return carry

    lax.fori_loop(0, 8, back0, 0)
    acc = grid16[0:16, :]
    for j in range(1, 8):
        acc = acc + grid16[16 * j : 16 * j + 16, :]
    dfl[0:16, :] = acc
    dfl[16:32, :] = par[24:40, :]

    def half(row, c):
        return dfl.at[pl.ds(pl.multiple_of(row + 16 * c, 16), 16), :]

    give = remote(half(0, 1 - p.c), half(32, 1 - p.c), fs, fr, p.b, p.sib)
    give.start()
    sc.along(5)
    low = dstem[...].astype(bf16)
    high = lax.Precision.HIGHEST
    acc = None
    for c in range(3):
        t = lax.dot_general(
            AB[:, 128 * c : 128 * c + 128].astype(bf16), low, CC, preferred_element_type=f32
        )
        d = lax.dot_general(hits(c), t, CC, precision=high, preferred_element_type=f32)
        acc = d if acc is None else acc + d
    acc = jnp.where(own_j, acc, 0.0)
    fold = (jnp.bitwise_and(iota((256, 128), 0), 31) == iota((256, 128), 1)).astype(f32)
    acc = lax.dot_general(acc, fold, CC, precision=high, preferred_element_type=f32)
    slots[6, p.chip] = jnp.dot(
        tile_c.astype(f32), acc, precision=high, preferred_element_type=f32
    )
    ex.send(6)
    squares = squares + sc.final(3, lost0)
    give.wait()
    zline = dfl.at[pl.ds(pl.multiple_of(64 + 16 * p.z, 16), 16), :]
    zline[...] = half(0, p.c)[...] + half(32, p.c)[...]
    for i in range(1, NZ):
        to = lax.rem(p.z + i, NZ)
        remote(zline, zline, hs, hr, p.b, 2 * to + p.c).start()
    squares = squares + sc.final(4, lost0)
    rest = dfl.at[64 : 64 + 16 * (NZ - 1), :]
    remote(rest, rest, hs, hr, p.b, p.sib).wait()
    square = dfl.at[pl.ds(pl.multiple_of(128 + 16 * p.b, 16), 16), :]
    square[...] = jnp.sum(dfl[64:128, :].reshape(NZ, 16, C), axis=0)
    for i in range(1, NB):
        to = lax.rem(p.b + i, NB)
        remote(square, square, js, jr, to, p.f).start()
    g_stem = ex.total(6)
    squares = squares + sc.final(5, lost0)
    slots[7, p.chip] = jnp.full((16, 128), jnp.sum(squares), f32)
    ex.send(7)
    rest = dfl.at[128 : 128 + 16 * (NB - 1), :]
    remote(rest, rest, js, jr, p.b, p.sib).wait()
    done = half(192, p.c)
    done[...] = jnp.sum(dfl[128:192, :].reshape(NB, 16, C), axis=0)
    give = remote(done, done, ms, mr, p.b, p.sib)
    give.start()
    give.wait()
    both = dfl[192:224, :]
    bias_all = tot3[6:7, :]
    bh_o[...] = both
    small_o[...] = g_stem
    norm_o[...] = jnp.zeros((8, C), f32)
    for k, sums in enumerate((sums0, sums1, sums2)):
        norm_o[2 * k : 2 * k + 1, :] = sums[1]
        norm_o[2 * k + 1 : 2 * k + 2, :] = sums[0]
    ng = norm_o[...]
    other = jnp.sum(both * both) + jnp.sum(g_stem * g_stem) + jnp.sum(bias_all * bias_all)
    other = other + jnp.sum(ng * ng)
    conv_sq = ex.total(7)[0:1, :]
    misc_o[...] = jnp.zeros((8, 128), f32)
    misc_o[0:1, :] = jnp.sqrt(conv_sq + other)
    misc_o[1:2, :] = tot3[5:6, :] / total
    misc_o[2:3, :] = bias_all
    for e in range(6):
        sc.end(e)
    for e in range(3, 6):
        sc.clear(e)


def step_call(images, labels, partner, valid, sizes, stem_w, bridge_t, conv_w, norm, head, bias):
    V, A, SM = pltpu.VMEM, pl.ANY, pltpu.SMEM
    spec = lambda m: pl.BlockSpec(memory_space=m)
    D = pltpu.SemaphoreType.DMA
    sh = jax.ShapeDtypeStruct
    return pl.pallas_call(
        step_kernel,
        out_shape=(
            sh((2, 3, 256, C), bf16), sh((32, C), f32), sh((16, 128), f32), sh((8, C), f32), sh((8, 128), f32),
        ),
        in_specs=[
            spec(V), spec(V), spec(V), spec(V), spec(SM), spec(V), spec(V), spec(A), spec(V), spec(V), spec(V),
        ],
        out_specs=(spec(V),) * 5,
        scratch_shapes=[
            V((2, 3, NZ, 2, 256, C), bf16), V((3, 10 * BLK, C), bf16), V((3, 10 * BLK, C), bf16),
            V((NZ, 2, 80, ROWS), bf16), V((NZ, 80, ROWS), bf16), V((NZ * 80, 128), f32),
            V((ROWS, C), f32), V((ROWS, C), f32), V((ROWS, C), f32),
            V((3, 3, 256, C), bf16), V((6, 3, 64, C), LINE), V((3, NZ, 256, C), bf16), V((3, NZ, 64, C), LINE),
            V((8, NCHIP, 16, 128), f32), V((8, 2, 16, 128), f32), V((2, NCHIP, 128), f32), V((NF, 40, 128), f32), V((40, C), f32),
            V((BLK, 128), f32), V((BLK, 384), f32), V((BLK, 128), f32), V((BLK, 128), f32), V((8, 128), f32),
            D((8,)), D((8,)), D((8,)), D((8,)), D, D, D, D, D((6, 4)), D((6, 4)), D((6, 12)), D((6, 12)), D((6,)), D((6,)), D((1,)),
            D((6, 6)), D((6, 6)), D((6, 3)), D((6, 3)), D((6, 3)), D((6, 3)), D((3,)), D((3,)), D, D,
            pltpu.SemaphoreType.REGULAR, D, D, D, D, D, D, D, D,
        ],
        compiler_params=pltpu.CompilerParams(
            collective_id=0, has_side_effects=True, vmem_limit_bytes=63 << 20
        ),
    )(images, labels, partner, valid, sizes, stem_w, bridge_t, conv_w, norm, head, bias)


def make_patches(images):
    number = images.shape[0]
    grid = images.reshape(number, 3, 32, 32)
    padded = jnp.pad(grid, ((0, 0), (0, 0), (1, 1), (1, 1)))
    pieces = [
        padded[:, :, row_off : row_off + 29 : 4, col_off : col_off + 29 : 4]
        for row_off in range(3)
        for col_off in range(3)
    ]
    stacked = jnp.stack(pieces, axis=2)
    return jnp.transpose(stacked, (1, 2, 0, 3, 4)).reshape(27, number * 64)


def shifted(feature_field):
    width, rows = feature_field.shape
    grid = feature_field.reshape(width, rows // 64, 8, 8)
    padded = jnp.pad(grid, ((0, 0), (0, 0), (1, 1), (1, 1)))
    pieces = [
        padded[:, :, row_off : row_off + 8, col_off : col_off + 8]
        for row_off in range(3)
        for col_off in range(3)
    ]
    return jnp.stack(pieces, axis=0).reshape(9 * width, rows)


def unshifted(parts, width):
    rows = parts.shape[1]
    grid = parts.reshape(9, width, rows // 64, 8, 8)
    summed = jnp.zeros((width, rows // 64, 10, 10), jnp.float32)
    for row_off in range(3):
        for col_off in range(3):
            summed = summed + jnp.pad(
                grid[3 * row_off + col_off],
                ((0, 0), (0, 0), (row_off, 2 - row_off), (col_off, 2 - col_off)),
            )
    return summed[:, :, 1:9, 1:9].reshape(width, rows)


def image_weights(valid_mask, group_sizes):
    shards, groups = group_sizes.shape
    capacity = valid_mask.shape[0] // shards
    group_ends = jnp.cumsum(group_sizes, axis=1)
    slot_index = jnp.arange(capacity, dtype=jnp.int32)
    member = jnp.sum(
        (slot_index[None, :, None] >= group_ends[:, None, :]).astype(jnp.int32), axis=2
    )
    member = jnp.minimum(member, groups - 1)
    chosen = (member[:, :, None] == jnp.arange(groups, dtype=jnp.int32)[None, None, :]).astype(
        jnp.float32
    )
    sizes_each = jnp.sum(chosen * group_sizes[:, None, :].astype(jnp.float32), axis=2)
    return valid_mask.astype(jnp.float32) / sizes_each.reshape(-1)


def norm_forward(feature_field, norm_gain, norm_shift, row_validity_mask, valid_count):
    batch_mean = (
        lax.psum(jnp.sum(feature_field * row_validity_mask, axis=1), ("batch", "filt"))
        / valid_count
    )
    centered_input = feature_field - batch_mean[:, None]
    batch_variance = (
        lax.psum(
            jnp.sum(centered_input * centered_input * row_validity_mask, axis=1), ("batch", "filt")
        )
        / valid_count
    )
    inverse_scale = lax.rsqrt(batch_variance + norm_epsilon)
    normalized_input = (feature_field - batch_mean[:, None]) * inverse_scale[:, None]
    norm_output = jnp.maximum(norm_gain[:, None] * normalized_input + norm_shift[:, None], 0.0)
    return (norm_output, normalized_input, inverse_scale)


def masked_norm_backward(
    output_gradient,
    norm_output,
    normalized_input,
    inverse_scale,
    norm_gain,
    row_validity_mask,
    valid_count,
):
    passed_rows = jnp.where(norm_output > 0.0, output_gradient, 0.0)
    shift_gradient, gain_gradient = lax.psum(
        (jnp.sum(passed_rows, axis=1), jnp.sum(passed_rows * normalized_input, axis=1)),
        ("batch", "filt"),
    )
    input_gradient = (
        passed_rows
        - row_validity_mask[None, :]
        * (shift_gradient[:, None] + normalized_input * gain_gradient[:, None])
        / valid_count
    )
    return ((norm_gain * inverse_scale)[:, None] * input_gradient, gain_gradient, shift_gradient)


def conv_forward(feature_field, weight_shard):
    stacked = shifted(feature_field)
    low_shard = weight_shard.astype(jnp.bfloat16)
    piece = lax.all_gather(low_shard, "filt", axis=0, tiled=True)
    norm_output = jnp.dot(
        piece.reshape(piece.shape[0], -1), stacked, preferred_element_type=jnp.float32
    )
    return (norm_output, None)


def conv_backward(feature_field, weight_shard, output_gradient):
    width = feature_field.shape[0]
    stacked = shifted(feature_field)
    rows_grad = output_gradient
    term = lax.dot_general(
        rows_grad, stacked, (((1,), (1,)), ((), ())), preferred_element_type=jnp.float32
    )
    weight_grad = lax.psum_scatter(
        term.reshape(lax.axis_size("filt") * weight_shard.shape[0], 9, width),
        "filt",
        scatter_dimension=0,
        tiled=True,
    )
    piece = lax.all_gather(weight_shard.astype(jnp.bfloat16), "filt", axis=0, tiled=True)
    rows_grad = output_gradient
    back = lax.dot_general(
        piece.reshape(piece.shape[0], -1),
        rows_grad,
        (((0,), (0,)), ((), ())),
        preferred_element_type=jnp.float32,
    )
    return (unshifted(back, width), weight_grad)


def adam_step(weight, output_gradient, first, second, rate, shrink, factor):
    clipped = output_gradient * factor
    first = beta_one * first + (1.0 - beta_one) * clipped
    second = beta_two * second + (1.0 - beta_two) * clipped * clipped
    ahead = first / (1.0 - beta_one**STEP)
    behind = second / (1.0 - beta_two**STEP)
    return (
        weight - rate * (ahead / (jnp.sqrt(behind) + adam_eps) + shrink * weight),
        first,
        second,
    )


def body(
    images,
    labels,
    partner,
    valid_mask,
    group_sizes,
    stem_weight,
    bridge_weight,
    conv_weight,
    norm_params,
    head_weight,
    head_bias,
    stem_first,
    stem_second,
    bridge_first,
    bridge_second,
    conv_first,
    conv_second,
    norm_first,
    norm_second,
    head_first,
    head_second,
    bias_first,
    bias_second,
):
    width = bridge_weight.shape[0]
    bridge_all, norm_all, head_all = (
        lax.all_gather(bridge_weight, "filt", axis=0, tiled=True),
        lax.all_gather(norm_params, "filt", axis=1, tiled=True),
        lax.all_gather(head_weight, "filt", axis=1, tiled=True),
    )
    labels_all, valid_all = (
        lax.all_gather(labels, ("batch", "filt"), axis=0, tiled=True),
        lax.all_gather(valid_mask, ("batch", "filt"), axis=0, tiled=True),
    )
    weight_all = image_weights(valid_all, group_sizes)
    total = jnp.sum(weight_all)
    valid_count = 64.0 * jnp.sum(valid_all.astype(jnp.float32))
    local = images.shape[0]
    image_weight = lax.dynamic_slice_in_dim(
        weight_all, lax.axis_index(("batch", "filt")) * local, local
    )
    row_validity_mask = jnp.repeat(valid_mask.astype(jnp.float32), 64)
    patch = make_patches(images)
    stem = jnp.dot(
        stem_weight.astype(jnp.bfloat16), patch, preferred_element_type=jnp.float32
    ).astype(jnp.bfloat16)
    base = jnp.dot(bridge_all.astype(jnp.bfloat16), stem, preferred_element_type=jnp.float32)
    first, first_hat, first_scale = norm_forward(
        base, norm_all[0], norm_all[1], row_validity_mask, valid_count
    )
    first_low = first.astype(jnp.bfloat16)
    inner, kept_zero = conv_forward(first_low, conv_weight[0])
    second, second_hat, second_scale = norm_forward(
        inner, norm_all[2], norm_all[3], row_validity_mask, valid_count
    )
    second_low = second.astype(jnp.bfloat16)
    branch, kept_one = conv_forward(second_low, conv_weight[1])
    final, final_hat, final_scale = norm_forward(
        base + branch, norm_all[4], norm_all[5], row_validity_mask, valid_count
    )
    pooled = jnp.mean(final.reshape(final.shape[0], local, 64), axis=2).astype(jnp.bfloat16)
    logits = (
        jnp.dot(head_all.astype(jnp.bfloat16), pooled, preferred_element_type=jnp.float32)
        + head_bias[:, None]
    )
    moved = logits - jnp.max(logits, axis=0, keepdims=True)
    logp = moved - jnp.log(jnp.sum(jnp.exp(moved), axis=0, keepdims=True))
    classes = jnp.arange(logits.shape[0], dtype=jnp.int32)
    partner_labels = jnp.take(labels_all, partner)
    target = own_share * (labels[None, :] == classes[:, None]).astype(jnp.float32) + (
        1.0 - own_share
    ) * (partner_labels[None, :] == classes[:, None]).astype(jnp.float32)
    loss_part = -jnp.sum(image_weight * jnp.sum(target * logp, axis=0))
    d_logits = ((jnp.exp(logp) - target) * (image_weight / total)[None, :]).astype(jnp.bfloat16)
    bias_grad = jnp.sum(d_logits.astype(jnp.float32), axis=1)
    head_grad = lax.dot_general(
        d_logits, pooled, (((1,), (1,)), ((), ())), preferred_element_type=jnp.float32
    )
    d_pooled = lax.dot_general(
        head_all.astype(jnp.bfloat16),
        d_logits,
        (((0,), (0,)), ((), ())),
        preferred_element_type=jnp.float32,
    )
    d_final = jnp.repeat(d_pooled / 64.0, 64, axis=1)
    d_block, gain_two, shift_two = masked_norm_backward(
        d_final, final, final_hat, final_scale, norm_all[4], row_validity_mask, valid_count
    )
    d_second, conv_grad_one = conv_backward(
        second_low, conv_weight[1], d_block.astype(jnp.bfloat16)
    )
    d_inner, gain_one, shift_one = masked_norm_backward(
        d_second, second, second_hat, second_scale, norm_all[2], row_validity_mask, valid_count
    )
    d_first, conv_grad_zero = conv_backward(first_low, conv_weight[0], d_inner.astype(jnp.bfloat16))
    d_lower, gain_zero, shift_zero = masked_norm_backward(
        d_first, first, first_hat, first_scale, norm_all[0], row_validity_mask, valid_count
    )
    d_base = (d_block + d_lower).astype(jnp.bfloat16)
    bridge_grad = lax.dot_general(
        d_base, stem, (((1,), (1,)), ((), ())), preferred_element_type=jnp.float32
    )
    d_stem = lax.dot_general(
        bridge_all.astype(jnp.bfloat16),
        d_base,
        (((0,), (0,)), ((), ())),
        preferred_element_type=jnp.float32,
    ).astype(jnp.bfloat16)
    stem_grad = lax.dot_general(
        d_stem, patch, (((1,), (1,)), ((), ())), preferred_element_type=jnp.float32
    )
    bridge_part, head_part = (
        lax.psum_scatter(bridge_grad, "filt", scatter_dimension=0, tiled=True),
        lax.psum_scatter(head_grad, "filt", scatter_dimension=1, tiled=True),
    )
    conv_grad, bridge_sum, head_sum = lax.psum(
        (jnp.stack([conv_grad_zero, conv_grad_one]), bridge_part, head_part), "batch"
    )
    stem_sum, bias_sum, loss_sum = lax.psum((stem_grad, bias_grad, loss_part), ("batch", "filt"))
    norm_full = jnp.stack([gain_zero, shift_zero, gain_one, shift_one, gain_two, shift_two])
    norm_grad = lax.dynamic_slice_in_dim(norm_full, lax.axis_index("filt") * width, width, 1)
    owned_square = (
        jnp.sum(conv_grad * conv_grad)
        + jnp.sum(bridge_sum * bridge_sum)
        + jnp.sum(norm_grad * norm_grad)
        + jnp.sum(head_sum * head_sum)
    )
    squares_all = (
        lax.psum(owned_square, "filt") + jnp.sum(stem_sum * stem_sum) + jnp.sum(bias_sum * bias_sum)
    )
    grad_norm = jnp.sqrt(squares_all)
    factor = clip_norm / jnp.maximum(grad_norm, clip_norm)
    stem_new = adam_step(stem_weight, stem_sum, stem_first, stem_second, 0.5, 0.05, factor)
    bridge_new = adam_step(
        bridge_weight, bridge_sum, bridge_first, bridge_second, 0.6, 0.05, factor
    )
    conv_new = adam_step(conv_weight, conv_grad, conv_first, conv_second, 0.033, 0.05, factor)
    norm_new = adam_step(norm_params, norm_grad, norm_first, norm_second, 0.5, 0.0, factor)
    head_new = adam_step(head_weight, head_sum, head_first, head_second, 0.1, 0.05, factor)
    bias_new = adam_step(head_bias, bias_sum, bias_first, bias_second, 0.5, 0.0, factor)
    return (
        stem_new[0],
        stem_new[1],
        stem_new[2],
        bridge_new[0],
        bridge_new[1],
        bridge_new[2],
        conv_new[0],
        conv_new[1],
        conv_new[2],
        norm_new[0],
        norm_new[1],
        norm_new[2],
        head_new[0],
        head_new[1],
        head_new[2],
        bias_new[0],
        bias_new[1],
        bias_new[2],
        grad_norm,
        loss_sum / total,
    )


def fast_body(
    images, labels, partner, valid_mask, group_sizes, stem_weight, bridge_weight, conv_weight, norm_params,
    head_weight, head_bias, stem_first, stem_second, bridge_first, bridge_second, conv_first, conv_second,
    norm_first, norm_second, head_first, head_second, bias_first, bias_second,
):
    width = bridge_weight.shape[0]
    conv_grad, both, g_stem, g_norm, misc = step_call(
        images, labels[None], partner[None], valid_mask[None], group_sizes, stem_weight, bridge_weight.T,
        conv_weight.transpose(0, 2, 1, 3), norm_params, head_weight, head_bias[None],
    )
    conv_grad = conv_grad[:, :, :240].reshape(2, 9, width, C).transpose(0, 2, 1, 3).astype(f32)
    both = lax.dynamic_slice_in_dim(both, lax.axis_index("filt") * width, width, 1)
    bridge_sum, head_sum = both[:16].T, both[16:26]
    norm_grad = lax.dynamic_slice_in_dim(g_norm[:6], lax.axis_index("filt") * width, width, 1)
    stem_sum, bias_sum = g_stem[:, :27], misc[2, :10]
    grad_norm, loss = misc[0, 0], misc[1, 0]
    factor = clip_norm / jnp.maximum(grad_norm, clip_norm)
    stem_new = adam_step(stem_weight, stem_sum, stem_first, stem_second, 0.5, 0.05, factor)
    bridge_new = adam_step(
        bridge_weight, bridge_sum, bridge_first, bridge_second, 0.6, 0.05, factor
    )
    conv_new = adam_step(conv_weight, conv_grad, conv_first, conv_second, 0.033, 0.05, factor)
    norm_new = adam_step(norm_params, norm_grad, norm_first, norm_second, 0.5, 0.0, factor)
    head_new = adam_step(head_weight, head_sum, head_first, head_second, 0.1, 0.05, factor)
    bias_new = adam_step(head_bias, bias_sum, bias_first, bias_second, 0.5, 0.0, factor)
    return (
        stem_new[0],
        stem_new[1],
        stem_new[2],
        bridge_new[0],
        bridge_new[1],
        bridge_new[2],
        conv_new[0],
        conv_new[1],
        conv_new[2],
        norm_new[0],
        norm_new[1],
        norm_new[2],
        head_new[0],
        head_new[1],
        head_new[2],
        bias_new[0],
        bias_new[1],
        bias_new[2],
        grad_norm,
        loss,
    )


def solution(mesh):
    in_specs = (
        P(("batch", "filt"), None),
        P(("batch", "filt")),
        P(("batch", "filt")),
        P(("batch", "filt")),
        P(),
        P(),
        P("filt", None),
        P(None, "filt", None, None),
        P(None, "filt"),
        P(None, "filt"),
        P(),
        P(),
        P(),
        P("filt", None),
        P("filt", None),
        P(None, "filt", None, None),
        P(None, "filt", None, None),
        P(None, "filt"),
        P(None, "filt"),
        P(None, "filt"),
        P(None, "filt"),
        P(),
        P(),
    )
    out_specs = (
        P(),
        P(),
        P(),
        P("filt", None),
        P("filt", None),
        P("filt", None),
        P(None, "filt", None, None),
        P(None, "filt", None, None),
        P(None, "filt", None, None),
        P(None, "filt"),
        P(None, "filt"),
        P(None, "filt"),
        P(None, "filt"),
        P(None, "filt"),
        P(None, "filt"),
        P(),
        P(),
        P(),
        P(),
        P(),
    )
    fits = mesh.shape["batch"] == NB and mesh.shape["filt"] == NF
    return jax.shard_map(fast_body if fits else body, mesh=mesh, in_specs=in_specs, out_specs=out_specs, check_vma=False)
```

```python
import jax
import jax.numpy as jnp
from jax import lax
from jax.experimental import pallas as pl
from jax.experimental.pallas import tpu as pltpu
from jax.sharding import PartitionSpec as P

STEP = 8

beta_one = 0.9
beta_two = 0.95
adam_eps = 1e-08
norm_epsilon = 1e-05
clip_norm = 0.01
own_share = 0.7

MESH = pl.DeviceIdType.MESH
bf16 = jnp.bfloat16
f32 = jnp.float32
LINE = bf16
NB, NF, NZ, NDEV, NCHIP = 4, 8, 4, 32, 16
C, IMG, ROWS = 640, 24, 1536
BLK = 8 * IMG
AC = (((1,), (1,)), ((), ()))
CC = (((0,), (0,)), ((), ()))


def iota(shape, dim):
    return lax.broadcasted_iota(jnp.int32, shape, dim)


def wide(row5):
    return jnp.concatenate([row5[k : k + 1, :] for k in range(5)], axis=1)


def column(row, n):
    eye = iota((n, n), 0) == iota((n, n), 1)
    return jnp.sum(jnp.where(eye, jnp.broadcast_to(row, (n, n)), 0.0), axis=1, keepdims=True)


class Place:
    def __init__(self):
        self.b = lax.axis_index("batch")
        self.f = lax.axis_index("filt")
        self.z = self.f // 2
        self.c = lax.rem(self.f, 2)
        self.me = self.b * NF + self.f
        self.chip = self.b * NZ + self.z
        self.xn = self.b + 1 - 2 * lax.rem(self.b, 2)
        self.yn = lax.rem(self.b + 2, NB)
        self.dn = (NB - 1) - self.b
        self.sib = self.f + 1 - 2 * self.c


def remote(src, dst, ssem, rsem, b, f):
    return pltpu.make_async_remote_copy(
        src_ref=src, dst_ref=dst, send_sem=ssem, recv_sem=rsem, device_id=(b, f), device_id_type=MESH
    )


def peers(p):
    for dz in (2, 1, 3, 0):
        for db in (3, 1, 2, 0):
            if dz or db:
                yield lax.rem(p.b + db, NB), lax.rem(p.z + dz, NZ)


def greet(p):
    sem = pltpu.get_barrier_semaphore()
    for b, z in peers(p):
        pl.semaphore_signal(sem, inc=1, device_id=(b, 2 * z + p.c), device_id_type=MESH)
    pl.semaphore_signal(sem, inc=1, device_id=(p.b, p.sib), device_id_type=MESH)


def met():
    pl.semaphore_wait(pltpu.get_barrier_semaphore(), NCHIP)


class Exchange:
    def __init__(self, p, slots, sibs, ssem, rsem, psem, qsem):
        self.p, self.slots, self.sibs = p, slots, sibs
        self.ssem, self.rsem, self.psem, self.qsem = ssem, rsem, psem, qsem

    def mine(self, e):
        return self.slots.at[e, self.p.chip]

    def send(self, e):
        p = self.p
        mine = self.mine(e)
        for b, z in peers(p):
            remote(mine, mine, self.ssem.at[e], self.rsem.at[e], b, 2 * z + p.c).start()

    def rest(self, e):
        p = self.p
        rest = self.slots.at[e, 0 : NCHIP - 1]
        return remote(rest, rest, self.ssem.at[e], self.rsem.at[e], p.b, p.sib)

    def across(self, e):
        p = self.p
        return remote(
            self.sibs.at[e, 0], self.sibs.at[e, 1], self.psem.at[e], self.qsem.at[e], p.b, p.sib
        )

    def wait(self, e):
        self.rest(e).wait_recv()

    def swap(self, e, value):
        self.sibs[e, 0] = value
        self.across(e).start()
        self.across(e).wait_recv()
        return self.sibs[e, 1]

    def drain(self, e):
        self.rest(e).wait_send()
        self.across(e).wait_send()

    def total(self, e):
        self.wait(e)
        own = jnp.sum(self.slots[e], axis=0)
        return own + self.swap(e, own)


def put_row(slot, row, value):
    for k in range(5):
        slot[row + k : row + k + 1, :] = value[:, 128 * k : 128 * k + 128]


def put_spare(slot, value):
    for k, row in enumerate((5, 6, 7, 13, 14)):
        slot[row : row + 1, :] = value[:, 128 * k : 128 * k + 128]


def spare(rows):
    return wide(jnp.concatenate([rows[5:8], rows[13:15]], axis=0))


def local_stats(src, mask, count, slot):
    def total(j, acc):
        x = src[pl.ds(pl.multiple_of(j * BLK, BLK), BLK), :]
        m = jnp.concatenate([mask[...]] * 5, axis=1)
        return acc + jnp.sum((x * m).reshape(BLK // 8, 8, C), axis=0)

    acc = lax.fori_loop(0, 8, total, jnp.zeros((8, C), f32))
    own_sum = jnp.sum(acc, axis=0, keepdims=True)
    own_mean = own_sum / jnp.maximum(count, 1.0)

    def squares(j, acc):
        x = src[pl.ds(pl.multiple_of(j * BLK, BLK), BLK), :]
        m = jnp.concatenate([mask[...]] * 5, axis=1)
        d = x - own_mean
        return acc + jnp.sum((d * d * m).reshape(BLK // 8, 8, C), axis=0)

    acc = lax.fori_loop(0, 8, squares, jnp.zeros((8, C), f32))
    put_row(slot, 0, own_sum)
    put_row(slot, 8, jnp.sum(acc, axis=0, keepdims=True))


def joint_stats(ex, e):
    ex.wait(e)
    every = ex.slots[e]
    n = ex.slots[0, :, 5:6, :]
    sums = every[:, 0:5, :]
    n_own, s_own = jnp.sum(n, axis=0), jnp.sum(sums, axis=0)
    m_own = s_own / jnp.maximum(n_own, 1.0)
    off = sums / jnp.maximum(n, 1.0) - m_own[None]
    q_own = jnp.sum(every[:, 8:13, :] + n * off * off, axis=0)
    rest = jnp.sum(every[:, 5:8, :], axis=0)
    more = jnp.sum(every[:, 13:16, :], axis=0)
    got = ex.swap(e, jnp.concatenate([s_own, rest, q_own, more], axis=0))
    n_sib = ex.sibs[0, 1, 5:6, :]
    s_sib, q_sib = got[0:5], got[8:13]
    count = n_own + n_sib
    mean = (s_own + s_sib) / count
    a, b = m_own - mean, s_sib / jnp.maximum(n_sib, 1.0) - mean
    spread = ((q_own + q_sib) + (n_own * a * a + n_sib * b * b)) / count
    return wide(mean), wide(lax.rsqrt(spread + norm_epsilon)), spare(got + jnp.concatenate([s_own, rest, q_own, more], axis=0))


def spread_rows(S, j, x):
    at = pl.ds(pl.multiple_of((j + 1) * BLK, BLK), BLK)
    gap = jnp.zeros((IMG, C), f32)
    S[0, at, :] = jnp.concatenate([gap, x[: BLK - IMG]], axis=0).astype(bf16)
    S[1, at, :] = x.astype(bf16)
    S[2, at, :] = jnp.concatenate([x[IMG:], gap], axis=0).astype(bf16)


def conv_part(S, W, k, u, r0, M):
    lhs = jnp.concatenate([S[u, pl.ds(r0 + v * BLK, M), :] for v in range(3)], axis=1)
    rhs = jnp.concatenate(
        [
            jnp.concatenate(
                [W[k, u, z, c, v * 80 : v * 80 + 80, :] for z in range(NZ) for c in range(2)], axis=0
            )
            for v in range(3)
        ],
        axis=1,
    )
    return lax.dot_general(lhs, rhs, AC, preferred_element_type=f32)


class Gather:
    def __init__(self, p, W, zs, zr, xs, xr, ds, dr):
        self.p, self.W = p, W
        self.zs, self.zr, self.xs, self.xr, self.ds, self.dr = zs, zr, xs, xr, ds, dr

    def part(self, s, z, b, row, n):
        return self.W.at[
            s // 3, lax.rem(s, 3), z, self.p.c, pl.ds(pl.multiple_of(b * 64 + row, 32), n), :
        ]

    def zcopy(self, s, i):
        p = self.p
        mine = self.part(s, p.z, p.b, 0, 64)
        to = lax.rem(p.z + i, NZ)
        return remote(mine, mine, self.zs.at[s, i], self.zr.at[s, i], p.b, 2 * to + p.c)

    def zsend(self, s):
        for i in (2, 1, 3):
            self.zcopy(s, i).start()

    def xcopy(self, s, i, d):
        p = self.p
        z = lax.rem(p.z + NZ - i, NZ)
        b, row, n, to = ((p.b, 0, 64, p.xn), (p.b, 0, 64, p.yn), (p.xn, 0, 32, p.yn), (p.yn, 32, 32, p.xn))[d]
        part = self.part(s, z, b, row, n)
        at = 3 * d + i - 1
        return remote(part, part, self.xs.at[s, at], self.xr.at[s, at], to, p.f)

    def relay(self, s):
        for i in range(1, NZ):
            self.zcopy(s, i).wait_recv()
            self.xcopy(s, i, 0).start()
            self.xcopy(s, i, 1).start()

    def turn(self, s):
        for i in range(1, NZ):
            self.xcopy(s, i, 0).wait_recv()
            self.xcopy(s, i, 2).start()
            self.xcopy(s, i, 1).wait_recv()
            self.xcopy(s, i, 3).start()

    def dcopy(self, s):
        p = self.p
        mine = self.W.at[s // 3, lax.rem(s, 3), :, p.c]
        return remote(mine, mine, self.ds.at[s], self.dr.at[s], p.b, p.sib)

    def across(self, s):
        for i in range(1, NZ):
            self.xcopy(s, i, 2).wait_recv()
            self.xcopy(s, i, 3).wait_recv()
        self.dcopy(s).start()

    def arrive(self, s):
        self.dcopy(s).wait_recv()

    def drain(self, s):
        for i in range(1, NZ):
            self.zcopy(s, i).wait_send()
            for d in range(4):
                self.xcopy(s, i, d).wait_send()
        self.dcopy(s).wait_send()


class Scatter:
    def __init__(self, p, W, RX, RZ, G, Q, GF, sems):
        self.p, self.W, self.RX, self.RZ, self.G, self.Q, self.GF = p, W, RX, RZ, G, Q, GF
        (self.bs, self.br, self.cs, self.cr, self.es, self.er) = sems

    def held(self, e, q, half):
        return self.G.at[e % 3, :, pl.ds(pl.multiple_of(q * 64 + 32 * half, 32), 32), :]

    def room(self, e, i):
        at = pl.ds(128 * (i % 2), 128)
        if e < 3:
            ref = self.RX.at[e, i // 2, at, :]
        else:
            ref = self.W.at[1, e % 3, i // 4, (i // 2) % 2, at, :]
        return ref

    def hop(self, e, i):
        p = self.p
        q, half, to = (
            (p.dn, 0, p.xn), (p.dn, 1, p.yn), (p.xn, 0, p.xn), (p.yn, 1, p.yn), (p.yn, 0, p.yn), (p.xn, 1, p.xn),
        )[i]
        return remote(
            self.held(e, q, half), self.room(e, i).reshape(NZ, 32, C), self.bs.at[e, i], self.br.at[e, i], to, p.f
        )

    def begin(self, e):
        for i in range(4):
            self.hop(e, i).start()

    def mid(self, e):
        p = self.p
        for i, q, half in ((0, p.yn, 0), (1, p.xn, 1)):
            self.hop(e, i).wait_recv()
            mine = self.held(e, q, half)
            got = self.room(e, i)[...].reshape(NZ, 32, C).astype(f32)
            mine[...] = (mine[...].astype(f32) + got).astype(bf16)
            self.hop(e, 4 + i).start()

    def out3(self, e, i):
        p = self.p
        to = lax.rem(p.z + i, NZ)
        return remote(
            self.Q.at[e % 3, to], self.RZ.at[e, i - 1], self.cs.at[e, i - 1], self.cr.at[e, i - 1], p.b, 2 * to + p.c
        )

    def out4(self, e, d):
        p = self.p
        to = (p.xn, p.yn, p.dn)[d]
        mine = self.GF.at[1 - e // 3, e % 3, pl.ds(pl.multiple_of(p.b * 64, 64), 64), :]
        return remote(mine, mine, self.es.at[e, d], self.er.at[e, d], to, p.f)

    def along(self, e):
        p = self.p
        for i in range(2, 6):
            self.hop(e, i).wait_recv()
        for half, ways in ((0, (2, 4)), (1, (3, 5))):
            acc = self.held(e, p.b, half)[...].astype(f32)
            for i in ways:
                acc = acc + self.room(e, i)[...].reshape(NZ, 32, C).astype(f32)
            self.Q[e % 3, :, 32 * half : 32 * half + 32, :] = acc.astype(self.Q.dtype)
        for i in (2, 1, 3):
            self.out3(e, i).start()

    def final(self, e, lost):
        p = self.p
        for i in range(1, NZ):
            self.out3(e, i).wait_recv()
        acc = self.Q[e % 3, p.z].astype(f32)
        for i in range(1, NZ):
            acc = acc + self.RZ[e, i - 1].astype(f32)
        acc = acc + lost
        low = acc.astype(bf16)
        self.GF[1 - e // 3, e % 3, pl.ds(pl.multiple_of(p.b * 64, 64), 64), :] = low
        for d in (2, 0, 1):
            self.out4(e, d).start()
        low = low.astype(f32)
        return jnp.sum((low * low).reshape(8, 8, C), axis=0)

    def clear(self, e):
        for i in range(6):
            self.hop(e, i).wait_send()
        for i in range(1, NZ):
            self.out3(e, i).wait_send()

    def end(self, e):
        for d in range(3):
            self.out4(e, d).wait()


def conv_back_rows(S, W, k, r0, M):
    acc = None
    for u in range(3):
        lhs = jnp.concatenate([S[2 - u, pl.ds(r0 + (2 - v) * BLK, M), :] for v in range(3)], axis=1)
        rhs = jnp.concatenate(
            [
                W[k, u, z, c, v * 80 : v * 80 + 80, :]
                for v in range(3)
                for z in range(NZ)
                for c in range(2)
            ],
            axis=0,
        )
        d = jnp.dot(lhs, rhs, preferred_element_type=f32)
        acc = d if acc is None else acc + d
    return acc


def own_rows(p, dyT):
    return jnp.concatenate([dyT[z, p.c] for z in range(NZ)], axis=0)


def sib_rows(dyS):
    return jnp.concatenate([dyS[z] for z in range(NZ)], axis=0)


def first_grad(p, S, dyT, acc):
    def tap(v, carry):
        at = pl.ds(pl.multiple_of(v * BLK, BLK), ROWS)
        acc[pl.ds(pl.multiple_of(v * 320, 320), 320), :] = jnp.dot(
            own_rows(p, dyT), S[0, at, :], preferred_element_type=f32
        )
        return carry

    lax.fori_loop(0, 3, tap, 0)


def filter_grad(p, S, S2, dyT, dyS, DS, mu, G, e, acc):
    u = e % 3
    if u == 0:
        ones = jnp.ones((ROWS, 128), bf16)
        DS[...] = jnp.dot(own_rows(p, dyT), ones, preferred_element_type=f32) + jnp.dot(
            sib_rows(dyS), ones, preferred_element_type=f32
        )

    def tap(v, carry):
        at = pl.ds(pl.multiple_of(v * BLK, BLK), ROWS)
        d = jnp.dot(sib_rows(dyS), S2[u, at, :], preferred_element_type=f32)
        if u == 0:
            d = d + acc[pl.ds(pl.multiple_of(v * 320, 320), 320), :]
        else:
            d = d + jnp.dot(own_rows(p, dyT), S[u, at, :], preferred_element_type=f32)
        d = d - jnp.concatenate([DS[...]] * 5, axis=1) * mu
        for z in range(NZ):
            G[u, z, pl.ds(pl.multiple_of(v * 80, 16), 80), :] = d[80 * z : 80 * z + 80].astype(bf16)
        return carry

    lax.fori_loop(0, 3, tap, 0)


def step_kernel(
    images, labels, partner, valid, sizes, stem_w, bridge_t, conv_w, norm, head, bias,
    GF, own_o, stem_o, misc_o,
    W, S, S2, dyT, dyS, DS, inner, block, dfl, RX, RZ, G, Q, slots, sibs, lab, gath, par, mask, AB, stem, dstem, pad,
    xs_, xr_, ps_, pr_, lbs, lbr, gs, gr, zs, zr, xs, xr, ds, dr, ls,
    bs, br, cs, cr, es, er, ts, tr, us, ur, free, fs, fr, hs, hr, js, jr, ms, mr,
):
    p = Place()
    ex = Exchange(p, slots, sibs, xs_, xr_, ps_, pr_)
    ga = Gather(p, W, zs, zr, xs, xr, ds, dr)
    sc = Scatter(p, W, RX, RZ, G, Q, GF, (bs, br, cs, cr, es, er))
    greet(p)
    def load(s):
        at = pl.ds(240 * s, 240)
        return pltpu.make_async_copy(conv_w.reshape(1440, C).at[at], block.at[at], ls.at[s])

    for s in range(6):
        load(s).start()
    mine = gath.at[p.z, p.c]
    mine[...] = jnp.zeros((40, 128), f32)
    mine[0:16, 0:80] = bridge_t[...]
    mine[16:22, 0:80] = norm[...]
    mine[24:34, 0:80] = head[...]

    def cast(s):
        load(s).wait()
        k, u = s // 3, s % 3
        for v in range(3):
            t = 9 * k + 3 * u + v
            W[k, u, p.z, p.c, 80 * v : 80 * v + 80, :] = block[80 * t : 80 * t + 80, :].astype(bf16)
        W[k, u, p.z, p.c, 240:256, :] = jnp.zeros((16, C), bf16)

    cast(0)
    met()
    for i in (2, 1, 3):
        to = lax.rem(p.z + i, NZ)
        remote(mine, mine, gs.at[0], gr.at[0], p.b, 2 * to + p.c).start()
    ga.zsend(0)
    for s in range(1, 6):
        cast(s)
        if s < 3:
            ga.zsend(s)
    img = pltpu.roll(images[...].astype(f32), 32, 1)
    lane = iota((IMG, 128), 1)
    for c in range(3):
        for i in range(8):
            a = img[:, 1024 * c + 128 * i : 1024 * c + 128 * i + 128]
            if i == 0:
                a = jnp.where(lane < 32, 0.0, a)
            AB[IMG * i : IMG * i + IMG, 128 * c : 128 * c + 128] = a
    tile_c = jnp.bitwise_and(iota((16, 128), 1), 15) == iota((16, 128), 0)
    wc = lax.dot_general(
        stem_w[...].astype(bf16), tile_c.astype(bf16), CC, preferred_element_type=f32
    )
    fold_r = (jnp.bitwise_and(iota((256, 27), 0), 31) == iota((256, 27), 1)).astype(bf16)
    own_j = iota((256, 128), 0) // 32 == iota((256, 128), 1) // 16
    bd = jnp.dot(fold_r, wc.astype(bf16), preferred_element_type=f32)
    bd = jnp.where(own_j, bd, 0.0).astype(bf16)
    l, r = iota((128, 256), 0), iota((128, 256), 1)
    v = jnp.bitwise_and(l, 31) - 4 * (r // 32) + 1

    def hits(c):
        want = 9 * c + 3 * (l // 32) + v
        hit = (l < 96) & (v >= 0) & (v < 3) & (want == jnp.bitwise_and(r, 31))
        return hit.astype(f32)

    acc = None
    for c in range(3):
        t = jnp.dot(hits(c).astype(bf16), bd, preferred_element_type=f32).astype(bf16)
        d = jnp.dot(
            AB[:, 128 * c : 128 * c + 128].astype(bf16), t, preferred_element_type=f32
        )
        acc = d if acc is None else acc + d
    stem[...] = acc.astype(bf16).astype(f32)
    ok = column(valid[...].astype(f32), IMG)
    q = p.f * IMG + iota((IMG, 1), 0)
    member = jnp.zeros((IMG, 1), jnp.int32)
    end = jnp.int32(0)
    for g in range(8):
        end = end + sizes[p.b, g]
        member = member + (q >= end).astype(jnp.int32)
    member = jnp.minimum(member, 7)
    size = jnp.zeros((IMG, 1), f32)
    for g in range(8):
        size = size + jnp.where(member == g, sizes[p.b, g].astype(f32), 0.0)
    weight = ok / size
    mask[...] = jnp.concatenate([jnp.broadcast_to(ok, (IMG, 128))] * 8, axis=0)
    count = 64.0 * jnp.sum(ok)
    own_row = labels[...].astype(f32)
    slot = ex.mine(0)
    slot[5:6, :] = jnp.full((1, 128), count, f32)
    slot[6:7, :] = jnp.concatenate([own_row, jnp.zeros((1, 104), f32)], axis=1)
    slot[7:8, :] = jnp.full((1, 128), jnp.sum(weight), f32)
    edge = jnp.zeros((BLK, C), bf16)
    for u in range(3):
        S[u, 0:BLK, :] = edge
        S[u, 9 * BLK : 10 * BLK, :] = edge
        for z in range(NZ):
            G[u, z, 240:256, :] = jnp.zeros((16, C), bf16)
    rest = gath.at[0 : NZ - 1, 0]
    remote(rest, rest, gs.at[0], gr.at[0], p.b, p.sib).wait()
    side = gath.at[:, p.c]
    pair = remote(side, side, gs.at[1], gr.at[1], p.b, p.sib)
    pair.start()
    pair.wait()
    lane = iota((40, 128), 1)
    for k in range(5):
        acc = jnp.zeros((40, 128), f32)
        for f in range(NF):
            lo, hi = max(80 * f, 128 * k), min(80 * f + 80, 128 * k + 128)
            if lo < hi:
                turned = pltpu.roll(gath[f // 2, f % 2], (80 * f - 128 * k) % 128, 1)
                acc = jnp.where((lane >= lo - 128 * k) & (lane < hi - 128 * k), turned, acc)
        par[:, 128 * k : 128 * k + 128] = acc
    bridge8 = jnp.concatenate([par[0:16, :].astype(bf16)] * 8, axis=0)

    def rows(j):
        return pl.ds(pl.multiple_of(j * BLK, BLK), BLK)

    def base_rows(j):
        pick = iota((BLK, 128), 1) // 16 == j
        x = jnp.where(pick, stem[...], 0.0).astype(bf16)
        return jnp.dot(x, bridge8, preferred_element_type=f32)

    def base_block(j, carry):
        inner[rows(j), :] = base_rows(j)
        return carry

    lax.fori_loop(0, 8, base_block, 0)
    local_stats(inner, mask, count, ex.mine(0))
    ex.send(0)
    ga.relay(0)
    ga.relay(1)
    ga.turn(0)

    def inner_rows(j):
        return inner[rows(j), :]

    def block_rows(j):
        return block[rows(j), :]

    def dfl_rows(j):
        return dfl[rows(j), :]

    def gain(k):
        return par[16 + 2 * k : 17 + 2 * k, :]

    def shift(k):
        return par[17 + 2 * k : 18 + 2 * k, :]

    def normed(src, stats, k):
        mean, scale = stats[:2]

        def one(j, acc):
            hat = (src(j) - mean) * scale
            out = jnp.maximum(gain(k) * hat + shift(k), 0.0)
            spread_rows(S, j, out)
            m = jnp.concatenate([mask[...]] * 5, axis=1)
            return acc + jnp.sum((out * m).reshape(BLK // 8, 8, C), axis=0)

        acc = lax.fori_loop(0, 8, one, jnp.zeros((8, C), f32))
        return jnp.sum(acc, axis=0, keepdims=True)

    stats0 = joint_stats(ex, 0)
    labs = remote(lab.at[0], lab.at[1], lbs, lbr, p.b, p.sib)
    lab[0] = slots[0, :, 6, :]
    labs.start()
    put_spare(ex.mine(1), normed(inner_rows, stats0, 0))
    for s in range(3, 6):
        ga.zsend(s)

    def conv(k, u, dst, start, acts):
        def one(it, carry):
            r0 = pl.multiple_of(it * 384, 384)
            at = pl.ds(r0, 384)
            d = conv_part(S, W, k, u, r0, 384)
            dst[at, :] = (dst[at, :] if start is None else start(it)) + d if start != 0 else d
            for when, act in acts.items():
                pl.when(it == when)(act)
            return carry

        lax.fori_loop(0, 4, one, 0)

    def share(u):
        return remote(S.at[u], S2.at[u], ts.at[u], tr.at[u], p.b, p.sib)

    def doing(f, *a):
        return lambda: f(*a)

    ga.relay(2)
    ga.turn(1)
    ga.across(0)
    ga.arrive(0)
    conv(0, 0, inner, 0, {0: doing(ga.turn, 2), 1: doing(ga.relay, 3)})
    ga.across(1)
    ga.relay(4)
    ga.across(2)
    ga.arrive(1)
    conv(0, 1, inner, None, {})
    ga.arrive(2)
    conv(0, 2, inner, None, {0: doing(ga.turn, 3), 2: doing(ga.relay, 5)})
    local_stats(inner, mask, count, ex.mine(1))
    ex.send(1)
    ga.turn(4)
    ga.across(3)
    stats1 = joint_stats(ex, 1)
    ga.turn(5)
    put_spare(ex.mine(2), normed(inner_rows, stats1, 1))
    ga.arrive(3)
    conv(1, 0, block, lambda it: jnp.concatenate([base_rows(2 * it), base_rows(2 * it + 1)], axis=0),
         {1: doing(ga.across, 4), 3: doing(ga.across, 5)})
    ga.arrive(4)
    for u in range(3):
        share(u).start()
    conv(1, 1, block, None, {})
    ga.arrive(5)
    conv(1, 2, block, None, {})
    local_stats(block, mask, count, ex.mine(2))
    ex.send(2)
    for s in range(6):
        ga.drain(s)
    lane = iota((IMG, 16), 1)
    label = column(own_row, IMG)
    mate = column(partner[...].astype(f32), IMG)
    home = jnp.floor((mate + 0.5) / 24.0)
    chip = jnp.floor((home + 0.5) / 2.0)
    at_chip = (iota((IMG, NCHIP), 1).astype(f32) == chip).astype(bf16)
    labs.wait()
    own_side = jnp.dot(at_chip, lab[0].astype(bf16), preferred_element_type=f32)
    sib_side = jnp.dot(at_chip, lab[1].astype(bf16), preferred_element_type=f32)
    there = jnp.where(home - 2.0 * chip == p.c.astype(f32), own_side, sib_side)
    spot = iota((IMG, 128), 1).astype(f32) == mate - 24.0 * home
    mate_label = jnp.sum(jnp.where(spot, there, 0.0), axis=1, keepdims=True)
    lane_f = lane.astype(f32)
    target = own_share * (lane_f == label).astype(f32) + (1.0 - own_share) * (
        lane_f == mate_label
    ).astype(f32)
    live = lane < 10
    head16 = par[24:40, :].astype(bf16)
    pad[...] = jnp.zeros((8, 128), f32)
    pad[0:1, 0:10] = bias[...]
    sides = sibs[0, 0] + sibs[0, 1]
    total = jnp.sum(sides[7:8, 0:1])
    valid_count = jnp.sum(sides[5:6, 0:1])
    stats2 = joint_stats(ex, 2)
    mu0, mu1 = stats1[2] / valid_count, stats2[2] / valid_count

    def pool(j, acc):
        hat = (block_rows(j) - stats2[0]) * stats2[1]
        out = jnp.maximum(gain(2) * hat + shift(2), 0.0)
        return acc + jnp.sum(out.reshape(8, IMG, C), axis=0)

    pooled = lax.fori_loop(0, 8, pool, jnp.zeros((IMG, C), f32)) / 64.0
    pooled = pooled.astype(bf16)
    logits = lax.dot_general(pooled, head16, AC, preferred_element_type=f32) + pad[0:1, 0:16]
    top = jnp.max(jnp.where(live, logits, -3e38), axis=1, keepdims=True)
    moved = jnp.where(live, logits - top, 0.0)
    size_sum = jnp.sum(jnp.where(live, jnp.exp(moved), 0.0), axis=1, keepdims=True)
    logp = moved - jnp.log(size_sum)
    loss_part = -jnp.sum(
        weight * jnp.sum(jnp.where(live, target * logp, 0.0), axis=1, keepdims=True)
    )
    d_logits = jnp.where(live, (jnp.exp(logp) - target) * (weight / total), 0.0).astype(bf16)
    g_bias = jnp.sum(d_logits.astype(f32), axis=0, keepdims=True)
    par[24:40, :] = lax.dot_general(d_logits, pooled, CC, preferred_element_type=f32)
    d_pooled = jnp.dot(d_logits, head16, preferred_element_type=f32)
    d_out24 = d_pooled / 64.0

    def zhat(src, j, stats):
        return (src(j) - stats[0]) * stats[1]

    def passed(hat, k, d_out):
        return jnp.where(gain(k) * hat + shift(k) > 0.0, d_out, 0.0)

    def grad_sums(src, stats, k, d_of, e):
        def one(j, acc):
            hat = zhat(src, j, stats)
            got = passed(hat, k, d_of(j))
            return (
                acc[0] + jnp.sum(got.reshape(BLK // 8, 8, C), axis=0),
                acc[1] + jnp.sum((got * hat).reshape(BLK // 8, 8, C), axis=0),
            )

        zero = jnp.zeros((8, C), f32)
        acc = lax.fori_loop(0, 8, one, (zero, zero))
        put_row(ex.mine(e), 0, jnp.sum(acc[0], axis=0, keepdims=True))
        put_row(ex.mine(e), 8, jnp.sum(acc[1], axis=0, keepdims=True))

    def grad_rows(src, stats, k, d_of, sums, j):
        hat = zhat(src, j, stats)
        m = jnp.concatenate([mask[...]] * 5, axis=1)
        got = passed(hat, k, d_of(j))
        return (gain(k) * stats[1]) * (got - m * (sums[0] + hat * sums[1]) / valid_count)

    def head_rows(j):
        return jnp.concatenate([d_out24] * 8, axis=0)

    def turn(src):
        for it in range(4):
            x = src[384 * it : 384 * it + 384, :].T.astype(bf16)
            for f in range(NF):
                dyT[f // 2, f % 2, :, 384 * it : 384 * it + 384] = x[80 * f : 80 * f + 80]

    trade = remote(dyT.at[:, 1 - p.c], dyS, us, ur, p.b, p.sib)

    grad_sums(block_rows, stats2, 2, head_rows, 3)
    slot = ex.mine(3)
    slot[5:6, :] = jnp.full((1, 128), loss_part, f32)
    slot[6:7, :] = jnp.concatenate([g_bias, jnp.zeros((1, 112), f32)], axis=1)
    ex.send(3)
    tot3 = ex.total(3)
    sums2 = wide(tot3[0:5]), wide(tot3[8:13])

    def low_sums(dst, src, stats, k, d_of, sums):
        def one(j, acc):
            d = grad_rows(src, stats, k, d_of, sums, j)
            dst[rows(j), :] = d
            return acc + jnp.sum(d.astype(bf16).astype(f32).reshape(BLK // 8, 8, C), axis=0)

        acc = lax.fori_loop(0, 8, one, jnp.zeros((8, C), f32))
        return jnp.sum(acc, axis=0, keepdims=True)

    def lost(dy_sums, mu):
        at = 64 * p.b + iota((64, C), 0)
        o = at - 80 * ((at >= 80).astype(jnp.int32) + (at >= 160).astype(jnp.int32))
        hit = (iota((64, C), 1) == 80 * p.f + o) & (at < 240)
        return jnp.sum(jnp.where(hit, dy_sums, 0.0), axis=1, keepdims=True) * mu

    put_spare(ex.mine(4), low_sums(block, block_rows, stats2, 2, head_rows, sums2))
    turn(block)
    trade.start()
    first_grad(p, S, dyT, dfl)
    for u in range(3):
        share(u).wait()
    trade.wait()
    filter_grad(p, S, S2, dyT, dyS, DS, mu1, G, 0, dfl)
    sc.begin(0)
    filter_grad(p, S, S2, dyT, dyS, DS, mu1, G, 1, dfl)
    sc.begin(1)
    filter_grad(p, S, S2, dyT, dyS, DS, mu1, G, 2, dfl)
    sc.mid(0)
    sc.begin(2)
    pl.semaphore_signal(free, inc=1, device_id=(p.b, p.sib), device_id_type=MESH)

    def spread(src):
        def one(j, carry):
            spread_rows(S, j, src[rows(j), :])
            return carry

        lax.fori_loop(0, 8, one, 0)

    spread(block)

    def back_conv1(it, carry):
        r0 = pl.multiple_of(it * 384, 384)
        dfl[pl.ds(r0, 384), :] = conv_back_rows(S, W, 1, r0, 384)

        @pl.when(it == 1)
        def _():
            sc.mid(1)

        @pl.when(it == 3)
        def _():
            sc.mid(2)

        return carry

    lax.fori_loop(0, 4, back_conv1, 0)
    grad_sums(inner_rows, stats1, 1, dfl_rows, 4)
    ex.send(4)
    normed(base_rows, stats0, 0)
    pl.semaphore_wait(free, 1)
    share(0).start()
    sc.along(0)
    tot4 = ex.total(4)
    sums1 = wide(tot4[0:5]), wide(tot4[8:13])
    lost1 = lost(spare(tot4), mu1)
    put_spare(ex.mine(5), low_sums(dfl, inner_rows, stats1, 1, dfl_rows, sums1))
    turn(dfl)
    trade.start()
    for u in range(1, 3):
        share(u).start()
    sc.along(1)
    first_grad(p, S, dyT, inner)
    sc.along(2)
    sc.clear(0)
    share(0).wait()
    trade.wait()
    filter_grad(p, S, S2, dyT, dyS, DS, mu0, G, 3, inner)
    sc.begin(3)
    squares = sc.final(0, lost1)
    sc.clear(1)
    share(1).wait()
    filter_grad(p, S, S2, dyT, dyS, DS, mu0, G, 4, inner)
    sc.begin(4)
    squares = squares + sc.final(1, lost1)
    sc.clear(2)
    share(2).wait()
    filter_grad(p, S, S2, dyT, dyS, DS, mu0, G, 5, inner)
    sc.mid(3)
    sc.begin(5)
    squares = squares + sc.final(2, lost1)
    spread(dfl)

    def back_conv0(it, carry):
        r0 = pl.multiple_of(it * 384, 384)
        inner[pl.ds(r0, 384), :] = conv_back_rows(S, W, 0, r0, 384)

        @pl.when(it == 1)
        def _():
            sc.mid(4)

        @pl.when(it == 2)
        def _():
            sc.along(3)

        return carry

    lax.fori_loop(0, 4, back_conv0, 0)

    grad_sums(base_rows, stats0, 0, inner_rows, 5)
    ex.send(5)
    sc.mid(5)
    sc.along(4)
    tot5 = ex.total(5)
    lost0 = lost(spare(tot5), mu0)
    squares = squares + sc.final(3, lost0)
    sums0 = wide(tot5[0:5]), wide(tot5[8:13])
    grid16 = dfl.at[512:640]
    grid16[...] = jnp.zeros((128, C), f32)
    dstem[...] = jnp.zeros((BLK, 128), f32)

    def back0(j, carry):
        d = block[rows(j), :] + grad_rows(base_rows, stats0, 0, inner_rows, sums0, j)
        d = d.astype(bf16)
        pick = iota((BLK, 128), 1) // 16 == j
        x = jnp.where(pick, stem[...], 0.0).astype(bf16)
        grid16[...] += lax.dot_general(x, d, CC, preferred_element_type=f32)
        y = lax.dot_general(d, bridge8, AC, preferred_element_type=f32)
        dstem[...] += jnp.where(pick, y, 0.0)
        return carry

    lax.fori_loop(0, 8, back0, 0)
    acc = grid16[0:16, :]
    for j in range(1, 8):
        acc = acc + grid16[16 * j : 16 * j + 16, :]
    dfl[0:16, :] = acc
    dfl[16:32, :] = par[24:40, :]

    def half(row, c):
        return dfl.at[pl.ds(pl.multiple_of(row + 16 * c, 16), 16), :]

    give = remote(half(0, 1 - p.c), half(32, 1 - p.c), fs, fr, p.b, p.sib)
    give.start()
    sc.along(5)
    low = dstem[...].astype(bf16)
    high = lax.Precision.HIGHEST
    acc = None
    for c in range(3):
        t = lax.dot_general(
            AB[:, 128 * c : 128 * c + 128].astype(bf16), low, CC, preferred_element_type=f32
        )
        d = lax.dot_general(hits(c), t, CC, precision=high, preferred_element_type=f32)
        acc = d if acc is None else acc + d
    acc = jnp.where(own_j, acc, 0.0)
    fold = (jnp.bitwise_and(iota((256, 128), 0), 31) == iota((256, 128), 1)).astype(f32)
    acc = lax.dot_general(acc, fold, CC, precision=high, preferred_element_type=f32)
    slots[6, p.chip] = jnp.dot(
        tile_c.astype(f32), acc, precision=high, preferred_element_type=f32
    )
    ex.send(6)
    give.wait()
    zline = dfl.at[pl.ds(pl.multiple_of(64 + 16 * p.z, 16), 16), :]
    zline[...] = half(0, p.c)[...] + half(32, p.c)[...]
    for i in range(1, NZ):
        to = lax.rem(p.z + i, NZ)
        remote(zline, zline, hs, hr, p.b, 2 * to + p.c).start()
    squares = squares + sc.final(4, lost0)
    rest = dfl.at[64 : 64 + 16 * (NZ - 1), :]
    remote(rest, rest, hs, hr, p.b, p.sib).wait()
    square = dfl.at[pl.ds(pl.multiple_of(128 + 16 * p.b, 16), 16), :]
    square[...] = jnp.sum(dfl[64:128, :].reshape(NZ, 16, C), axis=0)
    for i in range(1, NB):
        to = lax.rem(p.b + i, NB)
        remote(square, square, js, jr, to, p.f).start()
    g_stem = ex.total(6)
    squares = squares + sc.final(5, lost0)
    slots[7, p.chip] = jnp.full((16, 128), jnp.sum(squares), f32)
    ex.send(7)
    rest = dfl.at[128 : 128 + 16 * (NB - 1), :]
    remote(rest, rest, js, jr, p.b, p.sib).wait()
    done = half(192, p.c)
    done[...] = jnp.sum(dfl[128:192, :].reshape(NB, 16, C), axis=0)
    give = remote(done, done, ms, mr, p.b, p.sib)
    give.start()
    give.wait()
    both = dfl[192:224, :]
    bias_all = tot3[6:7, :]
    stem_o[...] = g_stem
    ng = [row for sums in (sums0, sums1, sums2) for row in (sums[1], sums[0])]
    ng = jnp.concatenate(ng + [jnp.zeros((2, C), f32)], axis=0)
    every = jnp.concatenate([both, ng], axis=0)
    pick = (iota((C, 128), 0) == 80 * p.f + iota((C, 128), 1)) & (iota((C, 128), 1) < 80)
    own_o[...] = jnp.dot(every, pick.astype(f32), precision=high, preferred_element_type=f32)
    other = jnp.sum(every * every) + jnp.sum(g_stem * g_stem) + jnp.sum(bias_all * bias_all)
    conv_sq = ex.total(7)[0:1, :]
    misc_o[...] = jnp.zeros((8, 128), f32)
    misc_o[0:1, :] = jnp.sqrt(conv_sq + other)
    misc_o[1:2, :] = tot3[5:6, :] / total
    misc_o[2:3, :] = bias_all
    for e in range(6):
        sc.end(e)
    for e in range(3, 6):
        sc.clear(e)
    for e in range(8):
        ex.drain(e)


def step_call(images, labels, partner, valid, sizes, stem_w, bridge_t, conv_w, norm, head, bias):
    V, A, SM = pltpu.VMEM, pl.ANY, pltpu.SMEM
    spec = lambda m: pl.BlockSpec(memory_space=m)
    D = pltpu.SemaphoreType.DMA
    sh = jax.ShapeDtypeStruct
    return pl.pallas_call(
        step_kernel,
        out_shape=(
            sh((2, 3, 256, C), bf16), sh((40, 128), f32), sh((16, 128), f32), sh((8, 128), f32),
        ),
        in_specs=[
            spec(V), spec(V), spec(V), spec(V), spec(SM), spec(V), spec(V), spec(A), spec(V), spec(V), spec(V),
        ],
        out_specs=(spec(V),) * 4,
        scratch_shapes=[
            V((2, 3, NZ, 2, 256, C), bf16), V((3, 10 * BLK, C), bf16), V((3, 10 * BLK, C), bf16),
            V((NZ, 2, 80, ROWS), bf16), V((NZ, 80, ROWS), bf16), V((NZ * 80, 128), f32),
            V((ROWS, C), f32), V((ROWS, C), f32), V((ROWS, C), f32),
            V((3, 3, 256, C), bf16), V((6, 3, 64, C), LINE), V((3, NZ, 256, C), bf16), V((3, NZ, 64, C), LINE),
            V((8, NCHIP, 16, 128), f32), V((8, 2, 16, 128), f32), V((2, NCHIP, 128), f32), V((NZ, 2, 40, 128), f32), V((40, C), f32),
            V((BLK, 128), f32), V((BLK, 384), f32), V((BLK, 128), f32), V((BLK, 128), f32), V((8, 128), f32),
            D((8,)), D((8,)), D((8,)), D((8,)), D, D, D((2,)), D((2,)), D((6, 4)), D((6, 4)), D((6, 12)), D((6, 12)), D((6,)), D((6,)), D((6,)),
            D((6, 6)), D((6, 6)), D((6, 3)), D((6, 3)), D((6, 3)), D((6, 3)), D((3,)), D((3,)), D, D,
            pltpu.SemaphoreType.REGULAR, D, D, D, D, D, D, D, D,
        ],
        compiler_params=pltpu.CompilerParams(
            collective_id=0, has_side_effects=True, vmem_limit_bytes=63 << 20
        ),
    )(images, labels, partner, valid, sizes, stem_w, bridge_t, conv_w, norm, head, bias)


def adam_rule(g, w, m, v, rate, shrink, factor):
    clipped = g * factor
    m = beta_one * m + (1.0 - beta_one) * clipped
    v = beta_two * v + (1.0 - beta_two) * clipped * clipped
    ahead = m / (1.0 - beta_one**STEP)
    behind = v / (1.0 - beta_two**STEP)
    return w - rate * (ahead / (jnp.sqrt(behind) + adam_eps) + shrink * w), m, v


def adam_kernel(G, misc, own, stem_g, *refs):
    ins, outs = refs[:18], refs[18:]
    factor = clip_norm / jnp.maximum(misc[0:1, :], clip_norm)

    def write(i, g, rate, shrink, f):
        w, m, v = (r[...] for r in ins[3 * i : 3 * i + 3])
        for o, x in zip(outs[3 * i : 3 * i + 3], adam_rule(g, w, m, v, rate, shrink, f)):
            o[...] = x

    g = G[0, 0, 0:240, :].astype(f32)
    write(0, g[None, None], 0.033, 0.05, jnp.concatenate([factor] * 5, axis=1)[None, None])

    @pl.when((pl.program_id(0) == 0) & (pl.program_id(1) == 0))
    def _():
        write(1, stem_g[:, 0:27], 0.5, 0.05, factor[:, 0:27])
        write(2, own[0:16, 0:80], 0.6, 0.05, factor[:, 0:80])
        write(3, own[32:38, 0:80], 0.5, 0.0, factor[:, 0:80])
        write(4, own[16:26, 0:80], 0.1, 0.05, factor[:, 0:80])
        write(5, misc[2:3, 0:10], 0.5, 0.0, factor[:, 0:10])


def adam_call(G, misc, own, stem_g, *state):
    whole = lambda x: pl.BlockSpec(x.shape, lambda k, u: (0,) * x.ndim)
    tile = lambda n: pl.BlockSpec((1, 1, n, C), lambda k, u: (k, u, 0, 0))
    specs = [tile(240)] * 3 + [whole(x) for x in state[3:]]
    return pl.pallas_call(
        adam_kernel,
        out_shape=tuple(jax.ShapeDtypeStruct(x.shape, f32) for x in state),
        grid=(2, 3),
        in_specs=[tile(256), whole(misc), whole(own), whole(stem_g)] + specs,
        out_specs=tuple(specs),
        compiler_params=pltpu.CompilerParams(vmem_limit_bytes=62 << 20),
    )(G, misc, own, stem_g, *state)


def make_patches(images):
    number = images.shape[0]
    grid = images.reshape(number, 3, 32, 32)
    padded = jnp.pad(grid, ((0, 0), (0, 0), (1, 1), (1, 1)))
    pieces = [
        padded[:, :, row_off : row_off + 29 : 4, col_off : col_off + 29 : 4]
        for row_off in range(3)
        for col_off in range(3)
    ]
    stacked = jnp.stack(pieces, axis=2)
    return jnp.transpose(stacked, (1, 2, 0, 3, 4)).reshape(27, number * 64)


def shifted(feature_field):
    width, rows = feature_field.shape
    grid = feature_field.reshape(width, rows // 64, 8, 8)
    padded = jnp.pad(grid, ((0, 0), (0, 0), (1, 1), (1, 1)))
    pieces = [
        padded[:, :, row_off : row_off + 8, col_off : col_off + 8]
        for row_off in range(3)
        for col_off in range(3)
    ]
    return jnp.stack(pieces, axis=0).reshape(9 * width, rows)


def unshifted(parts, width):
    rows = parts.shape[1]
    grid = parts.reshape(9, width, rows // 64, 8, 8)
    summed = jnp.zeros((width, rows // 64, 10, 10), jnp.float32)
    for row_off in range(3):
        for col_off in range(3):
            summed = summed + jnp.pad(
                grid[3 * row_off + col_off],
                ((0, 0), (0, 0), (row_off, 2 - row_off), (col_off, 2 - col_off)),
            )
    return summed[:, :, 1:9, 1:9].reshape(width, rows)


def image_weights(valid_mask, group_sizes):
    shards, groups = group_sizes.shape
    capacity = valid_mask.shape[0] // shards
    group_ends = jnp.cumsum(group_sizes, axis=1)
    slot_index = jnp.arange(capacity, dtype=jnp.int32)
    member = jnp.sum(
        (slot_index[None, :, None] >= group_ends[:, None, :]).astype(jnp.int32), axis=2
    )
    member = jnp.minimum(member, groups - 1)
    chosen = (member[:, :, None] == jnp.arange(groups, dtype=jnp.int32)[None, None, :]).astype(
        jnp.float32
    )
    sizes_each = jnp.sum(chosen * group_sizes[:, None, :].astype(jnp.float32), axis=2)
    return valid_mask.astype(jnp.float32) / sizes_each.reshape(-1)


def norm_forward(feature_field, norm_gain, norm_shift, row_validity_mask, valid_count):
    batch_mean = (
        lax.psum(jnp.sum(feature_field * row_validity_mask, axis=1), ("batch", "filt"))
        / valid_count
    )
    centered_input = feature_field - batch_mean[:, None]
    batch_variance = (
        lax.psum(
            jnp.sum(centered_input * centered_input * row_validity_mask, axis=1), ("batch", "filt")
        )
        / valid_count
    )
    inverse_scale = lax.rsqrt(batch_variance + norm_epsilon)
    normalized_input = (feature_field - batch_mean[:, None]) * inverse_scale[:, None]
    norm_output = jnp.maximum(norm_gain[:, None] * normalized_input + norm_shift[:, None], 0.0)
    return (norm_output, normalized_input, inverse_scale)


def masked_norm_backward(
    output_gradient,
    norm_output,
    normalized_input,
    inverse_scale,
    norm_gain,
    row_validity_mask,
    valid_count,
):
    passed_rows = jnp.where(norm_output > 0.0, output_gradient, 0.0)
    shift_gradient, gain_gradient = lax.psum(
        (jnp.sum(passed_rows, axis=1), jnp.sum(passed_rows * normalized_input, axis=1)),
        ("batch", "filt"),
    )
    input_gradient = (
        passed_rows
        - row_validity_mask[None, :]
        * (shift_gradient[:, None] + normalized_input * gain_gradient[:, None])
        / valid_count
    )
    return ((norm_gain * inverse_scale)[:, None] * input_gradient, gain_gradient, shift_gradient)


def conv_forward(feature_field, weight_shard):
    stacked = shifted(feature_field)
    low_shard = weight_shard.astype(jnp.bfloat16)
    piece = lax.all_gather(low_shard, "filt", axis=0, tiled=True)
    norm_output = jnp.dot(
        piece.reshape(piece.shape[0], -1), stacked, preferred_element_type=jnp.float32
    )
    return (norm_output, None)


def conv_backward(feature_field, weight_shard, output_gradient):
    width = feature_field.shape[0]
    stacked = shifted(feature_field)
    rows_grad = output_gradient
    term = lax.dot_general(
        rows_grad, stacked, (((1,), (1,)), ((), ())), preferred_element_type=jnp.float32
    )
    weight_grad = lax.psum_scatter(
        term.reshape(lax.axis_size("filt") * weight_shard.shape[0], 9, width),
        "filt",
        scatter_dimension=0,
        tiled=True,
    )
    piece = lax.all_gather(weight_shard.astype(jnp.bfloat16), "filt", axis=0, tiled=True)
    rows_grad = output_gradient
    back = lax.dot_general(
        piece.reshape(piece.shape[0], -1),
        rows_grad,
        (((0,), (0,)), ((), ())),
        preferred_element_type=jnp.float32,
    )
    return (unshifted(back, width), weight_grad)


def adam_step(weight, output_gradient, first, second, rate, shrink, factor):
    clipped = output_gradient * factor
    first = beta_one * first + (1.0 - beta_one) * clipped
    second = beta_two * second + (1.0 - beta_two) * clipped * clipped
    ahead = first / (1.0 - beta_one**STEP)
    behind = second / (1.0 - beta_two**STEP)
    return (
        weight - rate * (ahead / (jnp.sqrt(behind) + adam_eps) + shrink * weight),
        first,
        second,
    )


def body(
    images,
    labels,
    partner,
    valid_mask,
    group_sizes,
    stem_weight,
    bridge_weight,
    conv_weight,
    norm_params,
    head_weight,
    head_bias,
    stem_first,
    stem_second,
    bridge_first,
    bridge_second,
    conv_first,
    conv_second,
    norm_first,
    norm_second,
    head_first,
    head_second,
    bias_first,
    bias_second,
):
    width = bridge_weight.shape[0]
    bridge_all, norm_all, head_all = (
        lax.all_gather(bridge_weight, "filt", axis=0, tiled=True),
        lax.all_gather(norm_params, "filt", axis=1, tiled=True),
        lax.all_gather(head_weight, "filt", axis=1, tiled=True),
    )
    labels_all, valid_all = (
        lax.all_gather(labels, ("batch", "filt"), axis=0, tiled=True),
        lax.all_gather(valid_mask, ("batch", "filt"), axis=0, tiled=True),
    )
    weight_all = image_weights(valid_all, group_sizes)
    total = jnp.sum(weight_all)
    valid_count = 64.0 * jnp.sum(valid_all.astype(jnp.float32))
    local = images.shape[0]
    image_weight = lax.dynamic_slice_in_dim(
        weight_all, lax.axis_index(("batch", "filt")) * local, local
    )
    row_validity_mask = jnp.repeat(valid_mask.astype(jnp.float32), 64)
    patch = make_patches(images)
    stem = jnp.dot(
        stem_weight.astype(jnp.bfloat16), patch, preferred_element_type=jnp.float32
    ).astype(jnp.bfloat16)
    base = jnp.dot(bridge_all.astype(jnp.bfloat16), stem, preferred_element_type=jnp.float32)
    first, first_hat, first_scale = norm_forward(
        base, norm_all[0], norm_all[1], row_validity_mask, valid_count
    )
    first_low = first.astype(jnp.bfloat16)
    inner, kept_zero = conv_forward(first_low, conv_weight[0])
    second, second_hat, second_scale = norm_forward(
        inner, norm_all[2], norm_all[3], row_validity_mask, valid_count
    )
    second_low = second.astype(jnp.bfloat16)
    branch, kept_one = conv_forward(second_low, conv_weight[1])
    final, final_hat, final_scale = norm_forward(
        base + branch, norm_all[4], norm_all[5], row_validity_mask, valid_count
    )
    pooled = jnp.mean(final.reshape(final.shape[0], local, 64), axis=2).astype(jnp.bfloat16)
    logits = (
        jnp.dot(head_all.astype(jnp.bfloat16), pooled, preferred_element_type=jnp.float32)
        + head_bias[:, None]
    )
    moved = logits - jnp.max(logits, axis=0, keepdims=True)
    logp = moved - jnp.log(jnp.sum(jnp.exp(moved), axis=0, keepdims=True))
    classes = jnp.arange(logits.shape[0], dtype=jnp.int32)
    partner_labels = jnp.take(labels_all, partner)
    target = own_share * (labels[None, :] == classes[:, None]).astype(jnp.float32) + (
        1.0 - own_share
    ) * (partner_labels[None, :] == classes[:, None]).astype(jnp.float32)
    loss_part = -jnp.sum(image_weight * jnp.sum(target * logp, axis=0))
    d_logits = ((jnp.exp(logp) - target) * (image_weight / total)[None, :]).astype(jnp.bfloat16)
    bias_grad = jnp.sum(d_logits.astype(jnp.float32), axis=1)
    head_grad = lax.dot_general(
        d_logits, pooled, (((1,), (1,)), ((), ())), preferred_element_type=jnp.float32
    )
    d_pooled = lax.dot_general(
        head_all.astype(jnp.bfloat16),
        d_logits,
        (((0,), (0,)), ((), ())),
        preferred_element_type=jnp.float32,
    )
    d_final = jnp.repeat(d_pooled / 64.0, 64, axis=1)
    d_block, gain_two, shift_two = masked_norm_backward(
        d_final, final, final_hat, final_scale, norm_all[4], row_validity_mask, valid_count
    )
    d_second, conv_grad_one = conv_backward(
        second_low, conv_weight[1], d_block.astype(jnp.bfloat16)
    )
    d_inner, gain_one, shift_one = masked_norm_backward(
        d_second, second, second_hat, second_scale, norm_all[2], row_validity_mask, valid_count
    )
    d_first, conv_grad_zero = conv_backward(first_low, conv_weight[0], d_inner.astype(jnp.bfloat16))
    d_lower, gain_zero, shift_zero = masked_norm_backward(
        d_first, first, first_hat, first_scale, norm_all[0], row_validity_mask, valid_count
    )
    d_base = (d_block + d_lower).astype(jnp.bfloat16)
    bridge_grad = lax.dot_general(
        d_base, stem, (((1,), (1,)), ((), ())), preferred_element_type=jnp.float32
    )
    d_stem = lax.dot_general(
        bridge_all.astype(jnp.bfloat16),
        d_base,
        (((0,), (0,)), ((), ())),
        preferred_element_type=jnp.float32,
    ).astype(jnp.bfloat16)
    stem_grad = lax.dot_general(
        d_stem, patch, (((1,), (1,)), ((), ())), preferred_element_type=jnp.float32
    )
    bridge_part, head_part = (
        lax.psum_scatter(bridge_grad, "filt", scatter_dimension=0, tiled=True),
        lax.psum_scatter(head_grad, "filt", scatter_dimension=1, tiled=True),
    )
    conv_grad, bridge_sum, head_sum = lax.psum(
        (jnp.stack([conv_grad_zero, conv_grad_one]), bridge_part, head_part), "batch"
    )
    stem_sum, bias_sum, loss_sum = lax.psum((stem_grad, bias_grad, loss_part), ("batch", "filt"))
    norm_full = jnp.stack([gain_zero, shift_zero, gain_one, shift_one, gain_two, shift_two])
    norm_grad = lax.dynamic_slice_in_dim(norm_full, lax.axis_index("filt") * width, width, 1)
    owned_square = (
        jnp.sum(conv_grad * conv_grad)
        + jnp.sum(bridge_sum * bridge_sum)
        + jnp.sum(norm_grad * norm_grad)
        + jnp.sum(head_sum * head_sum)
    )
    squares_all = (
        lax.psum(owned_square, "filt") + jnp.sum(stem_sum * stem_sum) + jnp.sum(bias_sum * bias_sum)
    )
    grad_norm = jnp.sqrt(squares_all)
    factor = clip_norm / jnp.maximum(grad_norm, clip_norm)
    stem_new = adam_step(stem_weight, stem_sum, stem_first, stem_second, 0.5, 0.05, factor)
    bridge_new = adam_step(
        bridge_weight, bridge_sum, bridge_first, bridge_second, 0.6, 0.05, factor
    )
    conv_new = adam_step(conv_weight, conv_grad, conv_first, conv_second, 0.033, 0.05, factor)
    norm_new = adam_step(norm_params, norm_grad, norm_first, norm_second, 0.5, 0.0, factor)
    head_new = adam_step(head_weight, head_sum, head_first, head_second, 0.1, 0.05, factor)
    bias_new = adam_step(head_bias, bias_sum, bias_first, bias_second, 0.5, 0.0, factor)
    return (
        stem_new[0],
        stem_new[1],
        stem_new[2],
        bridge_new[0],
        bridge_new[1],
        bridge_new[2],
        conv_new[0],
        conv_new[1],
        conv_new[2],
        norm_new[0],
        norm_new[1],
        norm_new[2],
        head_new[0],
        head_new[1],
        head_new[2],
        bias_new[0],
        bias_new[1],
        bias_new[2],
        grad_norm,
        loss_sum / total,
    )


def fast_body(
    images, labels, partner, valid_mask, group_sizes, stem_weight, bridge_weight, conv_weight, norm_params,
    head_weight, head_bias, stem_first, stem_second, bridge_first, bridge_second, conv_first, conv_second,
    norm_first, norm_second, head_first, head_second, bias_first, bias_second,
):
    width = bridge_weight.shape[0]
    def rows(x):
        return x.transpose(0, 2, 1, 3).reshape(2, 3, 3 * width, C)

    def back(x):
        return x.reshape(2, 9, width, C).transpose(0, 2, 1, 3)

    G, own, stem_g, misc = step_call(
        images, labels[None], partner[None], valid_mask[None], group_sizes, stem_weight, bridge_weight.T,
        conv_weight.transpose(0, 2, 1, 3), norm_params, head_weight, head_bias[None],
    )
    new = adam_call(
        G, misc, own, stem_g,
        rows(conv_weight), rows(conv_first), rows(conv_second),
        stem_weight, stem_first, stem_second,
        bridge_weight.T, bridge_first.T, bridge_second.T,
        norm_params, norm_first, norm_second,
        head_weight, head_first, head_second,
        head_bias[None], bias_first[None], bias_second[None],
    )
    conv, stem, bridge, norm, head, bias = (new[i : i + 3] for i in range(0, 18, 3))
    return (
        *stem,
        *(x.T for x in bridge),
        *(back(x) for x in conv),
        *norm,
        *head,
        *(x[0] for x in bias),
        misc[0, 0],
        misc[1, 0],
    )


def solution(mesh):
    in_specs = (
        P(("batch", "filt"), None),
        P(("batch", "filt")),
        P(("batch", "filt")),
        P(("batch", "filt")),
        P(),
        P(),
        P("filt", None),
        P(None, "filt", None, None),
        P(None, "filt"),
        P(None, "filt"),
        P(),
        P(),
        P(),
        P("filt", None),
        P("filt", None),
        P(None, "filt", None, None),
        P(None, "filt", None, None),
        P(None, "filt"),
        P(None, "filt"),
        P(None, "filt"),
        P(None, "filt"),
        P(),
        P(),
    )
    out_specs = (
        P(),
        P(),
        P(),
        P("filt", None),
        P("filt", None),
        P("filt", None),
        P(None, "filt", None, None),
        P(None, "filt", None, None),
        P(None, "filt", None, None),
        P(None, "filt"),
        P(None, "filt"),
        P(None, "filt"),
        P(None, "filt"),
        P(None, "filt"),
        P(None, "filt"),
        P(),
        P(),
        P(),
        P(),
        P(),
    )
    fits = mesh.shape["batch"] == NB and mesh.shape["filt"] == NF
    return jax.shard_map(fast_body if fits else body, mesh=mesh, in_specs=in_specs, out_specs=out_specs, check_vma=False)
```

```python
import jax
import jax.numpy as jnp
from jax import lax
from jax.experimental import pallas as pl
from jax.experimental.pallas import tpu as pltpu
from jax.sharding import PartitionSpec as P

STEP = 8

beta_one = 0.9
beta_two = 0.95
adam_eps = 1e-08
norm_epsilon = 1e-05
clip_norm = 0.01
own_share = 0.7

MESH = pl.DeviceIdType.MESH
bf16 = jnp.bfloat16
f32 = jnp.float32
LINE = bf16
NB, NF, NZ, NDEV, NCHIP = 4, 8, 4, 32, 16
C, IMG, ROWS = 640, 24, 1536
BLK = 8 * IMG
AC = (((1,), (1,)), ((), ()))
CC = (((0,), (0,)), ((), ()))


def iota(shape, dim):
    return lax.broadcasted_iota(jnp.int32, shape, dim)


def wide(row5):
    return jnp.concatenate([row5[k : k + 1, :] for k in range(5)], axis=1)


def column(row, n):
    eye = iota((n, n), 0) == iota((n, n), 1)
    return jnp.sum(jnp.where(eye, jnp.broadcast_to(row, (n, n)), 0.0), axis=1, keepdims=True)


class Place:
    def __init__(self):
        self.b = lax.axis_index("batch")
        self.f = lax.axis_index("filt")
        self.z = self.f // 2
        self.c = lax.rem(self.f, 2)
        self.me = self.b * NF + self.f
        self.chip = self.b * NZ + self.z
        self.xn = self.b + 1 - 2 * lax.rem(self.b, 2)
        self.yn = lax.rem(self.b + 2, NB)
        self.dn = (NB - 1) - self.b
        self.sib = self.f + 1 - 2 * self.c


def remote(src, dst, ssem, rsem, b, f):
    return pltpu.make_async_remote_copy(
        src_ref=src, dst_ref=dst, send_sem=ssem, recv_sem=rsem, device_id=(b, f), device_id_type=MESH
    )


def peers(p):
    for dz in (2, 1, 3, 0):
        for db in (3, 1, 2, 0):
            if dz or db:
                yield lax.rem(p.b + db, NB), lax.rem(p.z + dz, NZ)


def greet(p):
    sem = pltpu.get_barrier_semaphore()
    for b, z in peers(p):
        pl.semaphore_signal(sem, inc=1, device_id=(b, 2 * z + p.c), device_id_type=MESH)
    pl.semaphore_signal(sem, inc=1, device_id=(p.b, p.sib), device_id_type=MESH)


def met():
    pl.semaphore_wait(pltpu.get_barrier_semaphore(), NCHIP)


class Exchange:
    def __init__(self, p, slots, sibs, ssem, rsem, psem, qsem):
        self.p, self.slots, self.sibs = p, slots, sibs
        self.ssem, self.rsem, self.psem, self.qsem = ssem, rsem, psem, qsem

    def mine(self, e):
        return self.slots.at[e, self.p.chip]

    def send(self, e):
        p = self.p
        mine = self.mine(e)
        for b, z in peers(p):
            remote(mine, mine, self.ssem.at[e], self.rsem.at[e], b, 2 * z + p.c).start()

    def rest(self, e):
        p = self.p
        rest = self.slots.at[e, 0 : NCHIP - 1]
        return remote(rest, rest, self.ssem.at[e], self.rsem.at[e], p.b, p.sib)

    def across(self, e):
        p = self.p
        return remote(
            self.sibs.at[e, 0], self.sibs.at[e, 1], self.psem.at[e], self.qsem.at[e], p.b, p.sib
        )

    def wait(self, e):
        self.rest(e).wait_recv()

    def swap(self, e, value):
        self.sibs[e, 0] = value
        self.across(e).start()
        self.across(e).wait_recv()
        return self.sibs[e, 1]

    def drain(self, e):
        self.rest(e).wait_send()
        self.across(e).wait_send()

    def total(self, e):
        self.wait(e)
        own = jnp.sum(self.slots[e], axis=0)
        return own + self.swap(e, own)


def put_row(slot, row, value):
    for k in range(5):
        slot[row + k : row + k + 1, :] = value[:, 128 * k : 128 * k + 128]


def put_spare(slot, value):
    for k, row in enumerate((5, 6, 7, 13, 14)):
        slot[row : row + 1, :] = value[:, 128 * k : 128 * k + 128]


def spare(rows):
    return wide(jnp.concatenate([rows[5:8], rows[13:15]], axis=0))


def local_stats(src, mask, count, slot):
    def total(j, acc):
        x = src[pl.ds(pl.multiple_of(j * BLK, BLK), BLK), :]
        m = jnp.concatenate([mask[...]] * 5, axis=1)
        return acc + jnp.sum((x * m).reshape(BLK // 8, 8, C), axis=0)

    acc = lax.fori_loop(0, 8, total, jnp.zeros((8, C), f32))
    own_sum = jnp.sum(acc, axis=0, keepdims=True)
    own_mean = own_sum / jnp.maximum(count, 1.0)

    def squares(j, acc):
        x = src[pl.ds(pl.multiple_of(j * BLK, BLK), BLK), :]
        m = jnp.concatenate([mask[...]] * 5, axis=1)
        d = x - own_mean
        return acc + jnp.sum((d * d * m).reshape(BLK // 8, 8, C), axis=0)

    acc = lax.fori_loop(0, 8, squares, jnp.zeros((8, C), f32))
    put_row(slot, 0, own_sum)
    put_row(slot, 8, jnp.sum(acc, axis=0, keepdims=True))


def joint_stats(ex, e):
    ex.wait(e)
    every = ex.slots[e]
    n = ex.slots[0, :, 5:6, :]
    sums = every[:, 0:5, :]
    n_own, s_own = jnp.sum(n, axis=0), jnp.sum(sums, axis=0)
    m_own = s_own / jnp.maximum(n_own, 1.0)
    off = sums / jnp.maximum(n, 1.0) - m_own[None]
    q_own = jnp.sum(every[:, 8:13, :] + n * off * off, axis=0)
    rest = jnp.sum(every[:, 5:8, :], axis=0)
    more = jnp.sum(every[:, 13:16, :], axis=0)
    got = ex.swap(e, jnp.concatenate([s_own, rest, q_own, more], axis=0))
    n_sib = ex.sibs[0, 1, 5:6, :]
    s_sib, q_sib = got[0:5], got[8:13]
    count = n_own + n_sib
    mean = (s_own + s_sib) / count
    a, b = m_own - mean, s_sib / jnp.maximum(n_sib, 1.0) - mean
    spread = ((q_own + q_sib) + (n_own * a * a + n_sib * b * b)) / count
    return wide(mean), wide(lax.rsqrt(spread + norm_epsilon)), spare(got + jnp.concatenate([s_own, rest, q_own, more], axis=0))


def spread_rows(S, j, x):
    at = pl.ds(pl.multiple_of((j + 1) * BLK, BLK), BLK)
    gap = jnp.zeros((IMG, C), f32)
    S[0][at, :] = jnp.concatenate([gap, x[: BLK - IMG]], axis=0).astype(bf16)
    S[1][at, :] = x.astype(bf16)
    S[2][at, :] = jnp.concatenate([x[IMG:], gap], axis=0).astype(bf16)


def conv_part(S, W, k, u, r0, M):
    lhs = jnp.concatenate([S[u][pl.ds(r0 + v * BLK, M), :] for v in range(3)], axis=1)
    rhs = jnp.concatenate(
        [
            jnp.concatenate(
                [W[k, u, z, c, v * 80 : v * 80 + 80, :] for z in range(NZ) for c in range(2)], axis=0
            )
            for v in range(3)
        ],
        axis=1,
    )
    return lax.dot_general(lhs, rhs, AC, preferred_element_type=f32)


class Gather:
    def __init__(self, p, W, zs, zr, xs, xr, ds, dr):
        self.p, self.W = p, W
        self.zs, self.zr, self.xs, self.xr, self.ds, self.dr = zs, zr, xs, xr, ds, dr

    def part(self, s, z, b, row, n):
        return self.W.at[
            s // 3, lax.rem(s, 3), z, self.p.c, pl.ds(pl.multiple_of(b * 64 + row, 32), n), :
        ]

    def zcopy(self, s, i):
        p = self.p
        mine = self.part(s, p.z, p.b, 0, 64)
        to = lax.rem(p.z + i, NZ)
        return remote(mine, mine, self.zs.at[s, i], self.zr.at[s, i], p.b, 2 * to + p.c)

    def zsend(self, s):
        for i in (2, 1, 3):
            self.zcopy(s, i).start()

    def xcopy(self, s, i, d):
        p = self.p
        z = lax.rem(p.z + NZ - i, NZ)
        b, row, n, to = ((p.b, 0, 64, p.xn), (p.b, 0, 64, p.yn), (p.xn, 0, 32, p.yn), (p.yn, 32, 32, p.xn))[d]
        part = self.part(s, z, b, row, n)
        at = 3 * d + i - 1
        return remote(part, part, self.xs.at[s, at], self.xr.at[s, at], to, p.f)

    def relay(self, s):
        for i in range(1, NZ):
            self.zcopy(s, i).wait_recv()
            self.xcopy(s, i, 0).start()
            self.xcopy(s, i, 1).start()

    def turn(self, s):
        for i in range(1, NZ):
            self.xcopy(s, i, 0).wait_recv()
            self.xcopy(s, i, 2).start()
            self.xcopy(s, i, 1).wait_recv()
            self.xcopy(s, i, 3).start()

    def dcopy(self, s):
        p = self.p
        mine = self.W.at[s // 3, lax.rem(s, 3), :, p.c]
        return remote(mine, mine, self.ds.at[s], self.dr.at[s], p.b, p.sib)

    def across(self, s):
        for i in range(1, NZ):
            self.xcopy(s, i, 2).wait_recv()
            self.xcopy(s, i, 3).wait_recv()
        self.dcopy(s).start()

    def arrive(self, s):
        self.dcopy(s).wait_recv()

    def drain(self, s):
        for i in range(1, NZ):
            self.zcopy(s, i).wait_send()
            for d in range(4):
                self.xcopy(s, i, d).wait_send()
        self.dcopy(s).wait_send()


class Scatter:
    def __init__(self, p, W, RX, RZ, G, Q, GF, sems):
        self.p, self.W, self.RX, self.RZ, self.G, self.Q, self.GF = p, W, RX, RZ, G, Q, GF
        (self.bs, self.br, self.cs, self.cr, self.es, self.er) = sems

    def held(self, e, q, half):
        return self.G.at[e % 3, :, pl.ds(pl.multiple_of(q * 64 + 32 * half, 32), 32), :]

    def room(self, e, i):
        at = pl.ds(128 * (i % 2), 128)
        if e < 3:
            ref = self.RX.at[e, i // 2, at, :]
        else:
            ref = self.W.at[1, e % 3, i // 4, (i // 2) % 2, at, :]
        return ref

    def hop(self, e, i):
        p = self.p
        q, half, to = (
            (p.dn, 0, p.xn), (p.dn, 1, p.yn), (p.xn, 0, p.xn), (p.yn, 1, p.yn), (p.yn, 0, p.yn), (p.xn, 1, p.xn),
        )[i]
        return remote(
            self.held(e, q, half), self.room(e, i).reshape(NZ, 32, C), self.bs.at[e, i], self.br.at[e, i], to, p.f
        )

    def begin(self, e):
        for i in range(4):
            self.hop(e, i).start()

    def mid(self, e):
        p = self.p
        for i, q, half in ((0, p.yn, 0), (1, p.xn, 1)):
            self.hop(e, i).wait_recv()
            mine = self.held(e, q, half)
            got = self.room(e, i)[...].reshape(NZ, 32, C).astype(f32)
            mine[...] = (mine[...].astype(f32) + got).astype(bf16)
            self.hop(e, 4 + i).start()

    def out3(self, e, i):
        p = self.p
        to = lax.rem(p.z + i, NZ)
        return remote(
            self.Q.at[e % 3, to], self.RZ.at[e, i - 1], self.cs.at[e, i - 1], self.cr.at[e, i - 1], p.b, 2 * to + p.c
        )

    def out4(self, e, d):
        p = self.p
        to = (p.xn, p.yn, p.dn)[d]
        mine = self.GF.at[1 - e // 3, e % 3, pl.ds(pl.multiple_of(p.b * 64, 64), 64), :]
        return remote(mine, mine, self.es.at[e, d], self.er.at[e, d], to, p.f)

    def along(self, e):
        p = self.p
        for i in range(2, 6):
            self.hop(e, i).wait_recv()
        for half, ways in ((0, (2, 4)), (1, (3, 5))):
            acc = self.held(e, p.b, half)[...].astype(f32)
            for i in ways:
                acc = acc + self.room(e, i)[...].reshape(NZ, 32, C).astype(f32)
            self.Q[e % 3, :, 32 * half : 32 * half + 32, :] = acc.astype(self.Q.dtype)
        for i in (2, 1, 3):
            self.out3(e, i).start()

    def final(self, e, lost):
        p = self.p
        for i in range(1, NZ):
            self.out3(e, i).wait_recv()
        acc = self.Q[e % 3, p.z].astype(f32)
        for i in range(1, NZ):
            acc = acc + self.RZ[e, i - 1].astype(f32)
        acc = acc + lost
        low = acc.astype(bf16)
        self.GF[1 - e // 3, e % 3, pl.ds(pl.multiple_of(p.b * 64, 64), 64), :] = low
        for d in (2, 0, 1):
            self.out4(e, d).start()
        low = low.astype(f32)
        return jnp.sum((low * low).reshape(8, 8, C), axis=0)

    def clear(self, e):
        for i in range(6):
            self.hop(e, i).wait_send()

    def clear_line(self, e):
        for i in range(1, NZ):
            self.out3(e, i).wait_send()

    def end(self, e):
        for d in range(3):
            self.out4(e, d).wait()


def conv_back_rows(S, W, k, r0, M):
    acc = None
    for u in range(3):
        lhs = jnp.concatenate([S[2 - u][pl.ds(r0 + (2 - v) * BLK, M), :] for v in range(3)], axis=1)
        rhs = jnp.concatenate(
            [
                W[k, u, z, c, v * 80 : v * 80 + 80, :]
                for v in range(3)
                for z in range(NZ)
                for c in range(2)
            ],
            axis=0,
        )
        d = jnp.dot(lhs, rhs, preferred_element_type=f32)
        acc = d if acc is None else acc + d
    return acc


def own_rows(p, dyT):
    return jnp.concatenate([dyT[z, p.c] for z in range(NZ)], axis=0)


def sib_rows(dyS):
    return jnp.concatenate([dyS[z] for z in range(NZ)], axis=0)


def first_grad(p, S, dyT, acc):
    def tap(v, carry):
        at = pl.ds(pl.multiple_of(v * BLK, BLK), ROWS)
        acc[pl.ds(pl.multiple_of(v * 320, 320), 320), :] = jnp.dot(
            own_rows(p, dyT), S[0][at, :], preferred_element_type=f32
        )
        return carry

    lax.fori_loop(0, 3, tap, 0)


def filter_grad(p, S, S2, dyT, dyS, DS, mu, G, e, acc):
    u = e % 3
    if u == 0:
        ones = jnp.ones((ROWS, 128), bf16)
        DS[...] = jnp.dot(own_rows(p, dyT), ones, preferred_element_type=f32) + jnp.dot(
            sib_rows(dyS), ones, preferred_element_type=f32
        )

    def tap(v, carry):
        at = pl.ds(pl.multiple_of(v * BLK, BLK), ROWS)
        d = jnp.dot(sib_rows(dyS), S2[u, at, :], preferred_element_type=f32)
        if u == 0:
            d = d + acc[pl.ds(pl.multiple_of(v * 320, 320), 320), :]
        else:
            d = d + jnp.dot(own_rows(p, dyT), S[u][at, :], preferred_element_type=f32)
        d = d - jnp.concatenate([DS[...]] * 5, axis=1) * mu
        for z in range(NZ):
            G[u, z, pl.ds(pl.multiple_of(v * 80, 16), 80), :] = d[80 * z : 80 * z + 80].astype(bf16)
        return carry

    lax.fori_loop(0, 3, tap, 0)


def step_kernel(
    images, labels, partner, valid, sizes, stem_w, bridge_t, conv_w, norm, head, bias,
    GF, own_o, stem_o, misc_o,
    W, S, S2, S3, dyT, dyS, DS, inner, block, dfl, RX, RZ, G, Q, slots, sibs, lab, gath, par, mask, AB, stem, dstem, pad,
    xs_, xr_, ps_, pr_, lbs, lbr, gs, gr, zs, zr, xs, xr, ds, dr, ls,
    bs, br, cs, cr, es, er, ts, tr, us, ur, free, fs, fr, hs, hr, js, jr, ms, mr,
):
    p = Place()
    ex = Exchange(p, slots, sibs, xs_, xr_, ps_, pr_)
    ga = Gather(p, W, zs, zr, xs, xr, ds, dr)
    sc = Scatter(p, W, RX, RZ, G, Q, GF, (bs, br, cs, cr, es, er))
    greet(p)
    SA = [S.at[u] for u in range(3)]
    SB = [S.at[0], S.at[1], S3]
    def load(s):
        at = pl.ds(240 * s, 240)
        return pltpu.make_async_copy(conv_w.reshape(1440, C).at[at], block.at[at], ls.at[s])

    for s in range(6):
        load(s).start()
    mine = gath.at[p.z, p.c]
    mine[...] = jnp.zeros((40, 128), f32)
    mine[0:16, 0:80] = bridge_t[...]
    mine[16:22, 0:80] = norm[...]
    mine[24:34, 0:80] = head[...]

    def cast(s):
        load(s).wait()
        k, u = s // 3, s % 3
        for v in range(3):
            t = 9 * k + 3 * u + v
            W[k, u, p.z, p.c, 80 * v : 80 * v + 80, :] = block[80 * t : 80 * t + 80, :].astype(bf16)
        W[k, u, p.z, p.c, 240:256, :] = jnp.zeros((16, C), bf16)

    cast(0)
    met()
    for i in (2, 1, 3):
        to = lax.rem(p.z + i, NZ)
        remote(mine, mine, gs.at[0], gr.at[0], p.b, 2 * to + p.c).start()
    ga.zsend(0)
    for s in range(1, 6):
        cast(s)
        if s < 3:
            ga.zsend(s)
    img = pltpu.roll(images[...].astype(f32), 32, 1)
    lane = iota((IMG, 128), 1)
    for c in range(3):
        for i in range(8):
            a = img[:, 1024 * c + 128 * i : 1024 * c + 128 * i + 128]
            if i == 0:
                a = jnp.where(lane < 32, 0.0, a)
            AB[IMG * i : IMG * i + IMG, 128 * c : 128 * c + 128] = a
    tile_c = jnp.bitwise_and(iota((16, 128), 1), 15) == iota((16, 128), 0)
    wc = lax.dot_general(
        stem_w[...].astype(bf16), tile_c.astype(bf16), CC, preferred_element_type=f32
    )
    fold_r = (jnp.bitwise_and(iota((256, 27), 0), 31) == iota((256, 27), 1)).astype(bf16)
    own_j = iota((256, 128), 0) // 32 == iota((256, 128), 1) // 16
    bd = jnp.dot(fold_r, wc.astype(bf16), preferred_element_type=f32)
    bd = jnp.where(own_j, bd, 0.0).astype(bf16)
    l, r = iota((128, 256), 0), iota((128, 256), 1)
    v = jnp.bitwise_and(l, 31) - 4 * (r // 32) + 1

    def hits(c):
        want = 9 * c + 3 * (l // 32) + v
        hit = (l < 96) & (v >= 0) & (v < 3) & (want == jnp.bitwise_and(r, 31))
        return hit.astype(f32)

    acc = None
    for c in range(3):
        t = jnp.dot(hits(c).astype(bf16), bd, preferred_element_type=f32).astype(bf16)
        d = jnp.dot(
            AB[:, 128 * c : 128 * c + 128].astype(bf16), t, preferred_element_type=f32
        )
        acc = d if acc is None else acc + d
    stem[...] = acc.astype(bf16).astype(f32)
    ok = column(valid[...].astype(f32), IMG)
    q = p.f * IMG + iota((IMG, 1), 0)
    member = jnp.zeros((IMG, 1), jnp.int32)
    end = jnp.int32(0)
    for g in range(8):
        end = end + sizes[p.b, g]
        member = member + (q >= end).astype(jnp.int32)
    member = jnp.minimum(member, 7)
    size = jnp.zeros((IMG, 1), f32)
    for g in range(8):
        size = size + jnp.where(member == g, sizes[p.b, g].astype(f32), 0.0)
    weight = ok / size
    mask[...] = jnp.concatenate([jnp.broadcast_to(ok, (IMG, 128))] * 8, axis=0)
    count = 64.0 * jnp.sum(ok)
    own_row = labels[...].astype(f32)
    slot = ex.mine(0)
    slot[5:6, :] = jnp.full((1, 128), count, f32)
    slot[6:7, :] = jnp.concatenate([own_row, jnp.zeros((1, 104), f32)], axis=1)
    slot[7:8, :] = jnp.full((1, 128), jnp.sum(weight), f32)
    edge = jnp.zeros((BLK, C), bf16)
    S3[0:BLK, :] = edge
    S3[9 * BLK : 10 * BLK, :] = edge
    for u in range(3):
        S[u, 0:BLK, :] = edge
        S[u, 9 * BLK : 10 * BLK, :] = edge
        for z in range(NZ):
            G[u, z, 240:256, :] = jnp.zeros((16, C), bf16)
    rest = gath.at[0 : NZ - 1, 0]
    remote(rest, rest, gs.at[0], gr.at[0], p.b, p.sib).wait()
    side = gath.at[:, p.c]
    pair = remote(side, side, gs.at[1], gr.at[1], p.b, p.sib)
    pair.start()
    pair.wait()
    lane = iota((40, 128), 1)
    for k in range(5):
        acc = jnp.zeros((40, 128), f32)
        for f in range(NF):
            lo, hi = max(80 * f, 128 * k), min(80 * f + 80, 128 * k + 128)
            if lo < hi:
                turned = pltpu.roll(gath[f // 2, f % 2], (80 * f - 128 * k) % 128, 1)
                acc = jnp.where((lane >= lo - 128 * k) & (lane < hi - 128 * k), turned, acc)
        par[:, 128 * k : 128 * k + 128] = acc
    bridge8 = jnp.concatenate([par[0:16, :].astype(bf16)] * 8, axis=0)

    def rows(j):
        return pl.ds(pl.multiple_of(j * BLK, BLK), BLK)

    def base_rows(j):
        pick = iota((BLK, 128), 1) // 16 == j
        x = jnp.where(pick, stem[...], 0.0).astype(bf16)
        return jnp.dot(x, bridge8, preferred_element_type=f32)

    def base_block(j, carry):
        inner[rows(j), :] = base_rows(j)
        return carry

    lax.fori_loop(0, 8, base_block, 0)
    local_stats(inner, mask, count, ex.mine(0))
    ex.send(0)
    ga.relay(0)
    ga.relay(1)
    ga.turn(0)

    def inner_rows(j):
        return inner[rows(j), :]

    def block_rows(j):
        return block[rows(j), :]

    def dfl_rows(j):
        return dfl[rows(j), :]

    def gain(k):
        return par[16 + 2 * k : 17 + 2 * k, :]

    def shift(k):
        return par[17 + 2 * k : 18 + 2 * k, :]

    def normed(src, stats, k, S):
        mean, scale = stats[:2]

        def one(j, acc):
            hat = (src(j) - mean) * scale
            out = jnp.maximum(gain(k) * hat + shift(k), 0.0)
            spread_rows(S, j, out)
            m = jnp.concatenate([mask[...]] * 5, axis=1)
            return acc + jnp.sum((out * m).reshape(BLK // 8, 8, C), axis=0)

        acc = lax.fori_loop(0, 8, one, jnp.zeros((8, C), f32))
        return jnp.sum(acc, axis=0, keepdims=True)

    stats0 = joint_stats(ex, 0)
    labs = remote(lab.at[0], lab.at[1], lbs, lbr, p.b, p.sib)
    lab[0] = slots[0, :, 6, :]
    labs.start()
    put_spare(ex.mine(1), normed(inner_rows, stats0, 0, SA))
    for s in range(3, 6):
        ga.zsend(s)

    def conv(k, u, dst, start, acts):
        def one(it, carry):
            r0 = pl.multiple_of(it * 384, 384)
            at = pl.ds(r0, 384)
            d = conv_part(SB if k else SA, W, k, u, r0, 384)
            dst[at, :] = (dst[at, :] if start is None else start(it)) + d if start != 0 else d
            for when, act in acts.items():
                pl.when(it == when)(act)
            return carry

        lax.fori_loop(0, 4, one, 0)

    def share(u, S=SA):
        return remote(S[u], S2.at[u], ts.at[u], tr.at[u], p.b, p.sib)

    def doing(f, *a):
        return lambda: f(*a)

    ga.relay(2)
    ga.turn(1)
    ga.across(0)
    ga.arrive(0)
    conv(0, 0, inner, 0, {0: doing(ga.turn, 2), 1: doing(ga.relay, 3)})
    ga.across(1)
    ga.across(2)
    ga.arrive(1)
    conv(0, 1, inner, None, {1: doing(ga.relay, 4)})
    ga.arrive(2)
    conv(0, 2, inner, None, {0: doing(ga.turn, 3), 2: doing(ga.relay, 5)})
    ga.turn(4)
    local_stats(inner, mask, count, ex.mine(1))
    ex.send(1)
    ga.across(3)
    ga.turn(5)
    stats1 = joint_stats(ex, 1)
    put_spare(ex.mine(2), normed(inner_rows, stats1, 1, SB))
    ga.arrive(3)
    conv(1, 0, block, lambda it: jnp.concatenate([base_rows(2 * it), base_rows(2 * it + 1)], axis=0),
         {1: doing(ga.across, 4), 3: doing(ga.across, 5)})
    ga.arrive(4)
    for u in range(3):
        share(u, SB).start()
    conv(1, 1, block, None, {})
    ga.arrive(5)
    conv(1, 2, block, None, {})
    local_stats(block, mask, count, ex.mine(2))
    ex.send(2)
    for s in range(6):
        ga.drain(s)
    lane = iota((IMG, 16), 1)
    label = column(own_row, IMG)
    mate = column(partner[...].astype(f32), IMG)
    home = jnp.floor((mate + 0.5) / 24.0)
    chip = jnp.floor((home + 0.5) / 2.0)
    at_chip = (iota((IMG, NCHIP), 1).astype(f32) == chip).astype(bf16)
    labs.wait()
    own_side = jnp.dot(at_chip, lab[0].astype(bf16), preferred_element_type=f32)
    sib_side = jnp.dot(at_chip, lab[1].astype(bf16), preferred_element_type=f32)
    there = jnp.where(home - 2.0 * chip == p.c.astype(f32), own_side, sib_side)
    spot = iota((IMG, 128), 1).astype(f32) == mate - 24.0 * home
    mate_label = jnp.sum(jnp.where(spot, there, 0.0), axis=1, keepdims=True)
    lane_f = lane.astype(f32)
    target = own_share * (lane_f == label).astype(f32) + (1.0 - own_share) * (
        lane_f == mate_label
    ).astype(f32)
    live = lane < 10
    head16 = par[24:40, :].astype(bf16)
    pad[...] = jnp.zeros((8, 128), f32)
    pad[0:1, 0:10] = bias[...]
    sides = sibs[0, 0] + sibs[0, 1]
    total = jnp.sum(sides[7:8, 0:1])
    valid_count = jnp.sum(sides[5:6, 0:1])
    stats2 = joint_stats(ex, 2)
    mu0, mu1 = stats1[2] / valid_count, stats2[2] / valid_count

    def pool(j, acc):
        hat = (block_rows(j) - stats2[0]) * stats2[1]
        out = jnp.maximum(gain(2) * hat + shift(2), 0.0)
        return acc + jnp.sum(out.reshape(8, IMG, C), axis=0)

    pooled = lax.fori_loop(0, 8, pool, jnp.zeros((IMG, C), f32)) / 64.0
    pooled = pooled.astype(bf16)
    logits = lax.dot_general(pooled, head16, AC, preferred_element_type=f32) + pad[0:1, 0:16]
    top = jnp.max(jnp.where(live, logits, -3e38), axis=1, keepdims=True)
    moved = jnp.where(live, logits - top, 0.0)
    size_sum = jnp.sum(jnp.where(live, jnp.exp(moved), 0.0), axis=1, keepdims=True)
    logp = moved - jnp.log(size_sum)
    loss_part = -jnp.sum(
        weight * jnp.sum(jnp.where(live, target * logp, 0.0), axis=1, keepdims=True)
    )
    d_logits = jnp.where(live, (jnp.exp(logp) - target) * (weight / total), 0.0).astype(bf16)
    g_bias = jnp.sum(d_logits.astype(f32), axis=0, keepdims=True)
    par[24:40, :] = lax.dot_general(d_logits, pooled, CC, preferred_element_type=f32)
    d_pooled = jnp.dot(d_logits, head16, preferred_element_type=f32)
    d_out24 = d_pooled / 64.0

    def zhat(src, j, stats):
        return (src(j) - stats[0]) * stats[1]

    def passed(hat, k, d_out):
        return jnp.where(gain(k) * hat + shift(k) > 0.0, d_out, 0.0)

    def grad_sums(src, stats, k, d_of, e):
        def one(j, acc):
            hat = zhat(src, j, stats)
            got = passed(hat, k, d_of(j))
            return (
                acc[0] + jnp.sum(got.reshape(BLK // 8, 8, C), axis=0),
                acc[1] + jnp.sum((got * hat).reshape(BLK // 8, 8, C), axis=0),
            )

        zero = jnp.zeros((8, C), f32)
        acc = lax.fori_loop(0, 8, one, (zero, zero))
        put_row(ex.mine(e), 0, jnp.sum(acc[0], axis=0, keepdims=True))
        put_row(ex.mine(e), 8, jnp.sum(acc[1], axis=0, keepdims=True))

    def grad_rows(src, stats, k, d_of, sums, j):
        hat = zhat(src, j, stats)
        m = jnp.concatenate([mask[...]] * 5, axis=1)
        got = passed(hat, k, d_of(j))
        return (gain(k) * stats[1]) * (got - m * (sums[0] + hat * sums[1]) / valid_count)

    def head_rows(j):
        return jnp.concatenate([d_out24] * 8, axis=0)

    def turn(src):
        for it in range(4):
            x = src[384 * it : 384 * it + 384, :].T.astype(bf16)
            for f in range(NF):
                dyT[f // 2, f % 2, :, 384 * it : 384 * it + 384] = x[80 * f : 80 * f + 80]

    trade = remote(dyT.at[:, 1 - p.c], dyS, us, ur, p.b, p.sib)

    grad_sums(block_rows, stats2, 2, head_rows, 3)
    slot = ex.mine(3)
    slot[5:6, :] = jnp.full((1, 128), loss_part, f32)
    slot[6:7, :] = jnp.concatenate([g_bias, jnp.zeros((1, 112), f32)], axis=1)
    ex.send(3)
    tot3 = ex.total(3)
    sums2 = wide(tot3[0:5]), wide(tot3[8:13])

    def low_sums(dst, src, stats, k, d_of, sums):
        def one(j, acc):
            d = grad_rows(src, stats, k, d_of, sums, j)
            dst[rows(j), :] = d
            return acc + jnp.sum(d.astype(bf16).astype(f32).reshape(BLK // 8, 8, C), axis=0)

        acc = lax.fori_loop(0, 8, one, jnp.zeros((8, C), f32))
        return jnp.sum(acc, axis=0, keepdims=True)

    def lost(dy_sums, mu):
        at = 64 * p.b + iota((64, C), 0)
        o = at - 80 * ((at >= 80).astype(jnp.int32) + (at >= 160).astype(jnp.int32))
        hit = (iota((64, C), 1) == 80 * p.f + o) & (at < 240)
        return jnp.sum(jnp.where(hit, dy_sums, 0.0), axis=1, keepdims=True) * mu

    put_spare(ex.mine(4), low_sums(block, block_rows, stats2, 2, head_rows, sums2))
    turn(block)
    trade.start()
    first_grad(p, SB, dyT, dfl)
    for u in range(3):
        share(u, SB).wait()
    trade.wait()
    filter_grad(p, SB, S2, dyT, dyS, DS, mu1, G, 0, dfl)
    sc.begin(0)
    filter_grad(p, SB, S2, dyT, dyS, DS, mu1, G, 1, dfl)
    sc.begin(1)
    def spread(src):
        def one(j, carry):
            spread_rows(SA, j, src[rows(j), :])
            return carry

        lax.fori_loop(0, 8, one, 0)

    spread(block)

    def back_conv1(it, carry):
        r0 = pl.multiple_of(it * 384, 384)
        dfl[pl.ds(r0, 384), :] = conv_back_rows(SA, W, 1, r0, 384)

        @pl.when(it == 0)
        def _():
            sc.mid(0)

        @pl.when(it == 2)
        def _():
            sc.mid(1)

        return carry

    lax.fori_loop(0, 4, back_conv1, 0)
    grad_sums(inner_rows, stats1, 1, dfl_rows, 4)
    ex.send(4)
    sc.along(0)
    filter_grad(p, SB, S2, dyT, dyS, DS, mu1, G, 2, None)
    sc.begin(2)
    pl.semaphore_signal(free, inc=1, device_id=(p.b, p.sib), device_id_type=MESH)
    normed(base_rows, stats0, 0, SA)
    sc.along(1)
    tot4 = ex.total(4)
    pl.semaphore_wait(free, 1)
    share(0).start()
    sums1 = wide(tot4[0:5]), wide(tot4[8:13])
    lost1 = lost(spare(tot4), mu1)
    put_spare(ex.mine(5), low_sums(dfl, inner_rows, stats1, 1, dfl_rows, sums1))
    turn(dfl)
    trade.start()
    for u in range(1, 3):
        share(u).start()
    first_grad(p, SA, dyT, inner)
    sc.mid(2)
    squares = sc.final(0, lost1)
    sc.clear(0)
    share(0).wait()
    trade.wait()
    filter_grad(p, SA, S2, dyT, dyS, DS, mu0, G, 3, inner)
    sc.begin(3)
    sc.clear(1)
    share(1).wait()
    filter_grad(p, SA, S2, dyT, dyS, DS, mu0, G, 4, inner)
    sc.begin(4)
    sc.along(2)
    sc.clear(2)
    share(2).wait()
    filter_grad(p, SA, S2, dyT, dyS, DS, mu0, G, 5, inner)
    sc.mid(3)
    sc.begin(5)
    spread(dfl)

    def back_conv0(it, carry):
        r0 = pl.multiple_of(it * 384, 384)
        inner[pl.ds(r0, 384), :] = conv_back_rows(SA, W, 0, r0, 384)

        @pl.when(it == 1)
        def _():
            sc.mid(4)

        @pl.when(it == 2)
        def _():
            sc.clear_line(0)
            sc.along(3)

        return carry

    lax.fori_loop(0, 4, back_conv0, 0)

    sc.mid(5)
    grad_sums(base_rows, stats0, 0, inner_rows, 5)
    ex.send(5)
    squares = squares + sc.final(1, lost1) + sc.final(2, lost1)
    sc.clear_line(1)
    sc.along(4)
    tot5 = ex.total(5)
    lost0 = lost(spare(tot5), mu0)
    squares = squares + sc.final(3, lost0)
    sc.clear_line(2)
    sc.along(5)
    sums0 = wide(tot5[0:5]), wide(tot5[8:13])
    grid16 = dfl.at[512:640]
    grid16[...] = jnp.zeros((128, C), f32)
    dstem[...] = jnp.zeros((BLK, 128), f32)

    def back0(i, carry):
        total_g, total_s = None, None
        for h in range(4):
            j = 4 * i + h
            d = block[rows(j), :] + grad_rows(base_rows, stats0, 0, inner_rows, sums0, j)
            d = d.astype(bf16)
            pick = iota((BLK, 128), 1) // 16 == j
            x = jnp.where(pick, stem[...], 0.0).astype(bf16)
            g = lax.dot_general(x, d, CC, preferred_element_type=f32)
            y = jnp.where(pick, lax.dot_general(d, bridge8, AC, preferred_element_type=f32), 0.0)
            total_g = g if total_g is None else total_g + g
            total_s = y if total_s is None else total_s + y
        grid16[...] += total_g
        dstem[...] += total_s
        return carry

    lax.fori_loop(0, 2, back0, 0)
    acc = grid16[0:16, :]
    for j in range(1, 8):
        acc = acc + grid16[16 * j : 16 * j + 16, :]
    dfl[0:16, :] = acc
    dfl[16:32, :] = par[24:40, :]

    def half(row, c):
        return dfl.at[pl.ds(pl.multiple_of(row + 16 * c, 16), 16), :]

    give = remote(half(0, 1 - p.c), half(32, 1 - p.c), fs, fr, p.b, p.sib)
    give.start()
    low = dstem[...].astype(bf16)
    high = lax.Precision.HIGHEST
    acc = None
    for c in range(3):
        t = lax.dot_general(
            AB[:, 128 * c : 128 * c + 128].astype(bf16), low, CC, preferred_element_type=f32
        )
        d = lax.dot_general(hits(c), t, CC, precision=high, preferred_element_type=f32)
        acc = d if acc is None else acc + d
    acc = jnp.where(own_j, acc, 0.0)
    fold = (jnp.bitwise_and(iota((256, 128), 0), 31) == iota((256, 128), 1)).astype(f32)
    acc = lax.dot_general(acc, fold, CC, precision=high, preferred_element_type=f32)
    slots[6, p.chip] = jnp.dot(
        tile_c.astype(f32), acc, precision=high, preferred_element_type=f32
    )
    ex.send(6)
    give.wait()
    zline = dfl.at[pl.ds(pl.multiple_of(64 + 16 * p.z, 16), 16), :]
    zline[...] = half(0, p.c)[...] + half(32, p.c)[...]
    for i in range(1, NZ):
        to = lax.rem(p.z + i, NZ)
        remote(zline, zline, hs, hr, p.b, 2 * to + p.c).start()
    squares = squares + sc.final(4, lost0)
    rest = dfl.at[64 : 64 + 16 * (NZ - 1), :]
    remote(rest, rest, hs, hr, p.b, p.sib).wait()
    square = dfl.at[pl.ds(pl.multiple_of(128 + 16 * p.b, 16), 16), :]
    square[...] = jnp.sum(dfl[64:128, :].reshape(NZ, 16, C), axis=0)
    for i in range(1, NB):
        to = lax.rem(p.b + i, NB)
        remote(square, square, js, jr, to, p.f).start()
    g_stem = ex.total(6)
    squares = squares + sc.final(5, lost0)
    slots[7, p.chip] = jnp.full((16, 128), jnp.sum(squares), f32)
    ex.send(7)
    rest = dfl.at[128 : 128 + 16 * (NB - 1), :]
    remote(rest, rest, js, jr, p.b, p.sib).wait()
    done = half(192, p.c)
    done[...] = jnp.sum(dfl[128:192, :].reshape(NB, 16, C), axis=0)
    give = remote(done, done, ms, mr, p.b, p.sib)
    give.start()
    give.wait()
    both = dfl[192:224, :]
    bias_all = tot3[6:7, :]
    stem_o[...] = g_stem
    ng = [row for sums in (sums0, sums1, sums2) for row in (sums[1], sums[0])]
    ng = jnp.concatenate(ng + [jnp.zeros((2, C), f32)], axis=0)
    every = jnp.concatenate([both, ng], axis=0)
    pick = (iota((C, 128), 0) == 80 * p.f + iota((C, 128), 1)) & (iota((C, 128), 1) < 80)
    own_o[...] = jnp.dot(every, pick.astype(f32), precision=high, preferred_element_type=f32)
    other = jnp.sum(every * every) + jnp.sum(g_stem * g_stem) + jnp.sum(bias_all * bias_all)
    conv_sq = ex.total(7)[0:1, :]
    misc_o[...] = jnp.zeros((8, 128), f32)
    misc_o[0:1, :] = jnp.sqrt(conv_sq + other)
    misc_o[1:2, :] = tot3[5:6, :] / total
    misc_o[2:3, :] = bias_all
    for e in range(6):
        sc.end(e)
    for e in range(3, 6):
        sc.clear(e)
        sc.clear_line(e)
    for e in range(8):
        ex.drain(e)


def step_call(images, labels, partner, valid, sizes, stem_w, bridge_t, conv_w, norm, head, bias):
    V, A, SM = pltpu.VMEM, pl.ANY, pltpu.SMEM
    spec = lambda m: pl.BlockSpec(memory_space=m)
    D = pltpu.SemaphoreType.DMA
    sh = jax.ShapeDtypeStruct
    return pl.pallas_call(
        step_kernel,
        out_shape=(
            sh((2, 3, 256, C), bf16), sh((40, 128), f32), sh((16, 128), f32), sh((8, 128), f32),
        ),
        in_specs=[
            spec(V), spec(V), spec(V), spec(V), spec(SM), spec(V), spec(V), spec(A), spec(V), spec(V), spec(V),
        ],
        out_specs=(spec(V),) * 4,
        scratch_shapes=[
            V((2, 3, NZ, 2, 256, C), bf16), V((3, 10 * BLK, C), bf16), V((3, 10 * BLK, C), bf16), V((10 * BLK, C), bf16),
            V((NZ, 2, 80, ROWS), bf16), V((NZ, 80, ROWS), bf16), V((NZ * 80, 128), f32),
            V((ROWS, C), f32), V((ROWS, C), f32), V((ROWS, C), f32),
            V((3, 3, 256, C), bf16), V((6, 3, 64, C), LINE), V((3, NZ, 256, C), bf16), V((3, NZ, 64, C), LINE),
            V((8, NCHIP, 16, 128), f32), V((8, 2, 16, 128), f32), V((2, NCHIP, 128), f32), V((NZ, 2, 40, 128), f32), V((40, C), f32),
            V((BLK, 128), f32), V((BLK, 384), f32), V((BLK, 128), f32), V((BLK, 128), f32), V((8, 128), f32),
            D((8,)), D((8,)), D((8,)), D((8,)), D, D, D((2,)), D((2,)), D((6, 4)), D((6, 4)), D((6, 12)), D((6, 12)), D((6,)), D((6,)), D((6,)),
            D((6, 6)), D((6, 6)), D((6, 3)), D((6, 3)), D((6, 3)), D((6, 3)), D((3,)), D((3,)), D, D,
            pltpu.SemaphoreType.REGULAR, D, D, D, D, D, D, D, D,
        ],
        compiler_params=pltpu.CompilerParams(
            collective_id=0, has_side_effects=True, vmem_limit_bytes=63 << 20
        ),
    )(images, labels, partner, valid, sizes, stem_w, bridge_t, conv_w, norm, head, bias)


def adam_rule(g, w, m, v, rate, shrink, factor):
    clipped = g * factor
    m = beta_one * m + (1.0 - beta_one) * clipped
    v = beta_two * v + (1.0 - beta_two) * clipped * clipped
    ahead = m / (1.0 - beta_one**STEP)
    behind = v / (1.0 - beta_two**STEP)
    return w - rate * (ahead / (jnp.sqrt(behind) + adam_eps) + shrink * w), m, v


def adam_kernel(G, misc, own, stem_g, *refs):
    ins, outs, (norm_o, loss_o, held, lsem, osem) = refs[:18], refs[18:36], refs[36:]
    norm_o[...] = misc[0:1, 0:1]
    loss_o[...] = misc[1:2, 0:1]
    factor = clip_norm / jnp.maximum(misc[0:1, :], clip_norm)
    wide_factor = jnp.concatenate([factor] * 5, axis=1)

    def load(s, i):
        return pltpu.make_async_copy(ins[i].at[s // 3, s % 3], held.at[i, s], lsem.at[i, s])

    def store(s, i):
        return pltpu.make_async_copy(held.at[i, s], outs[i].at[s // 3, s % 3], osem.at[i, s])

    for s in range(6):
        for i in range(3):
            load(s, i).start()

    def write(i, g, rate, shrink, f):
        w, m, v = (r[...] for r in ins[3 * i : 3 * i + 3])
        for o, x in zip(outs[3 * i : 3 * i + 3], adam_rule(g, w, m, v, rate, shrink, f)):
            o[...] = x

    write(1, stem_g[:, 0:27], 0.5, 0.05, factor[:, 0:27])
    write(2, own[0:16, 0:80], 0.6, 0.05, factor[:, 0:80])
    write(3, own[32:38, 0:80], 0.5, 0.0, factor[:, 0:80])
    write(4, own[16:26, 0:80], 0.1, 0.05, factor[:, 0:80])
    write(5, misc[2:3, 0:10], 0.5, 0.0, factor[:, 0:10])
    for s in range(6):
        for i in range(3):
            load(s, i).wait()

        def part(j, carry):
            at = pl.ds(pl.multiple_of(j * 48, 16), 48)
            new = adam_rule(
                G[s // 3, s % 3, at, :].astype(f32), held[0, s, at, :], held[1, s, at, :], held[2, s, at, :],
                0.033, 0.05, wide_factor,
            )
            for i in range(3):
                held[i, s, at, :] = new[i]
            return carry

        lax.fori_loop(0, 5, part, 0)
        for i in range(3):
            store(s, i).start()
    for s in range(6):
        for i in range(3):
            store(s, i).wait()


def adam_call(G, misc, own, stem_g, *state):
    V, A, D = pltpu.VMEM, pl.ANY, pltpu.SemaphoreType.DMA
    spec = lambda m: pl.BlockSpec(memory_space=m)
    return pl.pallas_call(
        adam_kernel,
        out_shape=tuple(jax.ShapeDtypeStruct(s, f32) for s in [x.shape for x in state] + [(1, 1)] * 2),
        in_specs=[spec(V)] * 4 + [spec(A)] * 3 + [spec(V)] * 15,
        out_specs=tuple([spec(A)] * 3 + [spec(V)] * 17),
        scratch_shapes=[V((3, 6, 240, C), f32), D((3, 6)), D((3, 6))],
        compiler_params=pltpu.CompilerParams(vmem_limit_bytes=62 << 20),
    )(G, misc, own, stem_g, *state)


def make_patches(images):
    number = images.shape[0]
    grid = images.reshape(number, 3, 32, 32)
    padded = jnp.pad(grid, ((0, 0), (0, 0), (1, 1), (1, 1)))
    pieces = [
        padded[:, :, row_off : row_off + 29 : 4, col_off : col_off + 29 : 4]
        for row_off in range(3)
        for col_off in range(3)
    ]
    stacked = jnp.stack(pieces, axis=2)
    return jnp.transpose(stacked, (1, 2, 0, 3, 4)).reshape(27, number * 64)


def shifted(feature_field):
    width, rows = feature_field.shape
    grid = feature_field.reshape(width, rows // 64, 8, 8)
    padded = jnp.pad(grid, ((0, 0), (0, 0), (1, 1), (1, 1)))
    pieces = [
        padded[:, :, row_off : row_off + 8, col_off : col_off + 8]
        for row_off in range(3)
        for col_off in range(3)
    ]
    return jnp.stack(pieces, axis=0).reshape(9 * width, rows)


def unshifted(parts, width):
    rows = parts.shape[1]
    grid = parts.reshape(9, width, rows // 64, 8, 8)
    summed = jnp.zeros((width, rows // 64, 10, 10), jnp.float32)
    for row_off in range(3):
        for col_off in range(3):
            summed = summed + jnp.pad(
                grid[3 * row_off + col_off],
                ((0, 0), (0, 0), (row_off, 2 - row_off), (col_off, 2 - col_off)),
            )
    return summed[:, :, 1:9, 1:9].reshape(width, rows)


def image_weights(valid_mask, group_sizes):
    shards, groups = group_sizes.shape
    capacity = valid_mask.shape[0] // shards
    group_ends = jnp.cumsum(group_sizes, axis=1)
    slot_index = jnp.arange(capacity, dtype=jnp.int32)
    member = jnp.sum(
        (slot_index[None, :, None] >= group_ends[:, None, :]).astype(jnp.int32), axis=2
    )
    member = jnp.minimum(member, groups - 1)
    chosen = (member[:, :, None] == jnp.arange(groups, dtype=jnp.int32)[None, None, :]).astype(
        jnp.float32
    )
    sizes_each = jnp.sum(chosen * group_sizes[:, None, :].astype(jnp.float32), axis=2)
    return valid_mask.astype(jnp.float32) / sizes_each.reshape(-1)


def norm_forward(feature_field, norm_gain, norm_shift, row_validity_mask, valid_count):
    batch_mean = (
        lax.psum(jnp.sum(feature_field * row_validity_mask, axis=1), ("batch", "filt"))
        / valid_count
    )
    centered_input = feature_field - batch_mean[:, None]
    batch_variance = (
        lax.psum(
            jnp.sum(centered_input * centered_input * row_validity_mask, axis=1), ("batch", "filt")
        )
        / valid_count
    )
    inverse_scale = lax.rsqrt(batch_variance + norm_epsilon)
    normalized_input = (feature_field - batch_mean[:, None]) * inverse_scale[:, None]
    norm_output = jnp.maximum(norm_gain[:, None] * normalized_input + norm_shift[:, None], 0.0)
    return (norm_output, normalized_input, inverse_scale)


def masked_norm_backward(
    output_gradient,
    norm_output,
    normalized_input,
    inverse_scale,
    norm_gain,
    row_validity_mask,
    valid_count,
):
    passed_rows = jnp.where(norm_output > 0.0, output_gradient, 0.0)
    shift_gradient, gain_gradient = lax.psum(
        (jnp.sum(passed_rows, axis=1), jnp.sum(passed_rows * normalized_input, axis=1)),
        ("batch", "filt"),
    )
    input_gradient = (
        passed_rows
        - row_validity_mask[None, :]
        * (shift_gradient[:, None] + normalized_input * gain_gradient[:, None])
        / valid_count
    )
    return ((norm_gain * inverse_scale)[:, None] * input_gradient, gain_gradient, shift_gradient)


def conv_forward(feature_field, weight_shard):
    stacked = shifted(feature_field)
    low_shard = weight_shard.astype(jnp.bfloat16)
    piece = lax.all_gather(low_shard, "filt", axis=0, tiled=True)
    norm_output = jnp.dot(
        piece.reshape(piece.shape[0], -1), stacked, preferred_element_type=jnp.float32
    )
    return (norm_output, None)


def conv_backward(feature_field, weight_shard, output_gradient):
    width = feature_field.shape[0]
    stacked = shifted(feature_field)
    rows_grad = output_gradient
    term = lax.dot_general(
        rows_grad, stacked, (((1,), (1,)), ((), ())), preferred_element_type=jnp.float32
    )
    weight_grad = lax.psum_scatter(
        term.reshape(lax.axis_size("filt") * weight_shard.shape[0], 9, width),
        "filt",
        scatter_dimension=0,
        tiled=True,
    )
    piece = lax.all_gather(weight_shard.astype(jnp.bfloat16), "filt", axis=0, tiled=True)
    rows_grad = output_gradient
    back = lax.dot_general(
        piece.reshape(piece.shape[0], -1),
        rows_grad,
        (((0,), (0,)), ((), ())),
        preferred_element_type=jnp.float32,
    )
    return (unshifted(back, width), weight_grad)


def adam_step(weight, output_gradient, first, second, rate, shrink, factor):
    clipped = output_gradient * factor
    first = beta_one * first + (1.0 - beta_one) * clipped
    second = beta_two * second + (1.0 - beta_two) * clipped * clipped
    ahead = first / (1.0 - beta_one**STEP)
    behind = second / (1.0 - beta_two**STEP)
    return (
        weight - rate * (ahead / (jnp.sqrt(behind) + adam_eps) + shrink * weight),
        first,
        second,
    )


def body(
    images,
    labels,
    partner,
    valid_mask,
    group_sizes,
    stem_weight,
    bridge_weight,
    conv_weight,
    norm_params,
    head_weight,
    head_bias,
    stem_first,
    stem_second,
    bridge_first,
    bridge_second,
    conv_first,
    conv_second,
    norm_first,
    norm_second,
    head_first,
    head_second,
    bias_first,
    bias_second,
):
    width = bridge_weight.shape[0]
    bridge_all, norm_all, head_all = (
        lax.all_gather(bridge_weight, "filt", axis=0, tiled=True),
        lax.all_gather(norm_params, "filt", axis=1, tiled=True),
        lax.all_gather(head_weight, "filt", axis=1, tiled=True),
    )
    labels_all, valid_all = (
        lax.all_gather(labels, ("batch", "filt"), axis=0, tiled=True),
        lax.all_gather(valid_mask, ("batch", "filt"), axis=0, tiled=True),
    )
    weight_all = image_weights(valid_all, group_sizes)
    total = jnp.sum(weight_all)
    valid_count = 64.0 * jnp.sum(valid_all.astype(jnp.float32))
    local = images.shape[0]
    image_weight = lax.dynamic_slice_in_dim(
        weight_all, lax.axis_index(("batch", "filt")) * local, local
    )
    row_validity_mask = jnp.repeat(valid_mask.astype(jnp.float32), 64)
    patch = make_patches(images)
    stem = jnp.dot(
        stem_weight.astype(jnp.bfloat16), patch, preferred_element_type=jnp.float32
    ).astype(jnp.bfloat16)
    base = jnp.dot(bridge_all.astype(jnp.bfloat16), stem, preferred_element_type=jnp.float32)
    first, first_hat, first_scale = norm_forward(
        base, norm_all[0], norm_all[1], row_validity_mask, valid_count
    )
    first_low = first.astype(jnp.bfloat16)
    inner, kept_zero = conv_forward(first_low, conv_weight[0])
    second, second_hat, second_scale = norm_forward(
        inner, norm_all[2], norm_all[3], row_validity_mask, valid_count
    )
    second_low = second.astype(jnp.bfloat16)
    branch, kept_one = conv_forward(second_low, conv_weight[1])
    final, final_hat, final_scale = norm_forward(
        base + branch, norm_all[4], norm_all[5], row_validity_mask, valid_count
    )
    pooled = jnp.mean(final.reshape(final.shape[0], local, 64), axis=2).astype(jnp.bfloat16)
    logits = (
        jnp.dot(head_all.astype(jnp.bfloat16), pooled, preferred_element_type=jnp.float32)
        + head_bias[:, None]
    )
    moved = logits - jnp.max(logits, axis=0, keepdims=True)
    logp = moved - jnp.log(jnp.sum(jnp.exp(moved), axis=0, keepdims=True))
    classes = jnp.arange(logits.shape[0], dtype=jnp.int32)
    partner_labels = jnp.take(labels_all, partner)
    target = own_share * (labels[None, :] == classes[:, None]).astype(jnp.float32) + (
        1.0 - own_share
    ) * (partner_labels[None, :] == classes[:, None]).astype(jnp.float32)
    loss_part = -jnp.sum(image_weight * jnp.sum(target * logp, axis=0))
    d_logits = ((jnp.exp(logp) - target) * (image_weight / total)[None, :]).astype(jnp.bfloat16)
    bias_grad = jnp.sum(d_logits.astype(jnp.float32), axis=1)
    head_grad = lax.dot_general(
        d_logits, pooled, (((1,), (1,)), ((), ())), preferred_element_type=jnp.float32
    )
    d_pooled = lax.dot_general(
        head_all.astype(jnp.bfloat16),
        d_logits,
        (((0,), (0,)), ((), ())),
        preferred_element_type=jnp.float32,
    )
    d_final = jnp.repeat(d_pooled / 64.0, 64, axis=1)
    d_block, gain_two, shift_two = masked_norm_backward(
        d_final, final, final_hat, final_scale, norm_all[4], row_validity_mask, valid_count
    )
    d_second, conv_grad_one = conv_backward(
        second_low, conv_weight[1], d_block.astype(jnp.bfloat16)
    )
    d_inner, gain_one, shift_one = masked_norm_backward(
        d_second, second, second_hat, second_scale, norm_all[2], row_validity_mask, valid_count
    )
    d_first, conv_grad_zero = conv_backward(first_low, conv_weight[0], d_inner.astype(jnp.bfloat16))
    d_lower, gain_zero, shift_zero = masked_norm_backward(
        d_first, first, first_hat, first_scale, norm_all[0], row_validity_mask, valid_count
    )
    d_base = (d_block + d_lower).astype(jnp.bfloat16)
    bridge_grad = lax.dot_general(
        d_base, stem, (((1,), (1,)), ((), ())), preferred_element_type=jnp.float32
    )
    d_stem = lax.dot_general(
        bridge_all.astype(jnp.bfloat16),
        d_base,
        (((0,), (0,)), ((), ())),
        preferred_element_type=jnp.float32,
    ).astype(jnp.bfloat16)
    stem_grad = lax.dot_general(
        d_stem, patch, (((1,), (1,)), ((), ())), preferred_element_type=jnp.float32
    )
    bridge_part, head_part = (
        lax.psum_scatter(bridge_grad, "filt", scatter_dimension=0, tiled=True),
        lax.psum_scatter(head_grad, "filt", scatter_dimension=1, tiled=True),
    )
    conv_grad, bridge_sum, head_sum = lax.psum(
        (jnp.stack([conv_grad_zero, conv_grad_one]), bridge_part, head_part), "batch"
    )
    stem_sum, bias_sum, loss_sum = lax.psum((stem_grad, bias_grad, loss_part), ("batch", "filt"))
    norm_full = jnp.stack([gain_zero, shift_zero, gain_one, shift_one, gain_two, shift_two])
    norm_grad = lax.dynamic_slice_in_dim(norm_full, lax.axis_index("filt") * width, width, 1)
    owned_square = (
        jnp.sum(conv_grad * conv_grad)
        + jnp.sum(bridge_sum * bridge_sum)
        + jnp.sum(norm_grad * norm_grad)
        + jnp.sum(head_sum * head_sum)
    )
    squares_all = (
        lax.psum(owned_square, "filt") + jnp.sum(stem_sum * stem_sum) + jnp.sum(bias_sum * bias_sum)
    )
    grad_norm = jnp.sqrt(squares_all)
    factor = clip_norm / jnp.maximum(grad_norm, clip_norm)
    stem_new = adam_step(stem_weight, stem_sum, stem_first, stem_second, 0.5, 0.05, factor)
    bridge_new = adam_step(
        bridge_weight, bridge_sum, bridge_first, bridge_second, 0.6, 0.05, factor
    )
    conv_new = adam_step(conv_weight, conv_grad, conv_first, conv_second, 0.033, 0.05, factor)
    norm_new = adam_step(norm_params, norm_grad, norm_first, norm_second, 0.5, 0.0, factor)
    head_new = adam_step(head_weight, head_sum, head_first, head_second, 0.1, 0.05, factor)
    bias_new = adam_step(head_bias, bias_sum, bias_first, bias_second, 0.5, 0.0, factor)
    return (
        stem_new[0],
        stem_new[1],
        stem_new[2],
        bridge_new[0],
        bridge_new[1],
        bridge_new[2],
        conv_new[0],
        conv_new[1],
        conv_new[2],
        norm_new[0],
        norm_new[1],
        norm_new[2],
        head_new[0],
        head_new[1],
        head_new[2],
        bias_new[0],
        bias_new[1],
        bias_new[2],
        grad_norm,
        loss_sum / total,
    )


def fast_body(
    images, labels, partner, valid_mask, group_sizes, stem_weight, bridge_weight, conv_weight, norm_params,
    head_weight, head_bias, stem_first, stem_second, bridge_first, bridge_second, conv_first, conv_second,
    norm_first, norm_second, head_first, head_second, bias_first, bias_second,
):
    width = bridge_weight.shape[0]
    def rows(x):
        return x.transpose(0, 2, 1, 3).reshape(2, 3, 3 * width, C)

    def back(x):
        return x.reshape(2, 9, width, C).transpose(0, 2, 1, 3)

    G, own, stem_g, misc = step_call(
        images, labels[None], partner[None], valid_mask[None], group_sizes, stem_weight, bridge_weight.T,
        conv_weight.transpose(0, 2, 1, 3), norm_params, head_weight, head_bias[None],
    )
    new = adam_call(
        G, misc, own, stem_g,
        rows(conv_weight), rows(conv_first), rows(conv_second),
        stem_weight, stem_first, stem_second,
        bridge_weight.T, bridge_first.T, bridge_second.T,
        norm_params, norm_first, norm_second,
        head_weight, head_first, head_second,
        head_bias[None], bias_first[None], bias_second[None],
    )
    conv, stem, bridge, norm, head, bias = (new[i : i + 3] for i in range(0, 18, 3))
    return (
        *stem,
        *(x.T for x in bridge),
        *(back(x) for x in conv),
        *norm,
        *head,
        *(x[0] for x in bias),
        new[18].reshape(()),
        new[19].reshape(()),
    )


def solution(mesh):
    in_specs = (
        P(("batch", "filt"), None),
        P(("batch", "filt")),
        P(("batch", "filt")),
        P(("batch", "filt")),
        P(),
        P(),
        P("filt", None),
        P(None, "filt", None, None),
        P(None, "filt"),
        P(None, "filt"),
        P(),
        P(),
        P(),
        P("filt", None),
        P("filt", None),
        P(None, "filt", None, None),
        P(None, "filt", None, None),
        P(None, "filt"),
        P(None, "filt"),
        P(None, "filt"),
        P(None, "filt"),
        P(),
        P(),
    )
    out_specs = (
        P(),
        P(),
        P(),
        P("filt", None),
        P("filt", None),
        P("filt", None),
        P(None, "filt", None, None),
        P(None, "filt", None, None),
        P(None, "filt", None, None),
        P(None, "filt"),
        P(None, "filt"),
        P(None, "filt"),
        P(None, "filt"),
        P(None, "filt"),
        P(None, "filt"),
        P(),
        P(),
        P(),
        P(),
        P(),
    )
    fits = mesh.shape["batch"] == NB and mesh.shape["filt"] == NF
    return jax.shard_map(fast_body if fits else body, mesh=mesh, in_specs=in_specs, out_specs=out_specs, check_vma=False)
```

```python
import jax
import jax.numpy as jnp
from jax import lax
from jax.experimental import pallas as pl
from jax.experimental.pallas import tpu as pltpu
from jax.sharding import PartitionSpec as P

STEP = 8

beta_one = 0.9
beta_two = 0.95
adam_eps = 1e-08
norm_epsilon = 1e-05
clip_norm = 0.01
own_share = 0.7

MESH = pl.DeviceIdType.MESH
bf16 = jnp.bfloat16
f32 = jnp.float32
LINE = bf16
NB, NF, NZ, NDEV, NCHIP = 4, 8, 4, 32, 16
C, IMG, ROWS = 640, 24, 1536
BLK = 8 * IMG
AC = (((1,), (1,)), ((), ()))
CC = (((0,), (0,)), ((), ()))


def iota(shape, dim):
    return lax.broadcasted_iota(jnp.int32, shape, dim)


def wide(row5):
    return jnp.concatenate([row5[k : k + 1, :] for k in range(5)], axis=1)


def column(row, n):
    eye = iota((n, n), 0) == iota((n, n), 1)
    return jnp.sum(jnp.where(eye, jnp.broadcast_to(row, (n, n)), 0.0), axis=1, keepdims=True)


class Place:
    def __init__(self):
        self.b = lax.axis_index("batch")
        self.f = lax.axis_index("filt")
        self.z = self.f // 2
        self.c = lax.rem(self.f, 2)
        self.me = self.b * NF + self.f
        self.chip = self.b * NZ + self.z
        self.xn = self.b + 1 - 2 * lax.rem(self.b, 2)
        self.yn = lax.rem(self.b + 2, NB)
        self.dn = (NB - 1) - self.b
        self.sib = self.f + 1 - 2 * self.c


def remote(src, dst, ssem, rsem, b, f):
    return pltpu.make_async_remote_copy(
        src_ref=src, dst_ref=dst, send_sem=ssem, recv_sem=rsem, device_id=(b, f), device_id_type=MESH
    )


def peers(p):
    for dz in (2, 1, 3, 0):
        for db in (3, 1, 2, 0):
            if dz or db:
                yield lax.rem(p.b + db, NB), lax.rem(p.z + dz, NZ)


def greet(p):
    sem = pltpu.get_barrier_semaphore()
    for b, z in peers(p):
        pl.semaphore_signal(sem, inc=1, device_id=(b, 2 * z + p.c), device_id_type=MESH)
    pl.semaphore_signal(sem, inc=1, device_id=(p.b, p.sib), device_id_type=MESH)


def met():
    pl.semaphore_wait(pltpu.get_barrier_semaphore(), NCHIP)


class Exchange:
    def __init__(self, p, slots, sibs, ssem, rsem, psem, qsem):
        self.p, self.slots, self.sibs = p, slots, sibs
        self.ssem, self.rsem, self.psem, self.qsem = ssem, rsem, psem, qsem

    def mine(self, e):
        return self.slots.at[e, self.p.chip]

    def send(self, e):
        p = self.p
        mine = self.mine(e)
        for b, z in peers(p):
            remote(mine, mine, self.ssem.at[e], self.rsem.at[e], b, 2 * z + p.c).start()

    def rest(self, e):
        p = self.p
        rest = self.slots.at[e, 0 : NCHIP - 1]
        return remote(rest, rest, self.ssem.at[e], self.rsem.at[e], p.b, p.sib)

    def across(self, e):
        p = self.p
        return remote(
            self.sibs.at[e, 0], self.sibs.at[e, 1], self.psem.at[e], self.qsem.at[e], p.b, p.sib
        )

    def wait(self, e):
        self.rest(e).wait_recv()

    def swap(self, e, value):
        self.sibs[e, 0] = value
        self.across(e).start()
        self.across(e).wait_recv()
        return self.sibs[e, 1]

    def drain(self, e):
        self.rest(e).wait_send()
        self.across(e).wait_send()

    def total(self, e):
        self.wait(e)
        own = jnp.sum(self.slots[e], axis=0)
        return own + self.swap(e, own)


def put_row(slot, row, value):
    for k in range(5):
        slot[row + k : row + k + 1, :] = value[:, 128 * k : 128 * k + 128]


def put_spare(slot, value):
    for k, row in enumerate((5, 6, 7, 13, 14)):
        slot[row : row + 1, :] = value[:, 128 * k : 128 * k + 128]


def spare(rows):
    return wide(jnp.concatenate([rows[5:8], rows[13:15]], axis=0))


def local_stats(src, mask, count, slot):
    def total(j, acc):
        x = src[pl.ds(pl.multiple_of(j * BLK, BLK), BLK), :]
        m = jnp.concatenate([mask[...]] * 5, axis=1)
        return acc + jnp.sum((x * m).reshape(BLK // 8, 8, C), axis=0)

    acc = lax.fori_loop(0, 8, total, jnp.zeros((8, C), f32))
    own_sum = jnp.sum(acc, axis=0, keepdims=True)
    own_mean = own_sum / jnp.maximum(count, 1.0)

    def squares(j, acc):
        x = src[pl.ds(pl.multiple_of(j * BLK, BLK), BLK), :]
        m = jnp.concatenate([mask[...]] * 5, axis=1)
        d = x - own_mean
        return acc + jnp.sum((d * d * m).reshape(BLK // 8, 8, C), axis=0)

    acc = lax.fori_loop(0, 8, squares, jnp.zeros((8, C), f32))
    put_row(slot, 0, own_sum)
    put_row(slot, 8, jnp.sum(acc, axis=0, keepdims=True))


def joint_stats(ex, e):
    ex.wait(e)
    every = ex.slots[e]
    n = ex.slots[0, :, 5:6, :]
    sums = every[:, 0:5, :]
    n_own, s_own = jnp.sum(n, axis=0), jnp.sum(sums, axis=0)
    m_own = s_own / jnp.maximum(n_own, 1.0)
    off = sums / jnp.maximum(n, 1.0) - m_own[None]
    q_own = jnp.sum(every[:, 8:13, :] + n * off * off, axis=0)
    rest = jnp.sum(every[:, 5:8, :], axis=0)
    more = jnp.sum(every[:, 13:16, :], axis=0)
    got = ex.swap(e, jnp.concatenate([s_own, rest, q_own, more], axis=0))
    n_sib = ex.sibs[0, 1, 5:6, :]
    s_sib, q_sib = got[0:5], got[8:13]
    count = n_own + n_sib
    mean = (s_own + s_sib) / count
    a, b = m_own - mean, s_sib / jnp.maximum(n_sib, 1.0) - mean
    spread = ((q_own + q_sib) + (n_own * a * a + n_sib * b * b)) / count
    return wide(mean), wide(lax.rsqrt(spread + norm_epsilon)), spare(got + jnp.concatenate([s_own, rest, q_own, more], axis=0))


def spread_rows(S, j, x):
    at = pl.ds(pl.multiple_of((j + 1) * BLK, BLK), BLK)
    gap = jnp.zeros((IMG, C), f32)
    S[0][at, :] = jnp.concatenate([gap, x[: BLK - IMG]], axis=0).astype(bf16)
    S[1][at, :] = x.astype(bf16)
    S[2][at, :] = jnp.concatenate([x[IMG:], gap], axis=0).astype(bf16)


def conv_part(S, W, k, u, r0, M):
    lhs = jnp.concatenate([S[u][pl.ds(r0 + v * BLK, M), :] for v in range(3)], axis=1)
    rhs = jnp.concatenate(
        [
            jnp.concatenate(
                [W[k, u, z, c, v * 80 : v * 80 + 80, :] for z in range(NZ) for c in range(2)], axis=0
            )
            for v in range(3)
        ],
        axis=1,
    )
    return lax.dot_general(lhs, rhs, AC, preferred_element_type=f32)


class Gather:
    def __init__(self, p, W, zs, zr, xs, xr, ds, dr):
        self.p, self.W = p, W
        self.zs, self.zr, self.xs, self.xr, self.ds, self.dr = zs, zr, xs, xr, ds, dr

    def part(self, s, z, b, row, n):
        return self.W.at[
            s // 3, lax.rem(s, 3), z, self.p.c, pl.ds(pl.multiple_of(b * 64 + row, 32), n), :
        ]

    def zcopy(self, s, i):
        p = self.p
        mine = self.part(s, p.z, p.b, 0, 64)
        to = lax.rem(p.z + i, NZ)
        return remote(mine, mine, self.zs.at[s, i], self.zr.at[s, i], p.b, 2 * to + p.c)

    def zsend(self, s):
        for i in (2, 1, 3):
            self.zcopy(s, i).start()

    def xcopy(self, s, i, d):
        p = self.p
        z = lax.rem(p.z + NZ - i, NZ)
        b, row, n, to = ((p.b, 0, 64, p.xn), (p.b, 0, 64, p.yn), (p.xn, 0, 32, p.yn), (p.yn, 32, 32, p.xn))[d]
        part = self.part(s, z, b, row, n)
        at = 3 * d + i - 1
        return remote(part, part, self.xs.at[s, at], self.xr.at[s, at], to, p.f)

    def relay(self, s):
        for i in range(1, NZ):
            self.zcopy(s, i).wait_recv()
            self.xcopy(s, i, 0).start()
            self.xcopy(s, i, 1).start()

    def turn(self, s):
        for i in range(1, NZ):
            self.xcopy(s, i, 0).wait_recv()
            self.xcopy(s, i, 2).start()
            self.xcopy(s, i, 1).wait_recv()
            self.xcopy(s, i, 3).start()

    def dcopy(self, s):
        p = self.p
        mine = self.W.at[s // 3, lax.rem(s, 3), :, p.c]
        return remote(mine, mine, self.ds.at[s], self.dr.at[s], p.b, p.sib)

    def across(self, s):
        for i in range(1, NZ):
            self.xcopy(s, i, 2).wait_recv()
            self.xcopy(s, i, 3).wait_recv()
        self.dcopy(s).start()

    def arrive(self, s):
        self.dcopy(s).wait_recv()

    def drain(self, s):
        for i in range(1, NZ):
            self.zcopy(s, i).wait_send()
            for d in range(4):
                self.xcopy(s, i, d).wait_send()
        self.dcopy(s).wait_send()


class Scatter:
    def __init__(self, p, W, RX, RZ, G, Q, GF, sems):
        self.p, self.W, self.RX, self.RZ, self.G, self.Q, self.GF = p, W, RX, RZ, G, Q, GF
        (self.bs, self.br, self.cs, self.cr, self.es, self.er) = sems

    def held(self, e, q, half):
        return self.G.at[e % 3, :, pl.ds(pl.multiple_of(q * 64 + 32 * half, 32), 32), :]

    def room(self, e, i):
        at = pl.ds(128 * (i % 2), 128)
        if e < 3:
            ref = self.RX.at[e, i // 2, at, :]
        else:
            ref = self.W.at[1, e % 3, i // 4, (i // 2) % 2, at, :]
        return ref

    def hop(self, e, i):
        p = self.p
        q, half, to = (
            (p.dn, 0, p.xn), (p.dn, 1, p.yn), (p.xn, 0, p.xn), (p.yn, 1, p.yn), (p.yn, 0, p.yn), (p.xn, 1, p.xn),
        )[i]
        return remote(
            self.held(e, q, half), self.room(e, i).reshape(NZ, 32, C), self.bs.at[e, i], self.br.at[e, i], to, p.f
        )

    def begin(self, e):
        for i in range(4):
            self.hop(e, i).start()

    def mid(self, e):
        p = self.p
        for i, q, half in ((0, p.yn, 0), (1, p.xn, 1)):
            self.hop(e, i).wait_recv()
            mine = self.held(e, q, half)
            got = self.room(e, i)[...].reshape(NZ, 32, C).astype(f32)
            mine[...] = (mine[...].astype(f32) + got).astype(bf16)
            self.hop(e, 4 + i).start()

    def out3(self, e, i):
        p = self.p
        to = lax.rem(p.z + i, NZ)
        return remote(
            self.Q.at[e % 3, to], self.RZ.at[e, i - 1], self.cs.at[e, i - 1], self.cr.at[e, i - 1], p.b, 2 * to + p.c
        )

    def out4(self, e, d):
        p = self.p
        to = (p.xn, p.yn, p.dn)[d]
        mine = self.GF.at[1 - e // 3, e % 3, pl.ds(pl.multiple_of(p.b * 64, 64), 64), :]
        return remote(mine, mine, self.es.at[e, d], self.er.at[e, d], to, p.f)

    def along(self, e):
        p = self.p
        for i in range(2, 6):
            self.hop(e, i).wait_recv()
        for half, ways in ((0, (2, 4)), (1, (3, 5))):
            acc = self.held(e, p.b, half)[...].astype(f32)
            for i in ways:
                acc = acc + self.room(e, i)[...].reshape(NZ, 32, C).astype(f32)
            self.Q[e % 3, :, 32 * half : 32 * half + 32, :] = acc.astype(self.Q.dtype)
        for i in (2, 1, 3):
            self.out3(e, i).start()

    def final(self, e, lost):
        p = self.p
        for i in range(1, NZ):
            self.out3(e, i).wait_recv()
        acc = self.Q[e % 3, p.z].astype(f32)
        for i in range(1, NZ):
            acc = acc + self.RZ[e, i - 1].astype(f32)
        acc = acc + lost
        low = acc.astype(bf16)
        self.GF[1 - e // 3, e % 3, pl.ds(pl.multiple_of(p.b * 64, 64), 64), :] = low
        for d in (2, 0, 1):
            self.out4(e, d).start()
        low = low.astype(f32)
        return jnp.sum((low * low).reshape(8, 8, C), axis=0)

    def clear(self, e):
        for i in range(6):
            self.hop(e, i).wait_send()

    def clear_line(self, e):
        for i in range(1, NZ):
            self.out3(e, i).wait_send()

    def end(self, e):
        for d in range(3):
            self.out4(e, d).wait()


class RowSum:
    def __init__(self, p, ref, ssem, rsem):
        self.p, self.ref, self.ssem, self.rsem = p, ref, ssem, rsem

    def eight(self, t, row, i):
        return self.ref.at[t, pl.ds(pl.multiple_of(row + 8 * i, 8), 8), :]

    def hop(self, t, n, src, dst, b, f):
        return remote(src, dst, self.ssem.at[t, n], self.rsem.at[t, n], b, f)

    def three(self, t, n, row):
        rest = self.ref.at[t, row : row + 24, :]
        return self.hop(t, n, rest, rest, self.p.b, self.p.sib)

    def give(self, t):
        p = self.p
        return self.hop(t, 0, self.eight(t, 0, 1 - p.c), self.eight(t, 16, 1 - p.c), p.b, p.sib)

    def along(self, t):
        p = self.p
        self.give(t).wait_recv()
        mine = self.eight(t, 32, p.z)
        mine[...] = self.eight(t, 0, p.c)[...] + self.eight(t, 16, p.c)[...]
        for i in (2, 1, 3):
            self.hop(t, 1, mine, mine, p.b, 2 * lax.rem(p.z + i, NZ) + p.c).start()

    def square(self, t):
        p = self.p
        self.three(t, 1, 32).wait_recv()
        mine = self.eight(t, 64, p.b)
        mine[...] = jnp.sum(self.ref[t, 32:64, :].reshape(NZ, 8, C), axis=0)
        for to in (p.dn, p.xn, p.yn):
            self.hop(t, 2, mine, mine, to, p.f).start()

    def back(self, t):
        p = self.p
        mine = self.eight(t, 96, p.c)
        return self.hop(t, 3, mine, mine, p.b, p.sib)

    def close(self, t):
        self.three(t, 2, 64).wait_recv()
        self.eight(t, 96, self.p.c)[...] = jnp.sum(self.ref[t, 64:96, :].reshape(NB, 8, C), axis=0)
        self.back(t).start()

    def result(self, t):
        self.back(t).wait_recv()
        return self.ref[t, 96:112, :]

    def drain(self, t):
        self.give(t).wait_send()
        self.three(t, 1, 32).wait_send()
        self.three(t, 2, 64).wait_send()
        self.back(t).wait_send()


def conv_back_rows(S, W, k, r0, M):
    acc = None
    for u in range(3):
        lhs = jnp.concatenate([S[2 - u][pl.ds(r0 + (2 - v) * BLK, M), :] for v in range(3)], axis=1)
        rhs = jnp.concatenate(
            [
                W[k, u, z, c, v * 80 : v * 80 + 80, :]
                for v in range(3)
                for z in range(NZ)
                for c in range(2)
            ],
            axis=0,
        )
        d = jnp.dot(lhs, rhs, preferred_element_type=f32)
        acc = d if acc is None else acc + d
    return acc


def own_rows(p, dyT):
    return jnp.concatenate([dyT[z, p.c] for z in range(NZ)], axis=0)


def sib_rows(dyS):
    return jnp.concatenate([dyS[z] for z in range(NZ)], axis=0)


def first_grad(p, S, dyT, acc):
    def tap(v, carry):
        at = pl.ds(pl.multiple_of(v * BLK, BLK), ROWS)
        acc[pl.ds(pl.multiple_of(v * 320, 320), 320), :] = jnp.dot(
            own_rows(p, dyT), S[0][at, :], preferred_element_type=f32
        )
        return carry

    lax.fori_loop(0, 3, tap, 0)


def filter_grad(p, S, S2, dyT, dyS, DS, mu, G, e, acc):
    u = e % 3
    if u == 0:
        ones = jnp.ones((ROWS, 128), bf16)
        DS[...] = jnp.dot(own_rows(p, dyT), ones, preferred_element_type=f32) + jnp.dot(
            sib_rows(dyS), ones, preferred_element_type=f32
        )

    def tap(v, carry):
        at = pl.ds(pl.multiple_of(v * BLK, BLK), ROWS)
        d = jnp.dot(sib_rows(dyS), S2[u, at, :], preferred_element_type=f32)
        if u == 0:
            d = d + acc[pl.ds(pl.multiple_of(v * 320, 320), 320), :]
        else:
            d = d + jnp.dot(own_rows(p, dyT), S[u][at, :], preferred_element_type=f32)
        d = d - jnp.concatenate([DS[...]] * 5, axis=1) * mu
        for z in range(NZ):
            G[u, z, pl.ds(pl.multiple_of(v * 80, 16), 80), :] = d[80 * z : 80 * z + 80].astype(bf16)
        return carry

    lax.fori_loop(0, 3, tap, 0)


def step_kernel(
    images, labels, partner, valid, sizes, stem_w, bridge_t, conv_w, norm, head, bias,
    GF, own_o, stem_o, misc_o,
    W, S, S2, S3, dyT, dyS, DS, inner, block, dfl, RX, RZ, G, Q, slots, sibs, lab, few, gath, par, mask, AB, stem, dstem, pad,
    xs_, xr_, ps_, pr_, lbs, lbr, gs, gr, zs, zr, xs, xr, ds, dr, ls,
    bs, br, cs, cr, es, er, ts, tr, us, ur, free, fs, fr,
):
    p = Place()
    ex = Exchange(p, slots, sibs, xs_, xr_, ps_, pr_)
    ga = Gather(p, W, zs, zr, xs, xr, ds, dr)
    sc = Scatter(p, W, RX, RZ, G, Q, GF, (bs, br, cs, cr, es, er))
    rs = RowSum(p, few, fs, fr)
    greet(p)
    SA = [S.at[u] for u in range(3)]
    SB = [S.at[0], S.at[1], S3]
    def load(s):
        at = pl.ds(240 * s, 240)
        return pltpu.make_async_copy(conv_w.reshape(1440, C).at[at], block.at[at], ls.at[s])

    for s in range(6):
        load(s).start()
    mine = gath.at[p.z, p.c]
    mine[...] = jnp.zeros((40, 128), f32)
    mine[0:16, 0:80] = bridge_t[...]
    mine[16:22, 0:80] = norm[...]
    mine[24:34, 0:80] = head[...]

    def cast(s):
        load(s).wait()
        k, u = s // 3, s % 3
        for v in range(3):
            t = 9 * k + 3 * u + v
            W[k, u, p.z, p.c, 80 * v : 80 * v + 80, :] = block[80 * t : 80 * t + 80, :].astype(bf16)
        W[k, u, p.z, p.c, 240:256, :] = jnp.zeros((16, C), bf16)

    cast(0)
    met()
    for i in (2, 1, 3):
        to = lax.rem(p.z + i, NZ)
        remote(mine, mine, gs.at[0], gr.at[0], p.b, 2 * to + p.c).start()
    ga.zsend(0)
    for s in range(1, 6):
        cast(s)
        if s < 2:
            ga.zsend(s)
    img = pltpu.roll(images[...].astype(f32), 32, 1)
    lane = iota((IMG, 128), 1)
    for c in range(3):
        for i in range(8):
            a = img[:, 1024 * c + 128 * i : 1024 * c + 128 * i + 128]
            if i == 0:
                a = jnp.where(lane < 32, 0.0, a)
            AB[IMG * i : IMG * i + IMG, 128 * c : 128 * c + 128] = a
    tile_c = jnp.bitwise_and(iota((16, 128), 1), 15) == iota((16, 128), 0)
    wc = lax.dot_general(
        stem_w[...].astype(bf16), tile_c.astype(bf16), CC, preferred_element_type=f32
    )
    fold_r = (jnp.bitwise_and(iota((256, 27), 0), 31) == iota((256, 27), 1)).astype(bf16)
    own_j = iota((256, 128), 0) // 32 == iota((256, 128), 1) // 16
    bd = jnp.dot(fold_r, wc.astype(bf16), preferred_element_type=f32)
    bd = jnp.where(own_j, bd, 0.0).astype(bf16)
    l, r = iota((128, 256), 0), iota((128, 256), 1)
    v = jnp.bitwise_and(l, 31) - 4 * (r // 32) + 1

    def hits(c):
        want = 9 * c + 3 * (l // 32) + v
        hit = (l < 96) & (v >= 0) & (v < 3) & (want == jnp.bitwise_and(r, 31))
        return hit.astype(f32)

    acc = None
    for c in range(3):
        t = jnp.dot(hits(c).astype(bf16), bd, preferred_element_type=f32).astype(bf16)
        d = jnp.dot(
            AB[:, 128 * c : 128 * c + 128].astype(bf16), t, preferred_element_type=f32
        )
        acc = d if acc is None else acc + d
    stem[...] = acc.astype(bf16).astype(f32)
    ok = column(valid[...].astype(f32), IMG)
    q = p.f * IMG + iota((IMG, 1), 0)
    member = jnp.zeros((IMG, 1), jnp.int32)
    end = jnp.int32(0)
    for g in range(8):
        end = end + sizes[p.b, g]
        member = member + (q >= end).astype(jnp.int32)
    member = jnp.minimum(member, 7)
    size = jnp.zeros((IMG, 1), f32)
    for g in range(8):
        size = size + jnp.where(member == g, sizes[p.b, g].astype(f32), 0.0)
    weight = ok / size
    mask[...] = jnp.concatenate([jnp.broadcast_to(ok, (IMG, 128))] * 8, axis=0)
    count = 64.0 * jnp.sum(ok)
    own_row = labels[...].astype(f32)
    slot = ex.mine(0)
    slot[5:6, :] = jnp.full((1, 128), count, f32)
    slot[6:7, :] = jnp.concatenate([own_row, jnp.zeros((1, 104), f32)], axis=1)
    slot[7:8, :] = jnp.full((1, 128), jnp.sum(weight), f32)
    edge = jnp.zeros((BLK, C), bf16)
    S3[0:BLK, :] = edge
    S3[9 * BLK : 10 * BLK, :] = edge
    for u in range(3):
        S[u, 0:BLK, :] = edge
        S[u, 9 * BLK : 10 * BLK, :] = edge
        for z in range(NZ):
            G[u, z, 240:256, :] = jnp.zeros((16, C), bf16)
    rest = gath.at[0 : NZ - 1, 0]
    remote(rest, rest, gs.at[0], gr.at[0], p.b, p.sib).wait()
    side = gath.at[:, p.c]
    pair = remote(side, side, gs.at[1], gr.at[1], p.b, p.sib)
    pair.start()
    pair.wait()
    lane = iota((40, 128), 1)
    for k in range(5):
        acc = jnp.zeros((40, 128), f32)
        for f in range(NF):
            lo, hi = max(80 * f, 128 * k), min(80 * f + 80, 128 * k + 128)
            if lo < hi:
                turned = pltpu.roll(gath[f // 2, f % 2], (80 * f - 128 * k) % 128, 1)
                acc = jnp.where((lane >= lo - 128 * k) & (lane < hi - 128 * k), turned, acc)
        par[:, 128 * k : 128 * k + 128] = acc
    bridge8 = jnp.concatenate([par[0:16, :].astype(bf16)] * 8, axis=0)

    def rows(j):
        return pl.ds(pl.multiple_of(j * BLK, BLK), BLK)

    def base_rows(j):
        pick = iota((BLK, 128), 1) // 16 == j
        x = jnp.where(pick, stem[...], 0.0).astype(bf16)
        return jnp.dot(x, bridge8, preferred_element_type=f32)

    def base_block(j, carry):
        inner[rows(j), :] = base_rows(j)
        return carry

    lax.fori_loop(0, 8, base_block, 0)
    local_stats(inner, mask, count, ex.mine(0))
    ex.send(0)
    ga.zsend(2)
    ga.relay(0)
    ga.turn(0)
    ga.relay(1)

    def inner_rows(j):
        return inner[rows(j), :]

    def block_rows(j):
        return block[rows(j), :]

    def dfl_rows(j):
        return dfl[rows(j), :]

    def gain(k):
        return par[16 + 2 * k : 17 + 2 * k, :]

    def shift(k):
        return par[17 + 2 * k : 18 + 2 * k, :]

    def normed(src, stats, k, S):
        mean, scale = stats[:2]

        def one(j, acc):
            hat = (src(j) - mean) * scale
            out = jnp.maximum(gain(k) * hat + shift(k), 0.0)
            spread_rows(S, j, out)
            m = jnp.concatenate([mask[...]] * 5, axis=1)
            return acc + jnp.sum((out * m).reshape(BLK // 8, 8, C), axis=0)

        acc = lax.fori_loop(0, 8, one, jnp.zeros((8, C), f32))
        return jnp.sum(acc, axis=0, keepdims=True)

    stats0 = joint_stats(ex, 0)
    labs = remote(lab.at[0], lab.at[1], lbs, lbr, p.b, p.sib)
    lab[0] = slots[0, :, 6, :]
    labs.start()
    put_spare(ex.mine(1), normed(inner_rows, stats0, 0, SA))
    for s in range(3, 6):
        ga.zsend(s)

    def conv(k, u, dst, start, acts):
        def one(it, carry):
            r0 = pl.multiple_of(it * 384, 384)
            at = pl.ds(r0, 384)
            d = conv_part(SB if k else SA, W, k, u, r0, 384)
            dst[at, :] = (dst[at, :] if start is None else start(it)) + d if start != 0 else d
            for when, act in acts.items():
                pl.when(it == when)(act)
            return carry

        lax.fori_loop(0, 4, one, 0)

    def share(u, S=SA):
        return remote(S[u], S2.at[u], ts.at[u], tr.at[u], p.b, p.sib)

    def doing(f, *a):
        return lambda: f(*a)

    ga.relay(2)
    ga.turn(1)
    ga.across(0)
    ga.arrive(0)
    conv(0, 0, inner, 0, {0: doing(ga.turn, 2), 1: doing(ga.relay, 3)})
    ga.across(1)
    ga.across(2)
    ga.arrive(1)
    conv(0, 1, inner, None, {1: doing(ga.relay, 4)})
    ga.arrive(2)
    conv(0, 2, inner, None, {0: doing(ga.turn, 3), 2: doing(ga.relay, 5)})
    ga.turn(4)
    local_stats(inner, mask, count, ex.mine(1))
    ex.send(1)
    ga.across(3)
    ga.turn(5)
    stats1 = joint_stats(ex, 1)
    put_spare(ex.mine(2), normed(inner_rows, stats1, 1, SB))
    ga.arrive(3)
    conv(1, 0, block, lambda it: jnp.concatenate([base_rows(2 * it), base_rows(2 * it + 1)], axis=0),
         {1: doing(ga.across, 4), 3: doing(ga.across, 5)})
    ga.arrive(4)
    for u in range(3):
        share(u, SB).start()
    conv(1, 1, block, None, {})
    ga.arrive(5)
    conv(1, 2, block, None, {})
    local_stats(block, mask, count, ex.mine(2))
    ex.send(2)
    for s in range(6):
        ga.drain(s)
    lane = iota((IMG, 16), 1)
    label = column(own_row, IMG)
    mate = column(partner[...].astype(f32), IMG)
    home = jnp.floor((mate + 0.5) / 24.0)
    chip = jnp.floor((home + 0.5) / 2.0)
    at_chip = (iota((IMG, NCHIP), 1).astype(f32) == chip).astype(bf16)
    labs.wait()
    own_side = jnp.dot(at_chip, lab[0].astype(bf16), preferred_element_type=f32)
    sib_side = jnp.dot(at_chip, lab[1].astype(bf16), preferred_element_type=f32)
    there = jnp.where(home - 2.0 * chip == p.c.astype(f32), own_side, sib_side)
    spot = iota((IMG, 128), 1).astype(f32) == mate - 24.0 * home
    mate_label = jnp.sum(jnp.where(spot, there, 0.0), axis=1, keepdims=True)
    lane_f = lane.astype(f32)
    target = own_share * (lane_f == label).astype(f32) + (1.0 - own_share) * (
        lane_f == mate_label
    ).astype(f32)
    live = lane < 10
    head16 = par[24:40, :].astype(bf16)
    pad[...] = jnp.zeros((8, 128), f32)
    pad[0:1, 0:10] = bias[...]
    sides = sibs[0, 0] + sibs[0, 1]
    total = jnp.sum(sides[7:8, 0:1])
    valid_count = jnp.sum(sides[5:6, 0:1])
    stats2 = joint_stats(ex, 2)
    mu0, mu1 = stats1[2] / valid_count, stats2[2] / valid_count

    def pool(j, acc):
        hat = (block_rows(j) - stats2[0]) * stats2[1]
        out = jnp.maximum(gain(2) * hat + shift(2), 0.0)
        return acc + jnp.sum(out.reshape(8, IMG, C), axis=0)

    pooled = lax.fori_loop(0, 8, pool, jnp.zeros((IMG, C), f32)) / 64.0
    pooled = pooled.astype(bf16)
    logits = lax.dot_general(pooled, head16, AC, preferred_element_type=f32) + pad[0:1, 0:16]
    top = jnp.max(jnp.where(live, logits, -3e38), axis=1, keepdims=True)
    moved = jnp.where(live, logits - top, 0.0)
    size_sum = jnp.sum(jnp.where(live, jnp.exp(moved), 0.0), axis=1, keepdims=True)
    logp = moved - jnp.log(size_sum)
    loss_part = -jnp.sum(
        weight * jnp.sum(jnp.where(live, target * logp, 0.0), axis=1, keepdims=True)
    )
    d_logits = jnp.where(live, (jnp.exp(logp) - target) * (weight / total), 0.0).astype(bf16)
    g_bias = jnp.sum(d_logits.astype(f32), axis=0, keepdims=True)
    few[0, 0:16, :] = lax.dot_general(d_logits, pooled, CC, preferred_element_type=f32)
    rs.give(0).start()
    d_pooled = jnp.dot(d_logits, head16, preferred_element_type=f32)
    d_out24 = d_pooled / 64.0

    def zhat(src, j, stats):
        return (src(j) - stats[0]) * stats[1]

    def passed(hat, k, d_out):
        return jnp.where(gain(k) * hat + shift(k) > 0.0, d_out, 0.0)

    def grad_sums(src, stats, k, d_of, e):
        def one(j, acc):
            hat = zhat(src, j, stats)
            got = passed(hat, k, d_of(j))
            return (
                acc[0] + jnp.sum(got.reshape(BLK // 8, 8, C), axis=0),
                acc[1] + jnp.sum((got * hat).reshape(BLK // 8, 8, C), axis=0),
            )

        zero = jnp.zeros((8, C), f32)
        acc = lax.fori_loop(0, 8, one, (zero, zero))
        put_row(ex.mine(e), 0, jnp.sum(acc[0], axis=0, keepdims=True))
        put_row(ex.mine(e), 8, jnp.sum(acc[1], axis=0, keepdims=True))

    def grad_rows(src, stats, k, d_of, sums, j):
        hat = zhat(src, j, stats)
        m = jnp.concatenate([mask[...]] * 5, axis=1)
        got = passed(hat, k, d_of(j))
        return (gain(k) * stats[1]) * (got - m * (sums[0] + hat * sums[1]) / valid_count)

    def head_rows(j):
        return jnp.concatenate([d_out24] * 8, axis=0)

    def turn(src):
        for it in range(4):
            x = src[384 * it : 384 * it + 384, :].T.astype(bf16)
            for f in range(NF):
                dyT[f // 2, f % 2, :, 384 * it : 384 * it + 384] = x[80 * f : 80 * f + 80]

    trade = remote(dyT.at[:, 1 - p.c], dyS, us, ur, p.b, p.sib)

    grad_sums(block_rows, stats2, 2, head_rows, 3)
    slot = ex.mine(3)
    slot[5:6, :] = jnp.full((1, 128), loss_part, f32)
    slot[6:7, :] = jnp.concatenate([g_bias, jnp.zeros((1, 112), f32)], axis=1)
    ex.send(3)
    tot3 = ex.total(3)
    sums2 = wide(tot3[0:5]), wide(tot3[8:13])

    def low_sums(dst, src, stats, k, d_of, sums):
        def one(j, acc):
            d = grad_rows(src, stats, k, d_of, sums, j)
            dst[rows(j), :] = d
            return acc + jnp.sum(d.astype(bf16).astype(f32).reshape(BLK // 8, 8, C), axis=0)

        acc = lax.fori_loop(0, 8, one, jnp.zeros((8, C), f32))
        return jnp.sum(acc, axis=0, keepdims=True)

    def lost(dy_sums, mu):
        at = 64 * p.b + iota((64, C), 0)
        o = at - 80 * ((at >= 80).astype(jnp.int32) + (at >= 160).astype(jnp.int32))
        hit = (iota((64, C), 1) == 80 * p.f + o) & (at < 240)
        return jnp.sum(jnp.where(hit, dy_sums, 0.0), axis=1, keepdims=True) * mu

    put_spare(ex.mine(4), low_sums(block, block_rows, stats2, 2, head_rows, sums2))
    turn(block)
    trade.start()
    first_grad(p, SB, dyT, dfl)
    for u in range(3):
        share(u, SB).wait()
    trade.wait()
    filter_grad(p, SB, S2, dyT, dyS, DS, mu1, G, 0, dfl)
    sc.begin(0)
    filter_grad(p, SB, S2, dyT, dyS, DS, mu1, G, 1, dfl)
    sc.begin(1)
    rs.along(0)
    def spread(src):
        def one(j, carry):
            spread_rows(SA, j, src[rows(j), :])
            return carry

        lax.fori_loop(0, 8, one, 0)

    spread(block)

    def back_conv1(it, carry):
        r0 = pl.multiple_of(it * 384, 384)
        dfl[pl.ds(r0, 384), :] = conv_back_rows(SA, W, 1, r0, 384)

        @pl.when(it == 0)
        def _():
            sc.mid(0)

        @pl.when(it == 2)
        def _():
            sc.mid(1)

        return carry

    lax.fori_loop(0, 4, back_conv1, 0)
    grad_sums(inner_rows, stats1, 1, dfl_rows, 4)
    ex.send(4)
    sc.along(0)
    filter_grad(p, SB, S2, dyT, dyS, DS, mu1, G, 2, None)
    sc.begin(2)
    rs.square(0)
    pl.semaphore_signal(free, inc=1, device_id=(p.b, p.sib), device_id_type=MESH)
    normed(base_rows, stats0, 0, SA)
    sc.along(1)
    tot4 = ex.total(4)
    pl.semaphore_wait(free, 1)
    share(0).start()
    sums1 = wide(tot4[0:5]), wide(tot4[8:13])
    lost1 = lost(spare(tot4), mu1)
    put_spare(ex.mine(5), low_sums(dfl, inner_rows, stats1, 1, dfl_rows, sums1))
    turn(dfl)
    trade.start()
    for u in range(1, 3):
        share(u).start()
    first_grad(p, SA, dyT, inner)
    sc.mid(2)
    squares = sc.final(0, lost1)
    sc.clear(0)
    share(0).wait()
    trade.wait()
    filter_grad(p, SA, S2, dyT, dyS, DS, mu0, G, 3, inner)
    sc.begin(3)
    rs.close(0)
    sc.clear(1)
    share(1).wait()
    filter_grad(p, SA, S2, dyT, dyS, DS, mu0, G, 4, inner)
    sc.begin(4)
    sc.along(2)
    sc.clear(2)
    share(2).wait()
    filter_grad(p, SA, S2, dyT, dyS, DS, mu0, G, 5, inner)
    sc.mid(3)
    sc.begin(5)
    spread(dfl)

    def back_conv0(it, carry):
        r0 = pl.multiple_of(it * 384, 384)
        inner[pl.ds(r0, 384), :] = conv_back_rows(SA, W, 0, r0, 384)

        @pl.when(it == 1)
        def _():
            sc.mid(4)

        @pl.when(it == 2)
        def _():
            sc.clear_line(0)
            sc.along(3)

        return carry

    lax.fori_loop(0, 4, back_conv0, 0)

    sc.mid(5)
    grad_sums(base_rows, stats0, 0, inner_rows, 5)
    ex.send(5)
    squares = squares + sc.final(1, lost1) + sc.final(2, lost1)
    sc.clear_line(1)
    sc.along(4)
    tot5 = ex.total(5)
    lost0 = lost(spare(tot5), mu0)
    squares = squares + sc.final(3, lost0)
    sc.clear_line(2)
    sc.along(5)
    sums0 = wide(tot5[0:5]), wide(tot5[8:13])
    grid16 = dfl.at[512:640]
    grid16[...] = jnp.zeros((128, C), f32)
    dstem[...] = jnp.zeros((BLK, 128), f32)

    def back0(i, carry):
        total_g, total_s = None, None
        for h in range(4):
            j = 4 * i + h
            d = block[rows(j), :] + grad_rows(base_rows, stats0, 0, inner_rows, sums0, j)
            d = d.astype(bf16)
            pick = iota((BLK, 128), 1) // 16 == j
            x = jnp.where(pick, stem[...], 0.0).astype(bf16)
            g = lax.dot_general(x, d, CC, preferred_element_type=f32)
            y = jnp.where(pick, lax.dot_general(d, bridge8, AC, preferred_element_type=f32), 0.0)
            total_g = g if total_g is None else total_g + g
            total_s = y if total_s is None else total_s + y
        grid16[...] += total_g
        dstem[...] += total_s
        return carry

    lax.fori_loop(0, 2, back0, 0)
    acc = grid16[0:16, :]
    for j in range(1, 8):
        acc = acc + grid16[16 * j : 16 * j + 16, :]
    few[1, 0:16, :] = acc
    rs.give(1).start()
    low = dstem[...].astype(bf16)
    high = lax.Precision.HIGHEST
    acc = None
    for c in range(3):
        t = lax.dot_general(
            AB[:, 128 * c : 128 * c + 128].astype(bf16), low, CC, preferred_element_type=f32
        )
        d = lax.dot_general(hits(c), t, CC, precision=high, preferred_element_type=f32)
        acc = d if acc is None else acc + d
    acc = jnp.where(own_j, acc, 0.0)
    fold = (jnp.bitwise_and(iota((256, 128), 0), 31) == iota((256, 128), 1)).astype(f32)
    acc = lax.dot_general(acc, fold, CC, precision=high, preferred_element_type=f32)
    slots[6, p.chip] = jnp.dot(
        tile_c.astype(f32), acc, precision=high, preferred_element_type=f32
    )
    ex.send(6)
    rs.along(1)
    squares = squares + sc.final(4, lost0)
    rs.square(1)
    g_stem = ex.total(6)
    squares = squares + sc.final(5, lost0)
    slots[7, p.chip] = jnp.full((16, 128), jnp.sum(squares), f32)
    ex.send(7)
    rs.close(1)
    both = jnp.concatenate([rs.result(1), rs.result(0)], axis=0)
    bias_all = tot3[6:7, :]
    stem_o[...] = g_stem
    ng = [row for sums in (sums0, sums1, sums2) for row in (sums[1], sums[0])]
    ng = jnp.concatenate(ng + [jnp.zeros((2, C), f32)], axis=0)
    every = jnp.concatenate([both, ng], axis=0)
    pick = (iota((C, 128), 0) == 80 * p.f + iota((C, 128), 1)) & (iota((C, 128), 1) < 80)
    own_o[...] = jnp.dot(every, pick.astype(f32), precision=high, preferred_element_type=f32)
    other = jnp.sum(every * every) + jnp.sum(g_stem * g_stem) + jnp.sum(bias_all * bias_all)
    conv_sq = ex.total(7)[0:1, :]
    misc_o[...] = jnp.zeros((8, 128), f32)
    misc_o[0:1, :] = jnp.sqrt(conv_sq + other)
    misc_o[1:2, :] = tot3[5:6, :] / total
    misc_o[2:3, :] = bias_all
    for e in range(6):
        sc.end(e)
    for e in range(3, 6):
        sc.clear(e)
        sc.clear_line(e)
    for e in range(8):
        ex.drain(e)
    rs.drain(0)
    rs.drain(1)


def step_call(images, labels, partner, valid, sizes, stem_w, bridge_t, conv_w, norm, head, bias):
    V, A, SM = pltpu.VMEM, pl.ANY, pltpu.SMEM
    spec = lambda m: pl.BlockSpec(memory_space=m)
    D = pltpu.SemaphoreType.DMA
    sh = jax.ShapeDtypeStruct
    return pl.pallas_call(
        step_kernel,
        out_shape=(
            sh((2, 3, 256, C), bf16), sh((40, 128), f32), sh((16, 128), f32), sh((8, 128), f32),
        ),
        in_specs=[
            spec(V), spec(V), spec(V), spec(V), spec(SM), spec(V), spec(V), spec(A), spec(V), spec(V), spec(V),
        ],
        out_specs=(spec(V),) * 4,
        scratch_shapes=[
            V((2, 3, NZ, 2, 256, C), bf16), V((3, 10 * BLK, C), bf16), V((3, 10 * BLK, C), bf16), V((10 * BLK, C), bf16),
            V((NZ, 2, 80, ROWS), bf16), V((NZ, 80, ROWS), bf16), V((NZ * 80, 128), f32),
            V((ROWS, C), f32), V((ROWS, C), f32), V((ROWS, C), f32),
            V((3, 3, 256, C), bf16), V((6, 3, 64, C), LINE), V((3, NZ, 256, C), bf16), V((3, NZ, 64, C), LINE),
            V((8, NCHIP, 16, 128), f32), V((8, 2, 16, 128), f32), V((2, NCHIP, 128), f32), V((2, 112, C), f32), V((NZ, 2, 40, 128), f32), V((40, C), f32),
            V((BLK, 128), f32), V((BLK, 384), f32), V((BLK, 128), f32), V((BLK, 128), f32), V((8, 128), f32),
            D((8,)), D((8,)), D((8,)), D((8,)), D, D, D((2,)), D((2,)), D((6, 4)), D((6, 4)), D((6, 12)), D((6, 12)), D((6,)), D((6,)), D((6,)),
            D((6, 6)), D((6, 6)), D((6, 3)), D((6, 3)), D((6, 3)), D((6, 3)), D((3,)), D((3,)), D, D,
            pltpu.SemaphoreType.REGULAR, D((2, 4)), D((2, 4)),
        ],
        compiler_params=pltpu.CompilerParams(
            collective_id=0, has_side_effects=True, vmem_limit_bytes=63 << 20
        ),
    )(images, labels, partner, valid, sizes, stem_w, bridge_t, conv_w, norm, head, bias)


def adam_rule(g, w, m, v, rate, shrink, factor):
    clipped = g * factor
    m = beta_one * m + (1.0 - beta_one) * clipped
    v = beta_two * v + (1.0 - beta_two) * clipped * clipped
    ahead = m / (1.0 - beta_one**STEP)
    behind = v / (1.0 - beta_two**STEP)
    return w - rate * (ahead / (jnp.sqrt(behind) + adam_eps) + shrink * w), m, v


def adam_kernel(G, misc, own, stem_g, *refs):
    ins, outs, (norm_o, loss_o, held, GV, lsem, osem, gsem) = refs[:18], refs[18:36], refs[36:]
    norm_o[...] = misc[0:1, 0:1]
    loss_o[...] = misc[1:2, 0:1]
    factor = clip_norm / jnp.maximum(misc[0:1, :], clip_norm)
    wide_factor = jnp.concatenate([factor] * 5, axis=1)

    def load(s, i):
        return pltpu.make_async_copy(ins[i].at[s // 3, s % 3], held.at[i, s], lsem.at[i, s])

    def store(s, i):
        return pltpu.make_async_copy(held.at[i, s], outs[i].at[s // 3, s % 3], osem.at[i, s])

    def grad(s):
        return pltpu.make_async_copy(G.at[s // 3, s % 3], GV.at[s], gsem.at[s])

    for s in range(6):
        grad(s).start()
        for i in range(3):
            load(s, i).start()

    def write(i, g, rate, shrink, f):
        w, m, v = (r[...] for r in ins[3 * i : 3 * i + 3])
        for o, x in zip(outs[3 * i : 3 * i + 3], adam_rule(g, w, m, v, rate, shrink, f)):
            o[...] = x

    write(1, stem_g[:, 0:27], 0.5, 0.05, factor[:, 0:27])
    write(2, own[0:16, 0:80], 0.6, 0.05, factor[:, 0:80])
    write(3, own[32:38, 0:80], 0.5, 0.0, factor[:, 0:80])
    write(4, own[16:26, 0:80], 0.1, 0.05, factor[:, 0:80])
    write(5, misc[2:3, 0:10], 0.5, 0.0, factor[:, 0:10])
    for s in range(6):
        for i in range(3):
            load(s, i).wait()
        grad(s).wait()

        def part(j, carry):
            at = pl.ds(pl.multiple_of(j * 48, 16), 48)
            new = adam_rule(
                GV[s, at, :].astype(f32), held[0, s, at, :], held[1, s, at, :], held[2, s, at, :],
                0.033, 0.05, wide_factor,
            )
            for i in range(3):
                held[i, s, at, :] = new[i]
            return carry

        lax.fori_loop(0, 5, part, 0)
        for i in range(3):
            store(s, i).start()
    for s in range(6):
        for i in range(3):
            store(s, i).wait()


def adam_call(G, misc, own, stem_g, *state):
    V, A, D = pltpu.VMEM, pl.ANY, pltpu.SemaphoreType.DMA
    spec = lambda m: pl.BlockSpec(memory_space=m)
    return pl.pallas_call(
        adam_kernel,
        out_shape=tuple(jax.ShapeDtypeStruct(s, f32) for s in [x.shape for x in state] + [(1, 1)] * 2),
        in_specs=[spec(A)] + [spec(V)] * 3 + [spec(A)] * 3 + [spec(V)] * 15,
        out_specs=tuple([spec(A)] * 3 + [spec(V)] * 17),
        scratch_shapes=[V((3, 6, 240, C), f32), V((6, 256, C), bf16), D((3, 6)), D((3, 6)), D((6,))],
        compiler_params=pltpu.CompilerParams(vmem_limit_bytes=62 << 20),
    )(G, misc, own, stem_g, *state)


def make_patches(images):
    number = images.shape[0]
    grid = images.reshape(number, 3, 32, 32)
    padded = jnp.pad(grid, ((0, 0), (0, 0), (1, 1), (1, 1)))
    pieces = [
        padded[:, :, row_off : row_off + 29 : 4, col_off : col_off + 29 : 4]
        for row_off in range(3)
        for col_off in range(3)
    ]
    stacked = jnp.stack(pieces, axis=2)
    return jnp.transpose(stacked, (1, 2, 0, 3, 4)).reshape(27, number * 64)


def shifted(feature_field):
    width, rows = feature_field.shape
    grid = feature_field.reshape(width, rows // 64, 8, 8)
    padded = jnp.pad(grid, ((0, 0), (0, 0), (1, 1), (1, 1)))
    pieces = [
        padded[:, :, row_off : row_off + 8, col_off : col_off + 8]
        for row_off in range(3)
        for col_off in range(3)
    ]
    return jnp.stack(pieces, axis=0).reshape(9 * width, rows)


def unshifted(parts, width):
    rows = parts.shape[1]
    grid = parts.reshape(9, width, rows // 64, 8, 8)
    summed = jnp.zeros((width, rows // 64, 10, 10), jnp.float32)
    for row_off in range(3):
        for col_off in range(3):
            summed = summed + jnp.pad(
                grid[3 * row_off + col_off],
                ((0, 0), (0, 0), (row_off, 2 - row_off), (col_off, 2 - col_off)),
            )
    return summed[:, :, 1:9, 1:9].reshape(width, rows)


def image_weights(valid_mask, group_sizes):
    shards, groups = group_sizes.shape
    capacity = valid_mask.shape[0] // shards
    group_ends = jnp.cumsum(group_sizes, axis=1)
    slot_index = jnp.arange(capacity, dtype=jnp.int32)
    member = jnp.sum(
        (slot_index[None, :, None] >= group_ends[:, None, :]).astype(jnp.int32), axis=2
    )
    member = jnp.minimum(member, groups - 1)
    chosen = (member[:, :, None] == jnp.arange(groups, dtype=jnp.int32)[None, None, :]).astype(
        jnp.float32
    )
    sizes_each = jnp.sum(chosen * group_sizes[:, None, :].astype(jnp.float32), axis=2)
    return valid_mask.astype(jnp.float32) / sizes_each.reshape(-1)


def norm_forward(feature_field, norm_gain, norm_shift, row_validity_mask, valid_count):
    batch_mean = (
        lax.psum(jnp.sum(feature_field * row_validity_mask, axis=1), ("batch", "filt"))
        / valid_count
    )
    centered_input = feature_field - batch_mean[:, None]
    batch_variance = (
        lax.psum(
            jnp.sum(centered_input * centered_input * row_validity_mask, axis=1), ("batch", "filt")
        )
        / valid_count
    )
    inverse_scale = lax.rsqrt(batch_variance + norm_epsilon)
    normalized_input = (feature_field - batch_mean[:, None]) * inverse_scale[:, None]
    norm_output = jnp.maximum(norm_gain[:, None] * normalized_input + norm_shift[:, None], 0.0)
    return (norm_output, normalized_input, inverse_scale)


def masked_norm_backward(
    output_gradient,
    norm_output,
    normalized_input,
    inverse_scale,
    norm_gain,
    row_validity_mask,
    valid_count,
):
    passed_rows = jnp.where(norm_output > 0.0, output_gradient, 0.0)
    shift_gradient, gain_gradient = lax.psum(
        (jnp.sum(passed_rows, axis=1), jnp.sum(passed_rows * normalized_input, axis=1)),
        ("batch", "filt"),
    )
    input_gradient = (
        passed_rows
        - row_validity_mask[None, :]
        * (shift_gradient[:, None] + normalized_input * gain_gradient[:, None])
        / valid_count
    )
    return ((norm_gain * inverse_scale)[:, None] * input_gradient, gain_gradient, shift_gradient)


def conv_forward(feature_field, weight_shard):
    stacked = shifted(feature_field)
    low_shard = weight_shard.astype(jnp.bfloat16)
    piece = lax.all_gather(low_shard, "filt", axis=0, tiled=True)
    norm_output = jnp.dot(
        piece.reshape(piece.shape[0], -1), stacked, preferred_element_type=jnp.float32
    )
    return (norm_output, None)


def conv_backward(feature_field, weight_shard, output_gradient):
    width = feature_field.shape[0]
    stacked = shifted(feature_field)
    rows_grad = output_gradient
    term = lax.dot_general(
        rows_grad, stacked, (((1,), (1,)), ((), ())), preferred_element_type=jnp.float32
    )
    weight_grad = lax.psum_scatter(
        term.reshape(lax.axis_size("filt") * weight_shard.shape[0], 9, width),
        "filt",
        scatter_dimension=0,
        tiled=True,
    )
    piece = lax.all_gather(weight_shard.astype(jnp.bfloat16), "filt", axis=0, tiled=True)
    rows_grad = output_gradient
    back = lax.dot_general(
        piece.reshape(piece.shape[0], -1),
        rows_grad,
        (((0,), (0,)), ((), ())),
        preferred_element_type=jnp.float32,
    )
    return (unshifted(back, width), weight_grad)


def adam_step(weight, output_gradient, first, second, rate, shrink, factor):
    clipped = output_gradient * factor
    first = beta_one * first + (1.0 - beta_one) * clipped
    second = beta_two * second + (1.0 - beta_two) * clipped * clipped
    ahead = first / (1.0 - beta_one**STEP)
    behind = second / (1.0 - beta_two**STEP)
    return (
        weight - rate * (ahead / (jnp.sqrt(behind) + adam_eps) + shrink * weight),
        first,
        second,
    )


def body(
    images,
    labels,
    partner,
    valid_mask,
    group_sizes,
    stem_weight,
    bridge_weight,
    conv_weight,
    norm_params,
    head_weight,
    head_bias,
    stem_first,
    stem_second,
    bridge_first,
    bridge_second,
    conv_first,
    conv_second,
    norm_first,
    norm_second,
    head_first,
    head_second,
    bias_first,
    bias_second,
):
    width = bridge_weight.shape[0]
    bridge_all, norm_all, head_all = (
        lax.all_gather(bridge_weight, "filt", axis=0, tiled=True),
        lax.all_gather(norm_params, "filt", axis=1, tiled=True),
        lax.all_gather(head_weight, "filt", axis=1, tiled=True),
    )
    labels_all, valid_all = (
        lax.all_gather(labels, ("batch", "filt"), axis=0, tiled=True),
        lax.all_gather(valid_mask, ("batch", "filt"), axis=0, tiled=True),
    )
    weight_all = image_weights(valid_all, group_sizes)
    total = jnp.sum(weight_all)
    valid_count = 64.0 * jnp.sum(valid_all.astype(jnp.float32))
    local = images.shape[0]
    image_weight = lax.dynamic_slice_in_dim(
        weight_all, lax.axis_index(("batch", "filt")) * local, local
    )
    row_validity_mask = jnp.repeat(valid_mask.astype(jnp.float32), 64)
    patch = make_patches(images)
    stem = jnp.dot(
        stem_weight.astype(jnp.bfloat16), patch, preferred_element_type=jnp.float32
    ).astype(jnp.bfloat16)
    base = jnp.dot(bridge_all.astype(jnp.bfloat16), stem, preferred_element_type=jnp.float32)
    first, first_hat, first_scale = norm_forward(
        base, norm_all[0], norm_all[1], row_validity_mask, valid_count
    )
    first_low = first.astype(jnp.bfloat16)
    inner, kept_zero = conv_forward(first_low, conv_weight[0])
    second, second_hat, second_scale = norm_forward(
        inner, norm_all[2], norm_all[3], row_validity_mask, valid_count
    )
    second_low = second.astype(jnp.bfloat16)
    branch, kept_one = conv_forward(second_low, conv_weight[1])
    final, final_hat, final_scale = norm_forward(
        base + branch, norm_all[4], norm_all[5], row_validity_mask, valid_count
    )
    pooled = jnp.mean(final.reshape(final.shape[0], local, 64), axis=2).astype(jnp.bfloat16)
    logits = (
        jnp.dot(head_all.astype(jnp.bfloat16), pooled, preferred_element_type=jnp.float32)
        + head_bias[:, None]
    )
    moved = logits - jnp.max(logits, axis=0, keepdims=True)
    logp = moved - jnp.log(jnp.sum(jnp.exp(moved), axis=0, keepdims=True))
    classes = jnp.arange(logits.shape[0], dtype=jnp.int32)
    partner_labels = jnp.take(labels_all, partner)
    target = own_share * (labels[None, :] == classes[:, None]).astype(jnp.float32) + (
        1.0 - own_share
    ) * (partner_labels[None, :] == classes[:, None]).astype(jnp.float32)
    loss_part = -jnp.sum(image_weight * jnp.sum(target * logp, axis=0))
    d_logits = ((jnp.exp(logp) - target) * (image_weight / total)[None, :]).astype(jnp.bfloat16)
    bias_grad = jnp.sum(d_logits.astype(jnp.float32), axis=1)
    head_grad = lax.dot_general(
        d_logits, pooled, (((1,), (1,)), ((), ())), preferred_element_type=jnp.float32
    )
    d_pooled = lax.dot_general(
        head_all.astype(jnp.bfloat16),
        d_logits,
        (((0,), (0,)), ((), ())),
        preferred_element_type=jnp.float32,
    )
    d_final = jnp.repeat(d_pooled / 64.0, 64, axis=1)
    d_block, gain_two, shift_two = masked_norm_backward(
        d_final, final, final_hat, final_scale, norm_all[4], row_validity_mask, valid_count
    )
    d_second, conv_grad_one = conv_backward(
        second_low, conv_weight[1], d_block.astype(jnp.bfloat16)
    )
    d_inner, gain_one, shift_one = masked_norm_backward(
        d_second, second, second_hat, second_scale, norm_all[2], row_validity_mask, valid_count
    )
    d_first, conv_grad_zero = conv_backward(first_low, conv_weight[0], d_inner.astype(jnp.bfloat16))
    d_lower, gain_zero, shift_zero = masked_norm_backward(
        d_first, first, first_hat, first_scale, norm_all[0], row_validity_mask, valid_count
    )
    d_base = (d_block + d_lower).astype(jnp.bfloat16)
    bridge_grad = lax.dot_general(
        d_base, stem, (((1,), (1,)), ((), ())), preferred_element_type=jnp.float32
    )
    d_stem = lax.dot_general(
        bridge_all.astype(jnp.bfloat16),
        d_base,
        (((0,), (0,)), ((), ())),
        preferred_element_type=jnp.float32,
    ).astype(jnp.bfloat16)
    stem_grad = lax.dot_general(
        d_stem, patch, (((1,), (1,)), ((), ())), preferred_element_type=jnp.float32
    )
    bridge_part, head_part = (
        lax.psum_scatter(bridge_grad, "filt", scatter_dimension=0, tiled=True),
        lax.psum_scatter(head_grad, "filt", scatter_dimension=1, tiled=True),
    )
    conv_grad, bridge_sum, head_sum = lax.psum(
        (jnp.stack([conv_grad_zero, conv_grad_one]), bridge_part, head_part), "batch"
    )
    stem_sum, bias_sum, loss_sum = lax.psum((stem_grad, bias_grad, loss_part), ("batch", "filt"))
    norm_full = jnp.stack([gain_zero, shift_zero, gain_one, shift_one, gain_two, shift_two])
    norm_grad = lax.dynamic_slice_in_dim(norm_full, lax.axis_index("filt") * width, width, 1)
    owned_square = (
        jnp.sum(conv_grad * conv_grad)
        + jnp.sum(bridge_sum * bridge_sum)
        + jnp.sum(norm_grad * norm_grad)
        + jnp.sum(head_sum * head_sum)
    )
    squares_all = (
        lax.psum(owned_square, "filt") + jnp.sum(stem_sum * stem_sum) + jnp.sum(bias_sum * bias_sum)
    )
    grad_norm = jnp.sqrt(squares_all)
    factor = clip_norm / jnp.maximum(grad_norm, clip_norm)
    stem_new = adam_step(stem_weight, stem_sum, stem_first, stem_second, 0.5, 0.05, factor)
    bridge_new = adam_step(
        bridge_weight, bridge_sum, bridge_first, bridge_second, 0.6, 0.05, factor
    )
    conv_new = adam_step(conv_weight, conv_grad, conv_first, conv_second, 0.033, 0.05, factor)
    norm_new = adam_step(norm_params, norm_grad, norm_first, norm_second, 0.5, 0.0, factor)
    head_new = adam_step(head_weight, head_sum, head_first, head_second, 0.1, 0.05, factor)
    bias_new = adam_step(head_bias, bias_sum, bias_first, bias_second, 0.5, 0.0, factor)
    return (
        stem_new[0],
        stem_new[1],
        stem_new[2],
        bridge_new[0],
        bridge_new[1],
        bridge_new[2],
        conv_new[0],
        conv_new[1],
        conv_new[2],
        norm_new[0],
        norm_new[1],
        norm_new[2],
        head_new[0],
        head_new[1],
        head_new[2],
        bias_new[0],
        bias_new[1],
        bias_new[2],
        grad_norm,
        loss_sum / total,
    )


def fast_body(
    images, labels, partner, valid_mask, group_sizes, stem_weight, bridge_weight, conv_weight, norm_params,
    head_weight, head_bias, stem_first, stem_second, bridge_first, bridge_second, conv_first, conv_second,
    norm_first, norm_second, head_first, head_second, bias_first, bias_second,
):
    width = bridge_weight.shape[0]
    def rows(x):
        return x.transpose(0, 2, 1, 3).reshape(2, 3, 3 * width, C)

    def back(x):
        return x.reshape(2, 9, width, C).transpose(0, 2, 1, 3)

    G, own, stem_g, misc = step_call(
        images, labels[None], partner[None], valid_mask[None], group_sizes, stem_weight, bridge_weight.T,
        conv_weight.transpose(0, 2, 1, 3), norm_params, head_weight, head_bias[None],
    )
    new = adam_call(
        G, misc, own, stem_g,
        rows(conv_weight), rows(conv_first), rows(conv_second),
        stem_weight, stem_first, stem_second,
        bridge_weight.T, bridge_first.T, bridge_second.T,
        norm_params, norm_first, norm_second,
        head_weight, head_first, head_second,
        head_bias[None], bias_first[None], bias_second[None],
    )
    conv, stem, bridge, norm, head, bias = (new[i : i + 3] for i in range(0, 18, 3))
    return (
        *stem,
        *(x.T for x in bridge),
        *(back(x) for x in conv),
        *norm,
        *head,
        *(x[0] for x in bias),
        new[18].reshape(()),
        new[19].reshape(()),
    )


def solution(mesh):
    in_specs = (
        P(("batch", "filt"), None),
        P(("batch", "filt")),
        P(("batch", "filt")),
        P(("batch", "filt")),
        P(),
        P(),
        P("filt", None),
        P(None, "filt", None, None),
        P(None, "filt"),
        P(None, "filt"),
        P(),
        P(),
        P(),
        P("filt", None),
        P("filt", None),
        P(None, "filt", None, None),
        P(None, "filt", None, None),
        P(None, "filt"),
        P(None, "filt"),
        P(None, "filt"),
        P(None, "filt"),
        P(),
        P(),
    )
    out_specs = (
        P(),
        P(),
        P(),
        P("filt", None),
        P("filt", None),
        P("filt", None),
        P(None, "filt", None, None),
        P(None, "filt", None, None),
        P(None, "filt", None, None),
        P(None, "filt"),
        P(None, "filt"),
        P(None, "filt"),
        P(None, "filt"),
        P(None, "filt"),
        P(None, "filt"),
        P(),
        P(),
        P(),
        P(),
        P(),
    )
    fits = mesh.shape["batch"] == NB and mesh.shape["filt"] == NF
    return jax.shard_map(fast_body if fits else body, mesh=mesh, in_specs=in_specs, out_specs=out_specs, check_vma=False)
```

```python
import jax
import jax.numpy as jnp
from jax import lax
from jax.experimental import pallas as pl
from jax.experimental.pallas import tpu as pltpu
from jax.sharding import PartitionSpec as P

STEP = 8

beta_one = 0.9
beta_two = 0.95
adam_eps = 1e-08
norm_epsilon = 1e-05
clip_norm = 0.01
own_share = 0.7

MESH = pl.DeviceIdType.MESH
bf16 = jnp.bfloat16
f32 = jnp.float32
LINE = bf16
NB, NF, NZ, NDEV, NCHIP = 4, 8, 4, 32, 16
C, IMG, ROWS = 640, 24, 1536
BLK = 8 * IMG
AC = (((1,), (1,)), ((), ()))
CC = (((0,), (0,)), ((), ()))


def iota(shape, dim):
    return lax.broadcasted_iota(jnp.int32, shape, dim)


def wide(row5):
    return jnp.concatenate([row5[k : k + 1, :] for k in range(5)], axis=1)


def column(row, n):
    eye = iota((n, n), 0) == iota((n, n), 1)
    return jnp.sum(jnp.where(eye, jnp.broadcast_to(row, (n, n)), 0.0), axis=1, keepdims=True)


class Place:
    def __init__(self):
        self.b = lax.axis_index("batch")
        self.f = lax.axis_index("filt")
        self.z = self.f // 2
        self.c = lax.rem(self.f, 2)
        self.me = self.b * NF + self.f
        self.chip = self.b * NZ + self.z
        self.xn = self.b + 1 - 2 * lax.rem(self.b, 2)
        self.yn = lax.rem(self.b + 2, NB)
        self.dn = (NB - 1) - self.b
        self.sib = self.f + 1 - 2 * self.c


def remote(src, dst, ssem, rsem, b, f):
    return pltpu.make_async_remote_copy(
        src_ref=src, dst_ref=dst, send_sem=ssem, recv_sem=rsem, device_id=(b, f), device_id_type=MESH
    )


def peers(p):
    for dz in (2, 1, 3, 0):
        for db in (3, 1, 2, 0):
            if dz or db:
                yield lax.rem(p.b + db, NB), lax.rem(p.z + dz, NZ)


def greet(p):
    sem = pltpu.get_barrier_semaphore()
    for b, z in peers(p):
        pl.semaphore_signal(sem, inc=1, device_id=(b, 2 * z + p.c), device_id_type=MESH)
    pl.semaphore_signal(sem, inc=1, device_id=(p.b, p.sib), device_id_type=MESH)


def met():
    pl.semaphore_wait(pltpu.get_barrier_semaphore(), NCHIP)


class Exchange:
    def __init__(self, p, slots, sibs, ssem, rsem, psem, qsem):
        self.p, self.slots, self.sibs = p, slots, sibs
        self.ssem, self.rsem, self.psem, self.qsem = ssem, rsem, psem, qsem

    def rows(self, e):
        return 8 if e == 7 else 16

    def mine(self, e):
        return self.slots.at[e, self.p.chip]

    def send(self, e):
        p = self.p
        mine = self.mine(e).at[0 : self.rows(e)]
        for b, z in peers(p):
            remote(mine, mine, self.ssem.at[e], self.rsem.at[e], b, 2 * z + p.c).start()

    def rest(self, e):
        p = self.p
        rest = self.slots.at[e, 0 : NCHIP - 1, 0 : self.rows(e)]
        return remote(rest, rest, self.ssem.at[e], self.rsem.at[e], p.b, p.sib)

    def across(self, e):
        p = self.p
        return remote(
            self.sibs.at[e, 0], self.sibs.at[e, 1], self.psem.at[e], self.qsem.at[e], p.b, p.sib
        )

    def wait(self, e):
        self.rest(e).wait_recv()

    def swap(self, e, value):
        self.sibs[e, 0] = value
        self.across(e).start()
        self.across(e).wait_recv()
        return self.sibs[e, 1]

    def drain(self, e):
        self.rest(e).wait_send()
        self.across(e).wait_send()

    def total(self, e):
        self.wait(e)
        own = jnp.sum(self.slots[e], axis=0)
        return own + self.swap(e, own)


def put_row(slot, row, value):
    for k in range(5):
        slot[row + k : row + k + 1, :] = value[:, 128 * k : 128 * k + 128]


def put_spare(slot, value):
    for k, row in enumerate((5, 6, 7, 13, 14)):
        slot[row : row + 1, :] = value[:, 128 * k : 128 * k + 128]


def spare(rows):
    return wide(jnp.concatenate([rows[5:8], rows[13:15]], axis=0))


def local_stats(src, mask, count, slot):
    def total(j, acc):
        x = src[pl.ds(pl.multiple_of(j * BLK, BLK), BLK), :]
        m = jnp.concatenate([mask[...]] * 5, axis=1)
        return acc + jnp.sum((x * m).reshape(BLK // 8, 8, C), axis=0)

    acc = lax.fori_loop(0, 8, total, jnp.zeros((8, C), f32))
    own_sum = jnp.sum(acc, axis=0, keepdims=True)
    own_mean = own_sum / jnp.maximum(count, 1.0)

    def squares(j, acc):
        x = src[pl.ds(pl.multiple_of(j * BLK, BLK), BLK), :]
        m = jnp.concatenate([mask[...]] * 5, axis=1)
        d = x - own_mean
        return acc + jnp.sum((d * d * m).reshape(BLK // 8, 8, C), axis=0)

    acc = lax.fori_loop(0, 8, squares, jnp.zeros((8, C), f32))
    put_row(slot, 0, own_sum)
    put_row(slot, 8, jnp.sum(acc, axis=0, keepdims=True))


def joint_stats(ex, e):
    ex.wait(e)
    every = ex.slots[e]
    n = ex.slots[0, :, 5:6, :]
    sums = every[:, 0:5, :]
    n_own, s_own = jnp.sum(n, axis=0), jnp.sum(sums, axis=0)
    m_own = s_own / jnp.maximum(n_own, 1.0)
    off = sums / jnp.maximum(n, 1.0) - m_own[None]
    q_own = jnp.sum(every[:, 8:13, :] + n * off * off, axis=0)
    rest = jnp.sum(every[:, 5:8, :], axis=0)
    more = jnp.sum(every[:, 13:16, :], axis=0)
    got = ex.swap(e, jnp.concatenate([s_own, rest, q_own, more], axis=0))
    n_sib = ex.sibs[0, 1, 5:6, :]
    s_sib, q_sib = got[0:5], got[8:13]
    count = n_own + n_sib
    mean = (s_own + s_sib) / count
    a, b = m_own - mean, s_sib / jnp.maximum(n_sib, 1.0) - mean
    spread = ((q_own + q_sib) + (n_own * a * a + n_sib * b * b)) / count
    return wide(mean), wide(lax.rsqrt(spread + norm_epsilon)), spare(got + jnp.concatenate([s_own, rest, q_own, more], axis=0))


def spread_rows(S, j, x):
    at = pl.ds(pl.multiple_of((j + 1) * BLK, BLK), BLK)
    gap = jnp.zeros((IMG, C), f32)
    S[0][at, :] = jnp.concatenate([gap, x[: BLK - IMG]], axis=0).astype(bf16)
    S[1][at, :] = x.astype(bf16)
    S[2][at, :] = jnp.concatenate([x[IMG:], gap], axis=0).astype(bf16)


def conv_part(S, W, k, u, r0, M):
    lhs = jnp.concatenate([S[u][pl.ds(r0 + v * BLK, M), :] for v in range(3)], axis=1)
    rhs = jnp.concatenate(
        [
            jnp.concatenate(
                [W[k, u, z, c, v * 80 : v * 80 + 80, :] for z in range(NZ) for c in range(2)], axis=0
            )
            for v in range(3)
        ],
        axis=1,
    )
    return lax.dot_general(lhs, rhs, AC, preferred_element_type=f32)


class Gather:
    def __init__(self, p, W, zs, zr, xs, xr, ds, dr):
        self.p, self.W = p, W
        self.zs, self.zr, self.xs, self.xr, self.ds, self.dr = zs, zr, xs, xr, ds, dr

    def part(self, s, z, b, row, n):
        return self.W.at[
            s // 3, lax.rem(s, 3), z, self.p.c, pl.ds(pl.multiple_of(b * 64 + row, 32), n), :
        ]

    def zcopy(self, s, i):
        p = self.p
        mine = self.part(s, p.z, p.b, 0, 64)
        to = lax.rem(p.z + i, NZ)
        return remote(mine, mine, self.zs.at[s, i], self.zr.at[s, i], p.b, 2 * to + p.c)

    def zsend(self, s):
        for i in (2, 1, 3):
            self.zcopy(s, i).start()

    def xcopy(self, s, i, d):
        p = self.p
        z = lax.rem(p.z + NZ - i, NZ)
        b, row, n, to = ((p.b, 0, 64, p.xn), (p.b, 0, 64, p.yn), (p.xn, 0, 32, p.yn), (p.yn, 32, 32, p.xn))[d]
        part = self.part(s, z, b, row, n)
        at = 3 * d + i - 1
        return remote(part, part, self.xs.at[s, at], self.xr.at[s, at], to, p.f)

    def relay(self, s):
        for i in range(1, NZ):
            self.zcopy(s, i).wait_recv()
            self.xcopy(s, i, 0).start()
            self.xcopy(s, i, 1).start()

    def turn(self, s):
        for i in range(1, NZ):
            self.xcopy(s, i, 0).wait_recv()
            self.xcopy(s, i, 2).start()
            self.xcopy(s, i, 1).wait_recv()
            self.xcopy(s, i, 3).start()

    def dcopy(self, s):
        p = self.p
        mine = self.W.at[s // 3, lax.rem(s, 3), :, p.c]
        return remote(mine, mine, self.ds.at[s], self.dr.at[s], p.b, p.sib)

    def across(self, s):
        for i in range(1, NZ):
            self.xcopy(s, i, 2).wait_recv()
            self.xcopy(s, i, 3).wait_recv()
        self.dcopy(s).start()

    def arrive(self, s):
        self.dcopy(s).wait_recv()

    def drain(self, s):
        for i in range(1, NZ):
            self.zcopy(s, i).wait_send()
            for d in range(4):
                self.xcopy(s, i, d).wait_send()
        self.dcopy(s).wait_send()


class Scatter:
    def __init__(self, p, W, RX, RZ, G, Q, GF, sems):
        self.p, self.W, self.RX, self.RZ, self.G, self.Q, self.GF = p, W, RX, RZ, G, Q, GF
        (self.bs, self.br, self.cs, self.cr, self.es, self.er) = sems

    def held(self, e, q, half):
        return self.G.at[e % 3, :, pl.ds(pl.multiple_of(q * 64 + 32 * half, 32), 32), :]

    def room(self, e, i):
        at = pl.ds(128 * (i % 2), 128)
        if e < 3:
            ref = self.RX.at[e, i // 2, at, :]
        else:
            ref = self.W.at[1, e % 3, i // 4, (i // 2) % 2, at, :]
        return ref

    def hop(self, e, i):
        p = self.p
        q, half, to = (
            (p.dn, 0, p.xn), (p.dn, 1, p.yn), (p.xn, 0, p.xn), (p.yn, 1, p.yn), (p.yn, 0, p.yn), (p.xn, 1, p.xn),
        )[i]
        return remote(
            self.held(e, q, half), self.room(e, i).reshape(NZ, 32, C), self.bs.at[e, i], self.br.at[e, i], to, p.f
        )

    def begin(self, e):
        for i in range(4):
            self.hop(e, i).start()

    def mid(self, e):
        p = self.p
        for i, q, half in ((0, p.yn, 0), (1, p.xn, 1)):
            self.hop(e, i).wait_recv()
            mine = self.held(e, q, half)
            got = self.room(e, i)[...].reshape(NZ, 32, C).astype(f32)
            mine[...] = (mine[...].astype(f32) + got).astype(bf16)
            self.hop(e, 4 + i).start()

    def out3(self, e, i):
        p = self.p
        to = lax.rem(p.z + i, NZ)
        return remote(
            self.Q.at[e % 3, to], self.RZ.at[e, i - 1], self.cs.at[e, i - 1], self.cr.at[e, i - 1], p.b, 2 * to + p.c
        )

    def out4(self, e, d):
        p = self.p
        to = (p.xn, p.yn, p.dn)[d]
        mine = self.GF.at[1 - e // 3, e % 3, pl.ds(pl.multiple_of(p.b * 64, 64), 64), :]
        return remote(mine, mine, self.es.at[e, d], self.er.at[e, d], to, p.f)

    def along(self, e):
        p = self.p
        for i in range(2, 6):
            self.hop(e, i).wait_recv()
        for half, ways in ((0, (2, 4)), (1, (3, 5))):
            acc = self.held(e, p.b, half)[...].astype(f32)
            for i in ways:
                acc = acc + self.room(e, i)[...].reshape(NZ, 32, C).astype(f32)
            self.Q[e % 3, :, 32 * half : 32 * half + 32, :] = acc.astype(self.Q.dtype)
        for i in (2, 1, 3):
            self.out3(e, i).start()

    def final(self, e, lost):
        p = self.p
        for i in range(1, NZ):
            self.out3(e, i).wait_recv()
        acc = self.Q[e % 3, p.z].astype(f32)
        for i in range(1, NZ):
            acc = acc + self.RZ[e, i - 1].astype(f32)
        acc = acc + lost
        low = acc.astype(bf16)
        self.GF[1 - e // 3, e % 3, pl.ds(pl.multiple_of(p.b * 64, 64), 64), :] = low
        for d in (2, 0, 1):
            self.out4(e, d).start()
        low = low.astype(f32)
        return jnp.sum((low * low).reshape(8, 8, C), axis=0)

    def clear(self, e):
        for i in range(6):
            self.hop(e, i).wait_send()

    def clear_line(self, e):
        for i in range(1, NZ):
            self.out3(e, i).wait_send()

    def end(self, e):
        for d in range(3):
            self.out4(e, d).wait()


class RowSum:
    def __init__(self, p, ref, ssem, rsem):
        self.p, self.ref, self.ssem, self.rsem = p, ref, ssem, rsem

    def eight(self, t, row, i):
        return self.ref.at[t, pl.ds(pl.multiple_of(row + 8 * i, 8), 8), :]

    def hop(self, t, n, src, dst, b, f):
        return remote(src, dst, self.ssem.at[t, n], self.rsem.at[t, n], b, f)

    def three(self, t, n, row):
        rest = self.ref.at[t, row : row + 24, :]
        return self.hop(t, n, rest, rest, self.p.b, self.p.sib)

    def give(self, t):
        p = self.p
        return self.hop(t, 0, self.eight(t, 0, 1 - p.c), self.eight(t, 16, 1 - p.c), p.b, p.sib)

    def along(self, t):
        p = self.p
        self.give(t).wait_recv()
        mine = self.eight(t, 32, p.b)
        mine[...] = self.eight(t, 0, p.c)[...] + self.eight(t, 16, p.c)[...]
        for to in (p.dn, p.xn, p.yn):
            self.hop(t, 1, mine, mine, to, p.f).start()

    def square(self, t):
        p = self.p
        self.three(t, 1, 32).wait_recv()
        mine = self.eight(t, 64, p.z)
        mine[...] = jnp.sum(self.ref[t, 32:64, :].reshape(NB, 8, C), axis=0)
        for i in (2, 1, 3):
            self.hop(t, 2, mine, mine, p.b, 2 * lax.rem(p.z + i, NZ) + p.c).start()

    def back(self, t):
        p = self.p
        mine = self.eight(t, 96, p.c)
        return self.hop(t, 3, mine, mine, p.b, p.sib)

    def close(self, t):
        self.three(t, 2, 64).wait_recv()
        self.eight(t, 96, self.p.c)[...] = jnp.sum(self.ref[t, 64:96, :].reshape(NZ, 8, C), axis=0)
        self.back(t).start()

    def result(self, t):
        self.back(t).wait_recv()
        return self.ref[t, 96:112, :]

    def drain(self, t):
        self.give(t).wait_send()
        self.three(t, 1, 32).wait_send()
        self.three(t, 2, 64).wait_send()
        self.back(t).wait_send()


def conv_back_rows(S, W, k, r0, M):
    acc = None
    for u in range(3):
        lhs = jnp.concatenate([S[2 - u][pl.ds(r0 + (2 - v) * BLK, M), :] for v in range(3)], axis=1)
        rhs = jnp.concatenate(
            [
                W[k, u, z, c, v * 80 : v * 80 + 80, :]
                for v in range(3)
                for z in range(NZ)
                for c in range(2)
            ],
            axis=0,
        )
        d = jnp.dot(lhs, rhs, preferred_element_type=f32)
        acc = d if acc is None else acc + d
    return acc


def own_rows(p, dyT):
    return jnp.concatenate([dyT[z, p.c] for z in range(NZ)], axis=0)


def sib_rows(dyS):
    return jnp.concatenate([dyS[z] for z in range(NZ)], axis=0)


def first_grad(p, S, dyT, acc):
    def tap(v, carry):
        at = pl.ds(pl.multiple_of(v * BLK, BLK), ROWS)
        acc[pl.ds(pl.multiple_of(v * 320, 320), 320), :] = jnp.dot(
            own_rows(p, dyT), S[0][at, :], preferred_element_type=f32
        )
        return carry

    lax.fori_loop(0, 3, tap, 0)


def filter_grad(p, S, S2, dyT, dyS, DS, mu, G, e, acc):
    u = e % 3
    if u == 0:
        ones = jnp.ones((ROWS, 128), bf16)
        DS[...] = jnp.dot(own_rows(p, dyT), ones, preferred_element_type=f32) + jnp.dot(
            sib_rows(dyS), ones, preferred_element_type=f32
        )

    def tap(v, carry):
        at = pl.ds(pl.multiple_of(v * BLK, BLK), ROWS)
        d = jnp.dot(sib_rows(dyS), S2[u, at, :], preferred_element_type=f32)
        if u == 0:
            d = d + acc[pl.ds(pl.multiple_of(v * 320, 320), 320), :]
        else:
            d = d + jnp.dot(own_rows(p, dyT), S[u][at, :], preferred_element_type=f32)
        d = d - jnp.concatenate([DS[...]] * 5, axis=1) * mu
        for z in range(NZ):
            G[u, z, pl.ds(pl.multiple_of(v * 80, 16), 80), :] = d[80 * z : 80 * z + 80].astype(bf16)
        return carry

    lax.fori_loop(0, 3, tap, 0)


def step_kernel(
    images, labels, partner, valid, sizes, stem_w, bridge_t, conv_w, norm, head, bias,
    GF_o, own_o, stem_o, misc_o,
    GF, W, S, S2, S3, dyT, dyS, DS, inner, block, dfl, RX, RZ, G, Q, slots, sibs, lab, few, gath, gathn, par, mask, AB, stem, dstem, pad, pad32,
    xs_, xr_, ps_, pr_, lbs, lbr, gs, gr, zs, zr, xs, xr, ds, dr, ls,
    bs, br, cs, cr, es, er, ts, tr, us, ur, free, fs, fr, os_,
):
    p = Place()
    ex = Exchange(p, slots, sibs, xs_, xr_, ps_, pr_)
    ga = Gather(p, W, zs, zr, xs, xr, ds, dr)
    sc = Scatter(p, W, RX, RZ, G, Q, GF, (bs, br, cs, cr, es, er))
    rs = RowSum(p, few, fs, fr)
    greet(p)
    SA = [S.at[u] for u in range(3)]
    SB = [S.at[0], S.at[1], S3]
    def load(s):
        at = pl.ds(240 * s, 240)
        return pltpu.make_async_copy(conv_w.reshape(1440, C).at[at], block.at[at], ls.at[s])

    for s in range(6):
        load(s).start()
    pad32[...] = jnp.zeros((32, 128), f32)
    pad32[0:16, 0:80] = bridge_t[...]
    pad32[16:26, 0:80] = head[...]
    gath[p.z, p.c] = pad32[...].astype(bf16)
    gathn[p.z, p.c] = jnp.zeros((8, 128), f32)
    gathn[p.z, p.c, 0:6, 0:80] = norm[...]

    def cast(s):
        load(s).wait()
        k, u = s // 3, s % 3
        for v in range(3):
            t = 9 * k + 3 * u + v
            W[k, u, p.z, p.c, 80 * v : 80 * v + 80, :] = block[80 * t : 80 * t + 80, :].astype(bf16)
        W[k, u, p.z, p.c, 240:256, :] = jnp.zeros((16, C), bf16)

    cast(0)
    met()
    for i in (2, 1, 3):
        to = lax.rem(p.z + i, NZ)
        for n, ref in enumerate((gath, gathn)):
            mine = ref.at[p.z, p.c]
            remote(mine, mine, gs.at[n], gr.at[n], p.b, 2 * to + p.c).start()
    ga.zsend(0)
    for s in range(1, 6):
        cast(s)
        if s < 2:
            ga.zsend(s)
    img = pltpu.roll(images[...].astype(f32), 32, 1)
    lane = iota((IMG, 128), 1)
    for c in range(3):
        for i in range(8):
            a = img[:, 1024 * c + 128 * i : 1024 * c + 128 * i + 128]
            if i == 0:
                a = jnp.where(lane < 32, 0.0, a)
            AB[IMG * i : IMG * i + IMG, 128 * c : 128 * c + 128] = a
    tile_c = jnp.bitwise_and(iota((16, 128), 1), 15) == iota((16, 128), 0)
    wc = lax.dot_general(
        stem_w[...].astype(bf16), tile_c.astype(bf16), CC, preferred_element_type=f32
    )
    fold_r = (jnp.bitwise_and(iota((256, 27), 0), 31) == iota((256, 27), 1)).astype(bf16)
    own_j = iota((256, 128), 0) // 32 == iota((256, 128), 1) // 16
    bd = jnp.dot(fold_r, wc.astype(bf16), preferred_element_type=f32)
    bd = jnp.where(own_j, bd, 0.0).astype(bf16)
    l, r = iota((128, 256), 0), iota((128, 256), 1)
    v = jnp.bitwise_and(l, 31) - 4 * (r // 32) + 1

    def hits(c):
        want = 9 * c + 3 * (l // 32) + v
        hit = (l < 96) & (v >= 0) & (v < 3) & (want == jnp.bitwise_and(r, 31))
        return hit.astype(f32)

    acc = None
    for c in range(3):
        t = jnp.dot(hits(c).astype(bf16), bd, preferred_element_type=f32).astype(bf16)
        d = jnp.dot(
            AB[:, 128 * c : 128 * c + 128].astype(bf16), t, preferred_element_type=f32
        )
        acc = d if acc is None else acc + d
    stem[...] = acc.astype(bf16).astype(f32)
    ok = column(valid[...].astype(f32), IMG)
    q = p.f * IMG + iota((IMG, 1), 0)
    member = jnp.zeros((IMG, 1), jnp.int32)
    end = jnp.int32(0)
    for g in range(8):
        end = end + sizes[p.b, g]
        member = member + (q >= end).astype(jnp.int32)
    member = jnp.minimum(member, 7)
    size = jnp.zeros((IMG, 1), f32)
    for g in range(8):
        size = size + jnp.where(member == g, sizes[p.b, g].astype(f32), 0.0)
    weight = ok / size
    mask[...] = jnp.concatenate([jnp.broadcast_to(ok, (IMG, 128))] * 8, axis=0)
    count = 64.0 * jnp.sum(ok)
    own_row = labels[...].astype(f32)
    slot = ex.mine(0)
    slot[5:6, :] = jnp.full((1, 128), count, f32)
    slot[6:7, :] = jnp.concatenate([own_row, jnp.zeros((1, 104), f32)], axis=1)
    slot[7:8, :] = jnp.full((1, 128), jnp.sum(weight), f32)
    edge = jnp.zeros((BLK, C), bf16)
    S3[0:BLK, :] = edge
    S3[9 * BLK : 10 * BLK, :] = edge
    for u in range(3):
        S[u, 0:BLK, :] = edge
        S[u, 9 * BLK : 10 * BLK, :] = edge
        for z in range(NZ):
            G[u, z, 240:256, :] = jnp.zeros((16, C), bf16)
    pairs = []
    for n, ref in enumerate((gath, gathn)):
        rest = ref.at[0 : NZ - 1, 0]
        remote(rest, rest, gs.at[n], gr.at[n], p.b, p.sib).wait()
        side = ref.at[:, p.c]
        pairs.append(remote(side, side, gs.at[2 + n], gr.at[2 + n], p.b, p.sib))
        pairs[n].start()
    for pair in pairs:
        pair.wait()
    lane = iota((40, 128), 1)
    for k in range(5):
        acc = jnp.zeros((40, 128), f32)
        for f in range(NF):
            lo, hi = max(80 * f, 128 * k), min(80 * f + 80, 128 * k + 128)
            if lo < hi:
                low = gath[f // 2, f % 2].astype(f32)
                all_rows = jnp.concatenate([low[0:16], gathn[f // 2, f % 2], low[16:32]], axis=0)
                turned = pltpu.roll(all_rows, (80 * f - 128 * k) % 128, 1)
                acc = jnp.where((lane >= lo - 128 * k) & (lane < hi - 128 * k), turned, acc)
        par[:, 128 * k : 128 * k + 128] = acc
    bridge8 = jnp.concatenate([par[0:16, :].astype(bf16)] * 8, axis=0)

    def rows(j):
        return pl.ds(pl.multiple_of(j * BLK, BLK), BLK)

    def base_rows(j):
        pick = iota((BLK, 128), 1) // 16 == j
        x = jnp.where(pick, stem[...], 0.0).astype(bf16)
        return jnp.dot(x, bridge8, preferred_element_type=f32)

    def base_block(j, carry):
        inner[rows(j), :] = base_rows(j)
        return carry

    lax.fori_loop(0, 8, base_block, 0)
    local_stats(inner, mask, count, ex.mine(0))
    ex.send(0)
    ga.zsend(2)
    ga.relay(0)
    ga.turn(0)
    ga.relay(1)

    def inner_rows(j):
        return inner[rows(j), :]

    def block_rows(j):
        return block[rows(j), :]

    def dfl_rows(j):
        return dfl[rows(j), :]

    def gain(k):
        return par[16 + 2 * k : 17 + 2 * k, :]

    def shift(k):
        return par[17 + 2 * k : 18 + 2 * k, :]

    def normed(src, stats, k, S):
        mean, scale = stats[:2]

        def one(j, acc):
            hat = (src(j) - mean) * scale
            out = jnp.maximum(gain(k) * hat + shift(k), 0.0)
            spread_rows(S, j, out)
            m = jnp.concatenate([mask[...]] * 5, axis=1)
            return acc + jnp.sum((out * m).reshape(BLK // 8, 8, C), axis=0)

        acc = lax.fori_loop(0, 8, one, jnp.zeros((8, C), f32))
        return jnp.sum(acc, axis=0, keepdims=True)

    stats0 = joint_stats(ex, 0)
    labs = remote(lab.at[0], lab.at[1], lbs, lbr, p.b, p.sib)
    lab[0] = slots[0, :, 6, :]
    labs.start()
    put_spare(ex.mine(1), normed(inner_rows, stats0, 0, SA))
    for s in range(3, 6):
        ga.zsend(s)

    def conv(k, u, dst, start, acts):
        def one(it, carry):
            r0 = pl.multiple_of(it * 384, 384)
            at = pl.ds(r0, 384)
            d = conv_part(SB if k else SA, W, k, u, r0, 384)
            dst[at, :] = (dst[at, :] if start is None else start(it)) + d if start != 0 else d
            for when, act in acts.items():
                pl.when(it == when)(act)
            return carry

        lax.fori_loop(0, 4, one, 0)

    def share(u, S=SA):
        return remote(S[u], S2.at[u], ts.at[u], tr.at[u], p.b, p.sib)

    def doing(f, *a):
        return lambda: f(*a)

    ga.relay(2)
    ga.turn(1)
    ga.across(0)
    ga.arrive(0)
    conv(0, 0, inner, 0, {0: doing(ga.turn, 2), 1: doing(ga.relay, 3)})
    ga.across(1)
    ga.across(2)
    ga.arrive(1)
    conv(0, 1, inner, None, {1: doing(ga.relay, 4)})
    ga.arrive(2)
    conv(0, 2, inner, None, {0: doing(ga.turn, 3), 2: doing(ga.relay, 5)})
    ga.turn(4)
    local_stats(inner, mask, count, ex.mine(1))
    ex.send(1)
    ga.across(3)
    ga.turn(5)
    stats1 = joint_stats(ex, 1)
    put_spare(ex.mine(2), normed(inner_rows, stats1, 1, SB))
    ga.arrive(3)
    conv(1, 0, block, lambda it: jnp.concatenate([base_rows(2 * it), base_rows(2 * it + 1)], axis=0),
         {1: doing(ga.across, 4), 3: doing(ga.across, 5)})
    ga.arrive(4)
    for u in range(3):
        share(u, SB).start()
    conv(1, 1, block, None, {})
    ga.arrive(5)
    conv(1, 2, block, None, {})
    local_stats(block, mask, count, ex.mine(2))
    ex.send(2)
    for s in range(6):
        ga.drain(s)
    lane = iota((IMG, 16), 1)
    label = column(own_row, IMG)
    mate = column(partner[...].astype(f32), IMG)
    home = jnp.floor((mate + 0.5) / 24.0)
    chip = jnp.floor((home + 0.5) / 2.0)
    at_chip = (iota((IMG, NCHIP), 1).astype(f32) == chip).astype(bf16)
    labs.wait()
    own_side = jnp.dot(at_chip, lab[0].astype(bf16), preferred_element_type=f32)
    sib_side = jnp.dot(at_chip, lab[1].astype(bf16), preferred_element_type=f32)
    there = jnp.where(home - 2.0 * chip == p.c.astype(f32), own_side, sib_side)
    spot = iota((IMG, 128), 1).astype(f32) == mate - 24.0 * home
    mate_label = jnp.sum(jnp.where(spot, there, 0.0), axis=1, keepdims=True)
    lane_f = lane.astype(f32)
    target = own_share * (lane_f == label).astype(f32) + (1.0 - own_share) * (
        lane_f == mate_label
    ).astype(f32)
    live = lane < 10
    head16 = par[24:40, :].astype(bf16)
    pad[...] = jnp.zeros((8, 128), f32)
    pad[0:1, 0:10] = bias[...]
    sides = sibs[0, 0] + sibs[0, 1]
    total = jnp.sum(sides[7:8, 0:1])
    valid_count = jnp.sum(sides[5:6, 0:1])
    stats2 = joint_stats(ex, 2)
    mu0, mu1 = stats1[2] / valid_count, stats2[2] / valid_count

    def pool(j, acc):
        hat = (block_rows(j) - stats2[0]) * stats2[1]
        out = jnp.maximum(gain(2) * hat + shift(2), 0.0)
        return acc + jnp.sum(out.reshape(8, IMG, C), axis=0)

    pooled = lax.fori_loop(0, 8, pool, jnp.zeros((IMG, C), f32)) / 64.0
    pooled = pooled.astype(bf16)
    logits = lax.dot_general(pooled, head16, AC, preferred_element_type=f32) + pad[0:1, 0:16]
    top = jnp.max(jnp.where(live, logits, -3e38), axis=1, keepdims=True)
    moved = jnp.where(live, logits - top, 0.0)
    size_sum = jnp.sum(jnp.where(live, jnp.exp(moved), 0.0), axis=1, keepdims=True)
    logp = moved - jnp.log(size_sum)
    loss_part = -jnp.sum(
        weight * jnp.sum(jnp.where(live, target * logp, 0.0), axis=1, keepdims=True)
    )
    d_logits = jnp.where(live, (jnp.exp(logp) - target) * (weight / total), 0.0).astype(bf16)
    g_bias = jnp.sum(d_logits.astype(f32), axis=0, keepdims=True)
    few[0, 0:16, :] = lax.dot_general(d_logits, pooled, CC, preferred_element_type=f32)
    rs.give(0).start()
    d_pooled = jnp.dot(d_logits, head16, preferred_element_type=f32)
    d_out24 = d_pooled / 64.0

    def zhat(src, j, stats):
        return (src(j) - stats[0]) * stats[1]

    def passed(hat, k, d_out):
        return jnp.where(gain(k) * hat + shift(k) > 0.0, d_out, 0.0)

    def grad_sums(src, stats, k, d_of, e):
        def one(j, acc):
            hat = zhat(src, j, stats)
            got = passed(hat, k, d_of(j))
            return (
                acc[0] + jnp.sum(got.reshape(BLK // 8, 8, C), axis=0),
                acc[1] + jnp.sum((got * hat).reshape(BLK // 8, 8, C), axis=0),
            )

        zero = jnp.zeros((8, C), f32)
        acc = lax.fori_loop(0, 8, one, (zero, zero))
        put_row(ex.mine(e), 0, jnp.sum(acc[0], axis=0, keepdims=True))
        put_row(ex.mine(e), 8, jnp.sum(acc[1], axis=0, keepdims=True))

    def grad_rows(src, stats, k, d_of, sums, j):
        hat = zhat(src, j, stats)
        m = jnp.concatenate([mask[...]] * 5, axis=1)
        got = passed(hat, k, d_of(j))
        return (gain(k) * stats[1]) * (got - m * (sums[0] + hat * sums[1]) / valid_count)

    def head_rows(j):
        return jnp.concatenate([d_out24] * 8, axis=0)

    def turn(src):
        for it in range(4):
            x = src[384 * it : 384 * it + 384, :].T.astype(bf16)
            for f in range(NF):
                dyT[f // 2, f % 2, :, 384 * it : 384 * it + 384] = x[80 * f : 80 * f + 80]

    trade = remote(dyT.at[:, 1 - p.c], dyS, us, ur, p.b, p.sib)

    grad_sums(block_rows, stats2, 2, head_rows, 3)
    slot = ex.mine(3)
    slot[5:6, :] = jnp.full((1, 128), loss_part, f32)
    slot[6:7, :] = jnp.concatenate([g_bias, jnp.zeros((1, 112), f32)], axis=1)
    ex.send(3)
    tot3 = ex.total(3)
    sums2 = wide(tot3[0:5]), wide(tot3[8:13])

    def low_sums(dst, src, stats, k, d_of, sums):
        def one(j, acc):
            d = grad_rows(src, stats, k, d_of, sums, j)
            dst[rows(j), :] = d
            return acc + jnp.sum(d.astype(bf16).astype(f32).reshape(BLK // 8, 8, C), axis=0)

        acc = lax.fori_loop(0, 8, one, jnp.zeros((8, C), f32))
        return jnp.sum(acc, axis=0, keepdims=True)

    def lost(dy_sums, mu):
        at = 64 * p.b + iota((64, C), 0)
        o = at - 80 * ((at >= 80).astype(jnp.int32) + (at >= 160).astype(jnp.int32))
        hit = (iota((64, C), 1) == 80 * p.f + o) & (at < 240)
        return jnp.sum(jnp.where(hit, dy_sums, 0.0), axis=1, keepdims=True) * mu

    put_spare(ex.mine(4), low_sums(block, block_rows, stats2, 2, head_rows, sums2))
    turn(block)
    trade.start()
    first_grad(p, SB, dyT, dfl)
    for u in range(3):
        share(u, SB).wait()
    trade.wait()
    filter_grad(p, SB, S2, dyT, dyS, DS, mu1, G, 0, dfl)
    sc.begin(0)
    filter_grad(p, SB, S2, dyT, dyS, DS, mu1, G, 1, dfl)
    sc.begin(1)
    rs.along(0)
    def spread(src):
        def one(j, carry):
            spread_rows(SA, j, src[rows(j), :])
            return carry

        lax.fori_loop(0, 8, one, 0)

    spread(block)

    def back_conv1(it, carry):
        r0 = pl.multiple_of(it * 384, 384)
        dfl[pl.ds(r0, 384), :] = conv_back_rows(SA, W, 1, r0, 384)

        @pl.when(it == 0)
        def _():
            sc.mid(0)

        @pl.when(it == 2)
        def _():
            sc.mid(1)

        return carry

    lax.fori_loop(0, 4, back_conv1, 0)
    grad_sums(inner_rows, stats1, 1, dfl_rows, 4)
    ex.send(4)
    sc.along(0)
    filter_grad(p, SB, S2, dyT, dyS, DS, mu1, G, 2, None)
    sc.begin(2)
    rs.square(0)
    pl.semaphore_signal(free, inc=1, device_id=(p.b, p.sib), device_id_type=MESH)
    normed(base_rows, stats0, 0, SA)
    sc.along(1)
    tot4 = ex.total(4)
    pl.semaphore_wait(free, 1)
    share(0).start()
    sums1 = wide(tot4[0:5]), wide(tot4[8:13])
    lost1 = lost(spare(tot4), mu1)
    put_spare(ex.mine(5), low_sums(dfl, inner_rows, stats1, 1, dfl_rows, sums1))
    turn(dfl)
    trade.start()
    for u in range(1, 3):
        share(u).start()
    first_grad(p, SA, dyT, inner)
    sc.mid(2)
    squares = sc.final(0, lost1)
    sc.clear(0)
    share(0).wait()
    trade.wait()
    filter_grad(p, SA, S2, dyT, dyS, DS, mu0, G, 3, inner)
    sc.begin(3)
    rs.close(0)
    sc.clear(1)
    share(1).wait()
    filter_grad(p, SA, S2, dyT, dyS, DS, mu0, G, 4, inner)
    sc.begin(4)
    sc.along(2)
    sc.clear(2)
    share(2).wait()
    filter_grad(p, SA, S2, dyT, dyS, DS, mu0, G, 5, inner)
    sc.mid(3)
    sc.begin(5)
    spread(dfl)

    def back_conv0(it, carry):
        r0 = pl.multiple_of(it * 384, 384)
        inner[pl.ds(r0, 384), :] = conv_back_rows(SA, W, 0, r0, 384)

        @pl.when(it == 1)
        def _():
            sc.mid(4)

        @pl.when(it == 2)
        def _():
            sc.clear_line(0)
            sc.along(3)

        return carry

    lax.fori_loop(0, 4, back_conv0, 0)

    sc.mid(5)
    grad_sums(base_rows, stats0, 0, inner_rows, 5)
    ex.send(5)
    squares = squares + sc.final(1, lost1) + sc.final(2, lost1)
    sc.clear_line(1)
    sc.along(4)
    tot5 = ex.total(5)
    lost0 = lost(spare(tot5), mu0)
    squares = squares + sc.final(3, lost0)
    sc.clear_line(2)
    sc.along(5)
    sums0 = wide(tot5[0:5]), wide(tot5[8:13])
    grid16 = dfl.at[512:640]
    grid16[...] = jnp.zeros((128, C), f32)
    dstem[...] = jnp.zeros((BLK, 128), f32)

    def back0(i, carry):
        total_g, total_s = None, None
        for h in range(4):
            j = 4 * i + h
            d = block[rows(j), :] + grad_rows(base_rows, stats0, 0, inner_rows, sums0, j)
            d = d.astype(bf16)
            pick = iota((BLK, 128), 1) // 16 == j
            x = jnp.where(pick, stem[...], 0.0).astype(bf16)
            g = lax.dot_general(x, d, CC, preferred_element_type=f32)
            y = jnp.where(pick, lax.dot_general(d, bridge8, AC, preferred_element_type=f32), 0.0)
            total_g = g if total_g is None else total_g + g
            total_s = y if total_s is None else total_s + y
        grid16[...] += total_g
        dstem[...] += total_s
        return carry

    lax.fori_loop(0, 2, back0, 0)
    acc = grid16[0:16, :]
    for j in range(1, 8):
        acc = acc + grid16[16 * j : 16 * j + 16, :]
    few[1, 0:16, :] = acc
    rs.give(1).start()
    low = dstem[...].astype(bf16)
    high = lax.Precision.HIGHEST
    acc = None
    for c in range(3):
        t = lax.dot_general(
            AB[:, 128 * c : 128 * c + 128].astype(bf16), low, CC, preferred_element_type=f32
        )
        d = lax.dot_general(hits(c), t, CC, precision=high, preferred_element_type=f32)
        acc = d if acc is None else acc + d
    acc = jnp.where(own_j, acc, 0.0)
    fold = (jnp.bitwise_and(iota((256, 128), 0), 31) == iota((256, 128), 1)).astype(f32)
    acc = lax.dot_general(acc, fold, CC, precision=high, preferred_element_type=f32)
    slots[6, p.chip] = jnp.dot(
        tile_c.astype(f32), acc, precision=high, preferred_element_type=f32
    )
    ex.send(6)
    rs.along(1)
    squares = squares + sc.final(4, lost0)
    rs.square(1)
    g_stem = ex.total(6)
    squares = squares + sc.final(5, lost0)
    slots[7, p.chip] = jnp.full((16, 128), jnp.sum(squares), f32)
    ex.send(7)

    def leave(e):
        at = 1 - e // 3, e % 3
        return pltpu.make_async_copy(GF.at[at], GF_o.at[at], os_.at[e])

    for e in range(4):
        sc.end(e)
        leave(e).start()
    rs.close(1)
    both = jnp.concatenate([rs.result(1), rs.result(0)], axis=0)
    bias_all = tot3[6:7, :]
    stem_o[...] = g_stem
    ng = [row for sums in (sums0, sums1, sums2) for row in (sums[1], sums[0])]
    ng = jnp.concatenate(ng + [jnp.zeros((2, C), f32)], axis=0)
    every = jnp.concatenate([both, ng], axis=0)
    pick = (iota((C, 128), 0) == 80 * p.f + iota((C, 128), 1)) & (iota((C, 128), 1) < 80)
    own_o[...] = jnp.dot(every, pick.astype(f32), precision=high, preferred_element_type=f32)
    other = jnp.sum(every * every) + jnp.sum(g_stem * g_stem) + jnp.sum(bias_all * bias_all)
    conv_sq = ex.total(7)[0:1, :]
    misc_o[...] = jnp.zeros((8, 128), f32)
    misc_o[0:1, :] = jnp.sqrt(conv_sq + other)
    misc_o[1:2, :] = tot3[5:6, :] / total
    misc_o[2:3, :] = bias_all
    for e in range(4, 6):
        sc.end(e)
        leave(e).start()
    for e in range(3, 6):
        sc.clear(e)
        sc.clear_line(e)
    for e in range(8):
        ex.drain(e)
    rs.drain(0)
    rs.drain(1)
    for e in range(6):
        leave(e).wait()


def step_call(images, labels, partner, valid, sizes, stem_w, bridge_t, conv_w, norm, head, bias):
    V, A, SM = pltpu.VMEM, pl.ANY, pltpu.SMEM
    spec = lambda m: pl.BlockSpec(memory_space=m)
    D = pltpu.SemaphoreType.DMA
    sh = jax.ShapeDtypeStruct
    return pl.pallas_call(
        step_kernel,
        out_shape=(
            sh((2, 3, 256, C), bf16), sh((40, 128), f32), sh((16, 128), f32), sh((8, 128), f32),
        ),
        in_specs=[
            spec(V), spec(V), spec(V), spec(V), spec(SM), spec(V), spec(V), spec(A), spec(V), spec(V), spec(V),
        ],
        out_specs=(spec(A),) + (spec(V),) * 3,
        scratch_shapes=[
            V((2, 3, 256, C), bf16), V((2, 3, NZ, 2, 256, C), bf16), V((3, 10 * BLK, C), bf16), V((3, 10 * BLK, C), bf16), V((10 * BLK, C), bf16),
            V((NZ, 2, 80, ROWS), bf16), V((NZ, 80, ROWS), bf16), V((NZ * 80, 128), f32),
            V((ROWS, C), f32), V((ROWS, C), f32), V((ROWS, C), f32),
            V((3, 3, 256, C), bf16), V((6, 3, 64, C), LINE), V((3, NZ, 256, C), bf16), V((3, NZ, 64, C), LINE),
            V((8, NCHIP, 16, 128), f32), V((8, 2, 16, 128), f32), V((2, NCHIP, 128), f32), V((2, 112, C), f32), V((NZ, 2, 32, 128), bf16), V((NZ, 2, 8, 128), f32), V((40, C), f32),
            V((BLK, 128), f32), V((BLK, 384), f32), V((BLK, 128), f32), V((BLK, 128), f32), V((8, 128), f32), V((32, 128), f32),
            D((8,)), D((8,)), D((8,)), D((8,)), D, D, D((4,)), D((4,)), D((6, 4)), D((6, 4)), D((6, 12)), D((6, 12)), D((6,)), D((6,)), D((6,)),
            D((6, 6)), D((6, 6)), D((6, 3)), D((6, 3)), D((6, 3)), D((6, 3)), D((3,)), D((3,)), D, D,
            pltpu.SemaphoreType.REGULAR, D((2, 4)), D((2, 4)), D((6,)),
        ],
        compiler_params=pltpu.CompilerParams(
            collective_id=0, has_side_effects=True, vmem_limit_bytes=63 << 20
        ),
    )(images, labels, partner, valid, sizes, stem_w, bridge_t, conv_w, norm, head, bias)


def adam_rule(g, w, m, v, rate, shrink, factor):
    clipped = g * factor
    m = beta_one * m + (1.0 - beta_one) * clipped
    v = beta_two * v + (1.0 - beta_two) * clipped * clipped
    ahead = m / (1.0 - beta_one**STEP)
    behind = v / (1.0 - beta_two**STEP)
    return w - rate * (ahead / (jnp.sqrt(behind) + adam_eps) + shrink * w), m, v


def adam_kernel(G, misc, own, stem_g, *refs):
    ins, outs, (norm_o, loss_o, held, GV, lsem, osem, gsem) = refs[:18], refs[18:36], refs[36:]
    norm_o[...] = misc[0:1, 0:1]
    loss_o[...] = misc[1:2, 0:1]
    factor = clip_norm / jnp.maximum(misc[0:1, :], clip_norm)
    wide_factor = jnp.concatenate([factor] * 5, axis=1)

    def load(s, i):
        return pltpu.make_async_copy(ins[i].at[s // 3, s % 3], held.at[i, s], lsem.at[i, s])

    def store(s, i):
        return pltpu.make_async_copy(held.at[i, s], outs[i].at[s // 3, s % 3], osem.at[i, s])

    def grad(s):
        return pltpu.make_async_copy(G.at[s // 3, s % 3], GV.at[s], gsem.at[s])

    for s in range(6):
        grad(s).start()
        for i in range(3):
            load(s, i).start()

    def write(i, g, rate, shrink, f):
        w, m, v = (r[...] for r in ins[3 * i : 3 * i + 3])
        for o, x in zip(outs[3 * i : 3 * i + 3], adam_rule(g, w, m, v, rate, shrink, f)):
            o[...] = x

    write(1, stem_g[:, 0:27], 0.5, 0.05, factor[:, 0:27])
    write(2, own[0:16, 0:80], 0.6, 0.05, factor[:, 0:80])
    write(3, own[32:38, 0:80], 0.5, 0.0, factor[:, 0:80])
    write(4, own[16:26, 0:80], 0.1, 0.05, factor[:, 0:80])
    write(5, misc[2:3, 0:10], 0.5, 0.0, factor[:, 0:10])
    for s in range(6):
        for i in range(3):
            load(s, i).wait()
        grad(s).wait()

        def part(j, carry):
            at = pl.ds(pl.multiple_of(j * 48, 16), 48)
            new = adam_rule(
                GV[s, at, :].astype(f32), held[0, s, at, :], held[1, s, at, :], held[2, s, at, :],
                0.033, 0.05, wide_factor,
            )
            for i in range(3):
                held[i, s, at, :] = new[i]
            return carry

        lax.fori_loop(0, 5, part, 0)
        for i in range(3):
            store(s, i).start()
    for s in range(6):
        for i in range(3):
            store(s, i).wait()


def adam_call(G, misc, own, stem_g, *state):
    V, A, D = pltpu.VMEM, pl.ANY, pltpu.SemaphoreType.DMA
    spec = lambda m: pl.BlockSpec(memory_space=m)
    return pl.pallas_call(
        adam_kernel,
        out_shape=tuple(jax.ShapeDtypeStruct(s, f32) for s in [x.shape for x in state] + [(1, 1)] * 2),
        in_specs=[spec(A)] + [spec(V)] * 3 + [spec(A)] * 3 + [spec(V)] * 15,
        out_specs=tuple([spec(A)] * 3 + [spec(V)] * 17),
        scratch_shapes=[V((3, 6, 240, C), f32), V((6, 256, C), bf16), D((3, 6)), D((3, 6)), D((6,))],
        compiler_params=pltpu.CompilerParams(vmem_limit_bytes=62 << 20),
    )(G, misc, own, stem_g, *state)


def make_patches(images):
    number = images.shape[0]
    grid = images.reshape(number, 3, 32, 32)
    padded = jnp.pad(grid, ((0, 0), (0, 0), (1, 1), (1, 1)))
    pieces = [
        padded[:, :, row_off : row_off + 29 : 4, col_off : col_off + 29 : 4]
        for row_off in range(3)
        for col_off in range(3)
    ]
    stacked = jnp.stack(pieces, axis=2)
    return jnp.transpose(stacked, (1, 2, 0, 3, 4)).reshape(27, number * 64)


def shifted(feature_field):
    width, rows = feature_field.shape
    grid = feature_field.reshape(width, rows // 64, 8, 8)
    padded = jnp.pad(grid, ((0, 0), (0, 0), (1, 1), (1, 1)))
    pieces = [
        padded[:, :, row_off : row_off + 8, col_off : col_off + 8]
        for row_off in range(3)
        for col_off in range(3)
    ]
    return jnp.stack(pieces, axis=0).reshape(9 * width, rows)


def unshifted(parts, width):
    rows = parts.shape[1]
    grid = parts.reshape(9, width, rows // 64, 8, 8)
    summed = jnp.zeros((width, rows // 64, 10, 10), jnp.float32)
    for row_off in range(3):
        for col_off in range(3):
            summed = summed + jnp.pad(
                grid[3 * row_off + col_off],
                ((0, 0), (0, 0), (row_off, 2 - row_off), (col_off, 2 - col_off)),
            )
    return summed[:, :, 1:9, 1:9].reshape(width, rows)


def image_weights(valid_mask, group_sizes):
    shards, groups = group_sizes.shape
    capacity = valid_mask.shape[0] // shards
    group_ends = jnp.cumsum(group_sizes, axis=1)
    slot_index = jnp.arange(capacity, dtype=jnp.int32)
    member = jnp.sum(
        (slot_index[None, :, None] >= group_ends[:, None, :]).astype(jnp.int32), axis=2
    )
    member = jnp.minimum(member, groups - 1)
    chosen = (member[:, :, None] == jnp.arange(groups, dtype=jnp.int32)[None, None, :]).astype(
        jnp.float32
    )
    sizes_each = jnp.sum(chosen * group_sizes[:, None, :].astype(jnp.float32), axis=2)
    return valid_mask.astype(jnp.float32) / sizes_each.reshape(-1)


def norm_forward(feature_field, norm_gain, norm_shift, row_validity_mask, valid_count):
    batch_mean = (
        lax.psum(jnp.sum(feature_field * row_validity_mask, axis=1), ("batch", "filt"))
        / valid_count
    )
    centered_input = feature_field - batch_mean[:, None]
    batch_variance = (
        lax.psum(
            jnp.sum(centered_input * centered_input * row_validity_mask, axis=1), ("batch", "filt")
        )
        / valid_count
    )
    inverse_scale = lax.rsqrt(batch_variance + norm_epsilon)
    normalized_input = (feature_field - batch_mean[:, None]) * inverse_scale[:, None]
    norm_output = jnp.maximum(norm_gain[:, None] * normalized_input + norm_shift[:, None], 0.0)
    return (norm_output, normalized_input, inverse_scale)


def masked_norm_backward(
    output_gradient,
    norm_output,
    normalized_input,
    inverse_scale,
    norm_gain,
    row_validity_mask,
    valid_count,
):
    passed_rows = jnp.where(norm_output > 0.0, output_gradient, 0.0)
    shift_gradient, gain_gradient = lax.psum(
        (jnp.sum(passed_rows, axis=1), jnp.sum(passed_rows * normalized_input, axis=1)),
        ("batch", "filt"),
    )
    input_gradient = (
        passed_rows
        - row_validity_mask[None, :]
        * (shift_gradient[:, None] + normalized_input * gain_gradient[:, None])
        / valid_count
    )
    return ((norm_gain * inverse_scale)[:, None] * input_gradient, gain_gradient, shift_gradient)


def conv_forward(feature_field, weight_shard):
    stacked = shifted(feature_field)
    low_shard = weight_shard.astype(jnp.bfloat16)
    piece = lax.all_gather(low_shard, "filt", axis=0, tiled=True)
    norm_output = jnp.dot(
        piece.reshape(piece.shape[0], -1), stacked, preferred_element_type=jnp.float32
    )
    return (norm_output, None)


def conv_backward(feature_field, weight_shard, output_gradient):
    width = feature_field.shape[0]
    stacked = shifted(feature_field)
    rows_grad = output_gradient
    term = lax.dot_general(
        rows_grad, stacked, (((1,), (1,)), ((), ())), preferred_element_type=jnp.float32
    )
    weight_grad = lax.psum_scatter(
        term.reshape(lax.axis_size("filt") * weight_shard.shape[0], 9, width),
        "filt",
        scatter_dimension=0,
        tiled=True,
    )
    piece = lax.all_gather(weight_shard.astype(jnp.bfloat16), "filt", axis=0, tiled=True)
    rows_grad = output_gradient
    back = lax.dot_general(
        piece.reshape(piece.shape[0], -1),
        rows_grad,
        (((0,), (0,)), ((), ())),
        preferred_element_type=jnp.float32,
    )
    return (unshifted(back, width), weight_grad)


def adam_step(weight, output_gradient, first, second, rate, shrink, factor):
    clipped = output_gradient * factor
    first = beta_one * first + (1.0 - beta_one) * clipped
    second = beta_two * second + (1.0 - beta_two) * clipped * clipped
    ahead = first / (1.0 - beta_one**STEP)
    behind = second / (1.0 - beta_two**STEP)
    return (
        weight - rate * (ahead / (jnp.sqrt(behind) + adam_eps) + shrink * weight),
        first,
        second,
    )


def body(
    images,
    labels,
    partner,
    valid_mask,
    group_sizes,
    stem_weight,
    bridge_weight,
    conv_weight,
    norm_params,
    head_weight,
    head_bias,
    stem_first,
    stem_second,
    bridge_first,
    bridge_second,
    conv_first,
    conv_second,
    norm_first,
    norm_second,
    head_first,
    head_second,
    bias_first,
    bias_second,
):
    width = bridge_weight.shape[0]
    bridge_all, norm_all, head_all = (
        lax.all_gather(bridge_weight, "filt", axis=0, tiled=True),
        lax.all_gather(norm_params, "filt", axis=1, tiled=True),
        lax.all_gather(head_weight, "filt", axis=1, tiled=True),
    )
    labels_all, valid_all = (
        lax.all_gather(labels, ("batch", "filt"), axis=0, tiled=True),
        lax.all_gather(valid_mask, ("batch", "filt"), axis=0, tiled=True),
    )
    weight_all = image_weights(valid_all, group_sizes)
    total = jnp.sum(weight_all)
    valid_count = 64.0 * jnp.sum(valid_all.astype(jnp.float32))
    local = images.shape[0]
    image_weight = lax.dynamic_slice_in_dim(
        weight_all, lax.axis_index(("batch", "filt")) * local, local
    )
    row_validity_mask = jnp.repeat(valid_mask.astype(jnp.float32), 64)
    patch = make_patches(images)
    stem = jnp.dot(
        stem_weight.astype(jnp.bfloat16), patch, preferred_element_type=jnp.float32
    ).astype(jnp.bfloat16)
    base = jnp.dot(bridge_all.astype(jnp.bfloat16), stem, preferred_element_type=jnp.float32)
    first, first_hat, first_scale = norm_forward(
        base, norm_all[0], norm_all[1], row_validity_mask, valid_count
    )
    first_low = first.astype(jnp.bfloat16)
    inner, kept_zero = conv_forward(first_low, conv_weight[0])
    second, second_hat, second_scale = norm_forward(
        inner, norm_all[2], norm_all[3], row_validity_mask, valid_count
    )
    second_low = second.astype(jnp.bfloat16)
    branch, kept_one = conv_forward(second_low, conv_weight[1])
    final, final_hat, final_scale = norm_forward(
        base + branch, norm_all[4], norm_all[5], row_validity_mask, valid_count
    )
    pooled = jnp.mean(final.reshape(final.shape[0], local, 64), axis=2).astype(jnp.bfloat16)
    logits = (
        jnp.dot(head_all.astype(jnp.bfloat16), pooled, preferred_element_type=jnp.float32)
        + head_bias[:, None]
    )
    moved = logits - jnp.max(logits, axis=0, keepdims=True)
    logp = moved - jnp.log(jnp.sum(jnp.exp(moved), axis=0, keepdims=True))
    classes = jnp.arange(logits.shape[0], dtype=jnp.int32)
    partner_labels = jnp.take(labels_all, partner)
    target = own_share * (labels[None, :] == classes[:, None]).astype(jnp.float32) + (
        1.0 - own_share
    ) * (partner_labels[None, :] == classes[:, None]).astype(jnp.float32)
    loss_part = -jnp.sum(image_weight * jnp.sum(target * logp, axis=0))
    d_logits = ((jnp.exp(logp) - target) * (image_weight / total)[None, :]).astype(jnp.bfloat16)
    bias_grad = jnp.sum(d_logits.astype(jnp.float32), axis=1)
    head_grad = lax.dot_general(
        d_logits, pooled, (((1,), (1,)), ((), ())), preferred_element_type=jnp.float32
    )
    d_pooled = lax.dot_general(
        head_all.astype(jnp.bfloat16),
        d_logits,
        (((0,), (0,)), ((), ())),
        preferred_element_type=jnp.float32,
    )
    d_final = jnp.repeat(d_pooled / 64.0, 64, axis=1)
    d_block, gain_two, shift_two = masked_norm_backward(
        d_final, final, final_hat, final_scale, norm_all[4], row_validity_mask, valid_count
    )
    d_second, conv_grad_one = conv_backward(
        second_low, conv_weight[1], d_block.astype(jnp.bfloat16)
    )
    d_inner, gain_one, shift_one = masked_norm_backward(
        d_second, second, second_hat, second_scale, norm_all[2], row_validity_mask, valid_count
    )
    d_first, conv_grad_zero = conv_backward(first_low, conv_weight[0], d_inner.astype(jnp.bfloat16))
    d_lower, gain_zero, shift_zero = masked_norm_backward(
        d_first, first, first_hat, first_scale, norm_all[0], row_validity_mask, valid_count
    )
    d_base = (d_block + d_lower).astype(jnp.bfloat16)
    bridge_grad = lax.dot_general(
        d_base, stem, (((1,), (1,)), ((), ())), preferred_element_type=jnp.float32
    )
    d_stem = lax.dot_general(
        bridge_all.astype(jnp.bfloat16),
        d_base,
        (((0,), (0,)), ((), ())),
        preferred_element_type=jnp.float32,
    ).astype(jnp.bfloat16)
    stem_grad = lax.dot_general(
        d_stem, patch, (((1,), (1,)), ((), ())), preferred_element_type=jnp.float32
    )
    bridge_part, head_part = (
        lax.psum_scatter(bridge_grad, "filt", scatter_dimension=0, tiled=True),
        lax.psum_scatter(head_grad, "filt", scatter_dimension=1, tiled=True),
    )
    conv_grad, bridge_sum, head_sum = lax.psum(
        (jnp.stack([conv_grad_zero, conv_grad_one]), bridge_part, head_part), "batch"
    )
    stem_sum, bias_sum, loss_sum = lax.psum((stem_grad, bias_grad, loss_part), ("batch", "filt"))
    norm_full = jnp.stack([gain_zero, shift_zero, gain_one, shift_one, gain_two, shift_two])
    norm_grad = lax.dynamic_slice_in_dim(norm_full, lax.axis_index("filt") * width, width, 1)
    owned_square = (
        jnp.sum(conv_grad * conv_grad)
        + jnp.sum(bridge_sum * bridge_sum)
        + jnp.sum(norm_grad * norm_grad)
        + jnp.sum(head_sum * head_sum)
    )
    squares_all = (
        lax.psum(owned_square, "filt") + jnp.sum(stem_sum * stem_sum) + jnp.sum(bias_sum * bias_sum)
    )
    grad_norm = jnp.sqrt(squares_all)
    factor = clip_norm / jnp.maximum(grad_norm, clip_norm)
    stem_new = adam_step(stem_weight, stem_sum, stem_first, stem_second, 0.5, 0.05, factor)
    bridge_new = adam_step(
        bridge_weight, bridge_sum, bridge_first, bridge_second, 0.6, 0.05, factor
    )
    conv_new = adam_step(conv_weight, conv_grad, conv_first, conv_second, 0.033, 0.05, factor)
    norm_new = adam_step(norm_params, norm_grad, norm_first, norm_second, 0.5, 0.0, factor)
    head_new = adam_step(head_weight, head_sum, head_first, head_second, 0.1, 0.05, factor)
    bias_new = adam_step(head_bias, bias_sum, bias_first, bias_second, 0.5, 0.0, factor)
    return (
        stem_new[0],
        stem_new[1],
        stem_new[2],
        bridge_new[0],
        bridge_new[1],
        bridge_new[2],
        conv_new[0],
        conv_new[1],
        conv_new[2],
        norm_new[0],
        norm_new[1],
        norm_new[2],
        head_new[0],
        head_new[1],
        head_new[2],
        bias_new[0],
        bias_new[1],
        bias_new[2],
        grad_norm,
        loss_sum / total,
    )


def fast_body(
    images, labels, partner, valid_mask, group_sizes, stem_weight, bridge_weight, conv_weight, norm_params,
    head_weight, head_bias, stem_first, stem_second, bridge_first, bridge_second, conv_first, conv_second,
    norm_first, norm_second, head_first, head_second, bias_first, bias_second,
):
    width = bridge_weight.shape[0]
    def rows(x):
        return x.transpose(0, 2, 1, 3).reshape(2, 3, 3 * width, C)

    def back(x):
        return x.reshape(2, 9, width, C).transpose(0, 2, 1, 3)

    G, own, stem_g, misc = step_call(
        images, labels[None], partner[None], valid_mask[None], group_sizes, stem_weight, bridge_weight.T,
        conv_weight.transpose(0, 2, 1, 3), norm_params, head_weight, head_bias[None],
    )
    new = adam_call(
        G, misc, own, stem_g,
        rows(conv_weight), rows(conv_first), rows(conv_second),
        stem_weight, stem_first, stem_second,
        bridge_weight.T, bridge_first.T, bridge_second.T,
        norm_params, norm_first, norm_second,
        head_weight, head_first, head_second,
        head_bias[None], bias_first[None], bias_second[None],
    )
    conv, stem, bridge, norm, head, bias = (new[i : i + 3] for i in range(0, 18, 3))
    return (
        *stem,
        *(x.T for x in bridge),
        *(back(x) for x in conv),
        *norm,
        *head,
        *(x[0] for x in bias),
        new[18].reshape(()),
        new[19].reshape(()),
    )


def solution(mesh):
    in_specs = (
        P(("batch", "filt"), None),
        P(("batch", "filt")),
        P(("batch", "filt")),
        P(("batch", "filt")),
        P(),
        P(),
        P("filt", None),
        P(None, "filt", None, None),
        P(None, "filt"),
        P(None, "filt"),
        P(),
        P(),
        P(),
        P("filt", None),
        P("filt", None),
        P(None, "filt", None, None),
        P(None, "filt", None, None),
        P(None, "filt"),
        P(None, "filt"),
        P(None, "filt"),
        P(None, "filt"),
        P(),
        P(),
    )
    out_specs = (
        P(),
        P(),
        P(),
        P("filt", None),
        P("filt", None),
        P("filt", None),
        P(None, "filt", None, None),
        P(None, "filt", None, None),
        P(None, "filt", None, None),
        P(None, "filt"),
        P(None, "filt"),
        P(None, "filt"),
        P(None, "filt"),
        P(None, "filt"),
        P(None, "filt"),
        P(),
        P(),
        P(),
        P(),
        P(),
    )
    fits = mesh.shape["batch"] == NB and mesh.shape["filt"] == NF
    return jax.shard_map(fast_body if fits else body, mesh=mesh, in_specs=in_specs, out_specs=out_specs, check_vma=False)
```

```python
import jax
import jax.numpy as jnp
from jax import lax
from jax.experimental import pallas as pl
from jax.experimental.pallas import tpu as pltpu
from jax.sharding import PartitionSpec as P

STEP = 8

beta_one = 0.9
beta_two = 0.95
adam_eps = 1e-08
norm_epsilon = 1e-05
clip_norm = 0.01
own_share = 0.7

MESH = pl.DeviceIdType.MESH
bf16 = jnp.bfloat16
f32 = jnp.float32
LINE = bf16
NB, NF, NZ, NDEV, NCHIP = 4, 8, 4, 32, 16
C, IMG, ROWS = 640, 24, 1536
BLK = 8 * IMG
AC = (((1,), (1,)), ((), ()))
CC = (((0,), (0,)), ((), ()))


def iota(shape, dim):
    return lax.broadcasted_iota(jnp.int32, shape, dim)


def wide(row5):
    return jnp.concatenate([row5[k : k + 1, :] for k in range(5)], axis=1)


def column(row, n):
    eye = iota((n, n), 0) == iota((n, n), 1)
    return jnp.sum(jnp.where(eye, jnp.broadcast_to(row, (n, n)), 0.0), axis=1, keepdims=True)


class Place:
    def __init__(self):
        self.b = lax.axis_index("batch")
        self.f = lax.axis_index("filt")
        self.z = self.f // 2
        self.c = lax.rem(self.f, 2)
        self.me = self.b * NF + self.f
        self.chip = self.b * NZ + self.z
        self.xn = self.b + 1 - 2 * lax.rem(self.b, 2)
        self.yn = lax.rem(self.b + 2, NB)
        self.dn = (NB - 1) - self.b
        self.sib = self.f + 1 - 2 * self.c


def remote(src, dst, ssem, rsem, b, f):
    return pltpu.make_async_remote_copy(
        src_ref=src, dst_ref=dst, send_sem=ssem, recv_sem=rsem, device_id=(b, f), device_id_type=MESH
    )


def peers(p):
    for dz in (2, 1, 3, 0):
        for db in (3, 1, 2, 0):
            if dz or db:
                yield lax.rem(p.b + db, NB), lax.rem(p.z + dz, NZ)


def greet(p):
    sem = pltpu.get_barrier_semaphore()
    for b, z in peers(p):
        pl.semaphore_signal(sem, inc=1, device_id=(b, 2 * z + p.c), device_id_type=MESH)
    pl.semaphore_signal(sem, inc=1, device_id=(p.b, p.sib), device_id_type=MESH)


def met():
    pl.semaphore_wait(pltpu.get_barrier_semaphore(), NCHIP)


class Exchange:
    def __init__(self, p, slots, sibs, ssem, rsem, psem, qsem):
        self.p, self.slots, self.sibs = p, slots, sibs
        self.ssem, self.rsem, self.psem, self.qsem = ssem, rsem, psem, qsem

    def rows(self, e):
        return 8 if e == 7 else 16

    def mine(self, e):
        return self.slots.at[e, self.p.chip]

    def send(self, e):
        p = self.p
        mine = self.mine(e).at[0 : self.rows(e)]
        for b, z in peers(p):
            remote(mine, mine, self.ssem.at[e], self.rsem.at[e], b, 2 * z + p.c).start()

    def rest(self, e):
        p = self.p
        rest = self.slots.at[e, 0 : NCHIP - 1, 0 : self.rows(e)]
        return remote(rest, rest, self.ssem.at[e], self.rsem.at[e], p.b, p.sib)

    def across(self, e):
        p = self.p
        return remote(
            self.sibs.at[e, 0], self.sibs.at[e, 1], self.psem.at[e], self.qsem.at[e], p.b, p.sib
        )

    def wait(self, e):
        self.rest(e).wait_recv()

    def swap(self, e, value):
        self.sibs[e, 0] = value
        self.across(e).start()
        self.across(e).wait_recv()
        return self.sibs[e, 1]

    def drain(self, e):
        self.rest(e).wait_send()
        self.across(e).wait_send()

    def total(self, e):
        self.wait(e)
        own = jnp.sum(self.slots[e], axis=0)
        return own + self.swap(e, own)


def put_row(slot, row, value):
    for k in range(5):
        slot[row + k : row + k + 1, :] = value[:, 128 * k : 128 * k + 128]


def put_spare(slot, value):
    for k, row in enumerate((5, 6, 7, 13, 14)):
        slot[row : row + 1, :] = value[:, 128 * k : 128 * k + 128]


def spare(rows):
    return wide(jnp.concatenate([rows[5:8], rows[13:15]], axis=0))


def local_stats(src, mask, count, slot):
    def total(j, acc):
        x = src[pl.ds(pl.multiple_of(j * BLK, BLK), BLK), :]
        m = jnp.concatenate([mask[...]] * 5, axis=1)
        return acc + jnp.sum((x * m).reshape(BLK // 8, 8, C), axis=0)

    acc = lax.fori_loop(0, 8, total, jnp.zeros((8, C), f32))
    own_sum = jnp.sum(acc, axis=0, keepdims=True)
    own_mean = own_sum / jnp.maximum(count, 1.0)

    def squares(j, acc):
        x = src[pl.ds(pl.multiple_of(j * BLK, BLK), BLK), :]
        m = jnp.concatenate([mask[...]] * 5, axis=1)
        d = x - own_mean
        return acc + jnp.sum((d * d * m).reshape(BLK // 8, 8, C), axis=0)

    acc = lax.fori_loop(0, 8, squares, jnp.zeros((8, C), f32))
    put_row(slot, 0, own_sum)
    put_row(slot, 8, jnp.sum(acc, axis=0, keepdims=True))


def joint_stats(ex, e):
    ex.wait(e)
    every = ex.slots[e]
    n = ex.slots[0, :, 5:6, :]
    sums = every[:, 0:5, :]
    n_own, s_own = jnp.sum(n, axis=0), jnp.sum(sums, axis=0)
    m_own = s_own / jnp.maximum(n_own, 1.0)
    off = sums / jnp.maximum(n, 1.0) - m_own[None]
    q_own = jnp.sum(every[:, 8:13, :] + n * off * off, axis=0)
    rest = jnp.sum(every[:, 5:8, :], axis=0)
    more = jnp.sum(every[:, 13:16, :], axis=0)
    got = ex.swap(e, jnp.concatenate([s_own, rest, q_own, more], axis=0))
    n_sib = ex.sibs[0, 1, 5:6, :]
    s_sib, q_sib = got[0:5], got[8:13]
    count = n_own + n_sib
    mean = (s_own + s_sib) / count
    a, b = m_own - mean, s_sib / jnp.maximum(n_sib, 1.0) - mean
    spread = ((q_own + q_sib) + (n_own * a * a + n_sib * b * b)) / count
    return wide(mean), wide(lax.rsqrt(spread + norm_epsilon)), spare(got + jnp.concatenate([s_own, rest, q_own, more], axis=0))


def spread_rows(S, j, x):
    at = pl.ds(pl.multiple_of((j + 1) * BLK, BLK), BLK)
    gap = jnp.zeros((IMG, C), f32)
    S[0][at, :] = jnp.concatenate([gap, x[: BLK - IMG]], axis=0).astype(bf16)
    S[1][at, :] = x.astype(bf16)
    S[2][at, :] = jnp.concatenate([x[IMG:], gap], axis=0).astype(bf16)


def conv_part(S, W, k, u, r0, M):
    lhs = jnp.concatenate([S[u][pl.ds(r0 + v * BLK, M), :] for v in range(3)], axis=1)
    rhs = jnp.concatenate(
        [
            jnp.concatenate(
                [W[k, u, z, c, v * 80 : v * 80 + 80, :] for z in range(NZ) for c in range(2)], axis=0
            )
            for v in range(3)
        ],
        axis=1,
    )
    return lax.dot_general(lhs, rhs, AC, preferred_element_type=f32)


class Gather:
    def __init__(self, p, W, zs, zr, xs, xr, ds, dr):
        self.p, self.W = p, W
        self.zs, self.zr, self.xs, self.xr, self.ds, self.dr = zs, zr, xs, xr, ds, dr

    def part(self, s, z, b, row, n):
        return self.W.at[
            s // 3, lax.rem(s, 3), z, self.p.c, pl.ds(pl.multiple_of(b * 64 + row, 32), n), :
        ]

    def zcopy(self, s, i):
        p = self.p
        mine = self.part(s, p.z, p.b, 0, 64)
        to = lax.rem(p.z + i, NZ)
        return remote(mine, mine, self.zs.at[s, i], self.zr.at[s, i], p.b, 2 * to + p.c)

    def zsend(self, s):
        for i in (2, 1, 3):
            self.zcopy(s, i).start()

    def xcopy(self, s, i, d):
        p = self.p
        z = lax.rem(p.z + NZ - i, NZ)
        b, row, n, to = ((p.b, 0, 64, p.xn), (p.b, 0, 64, p.yn), (p.xn, 0, 32, p.yn), (p.yn, 32, 32, p.xn))[d]
        part = self.part(s, z, b, row, n)
        at = 3 * d + i - 1
        return remote(part, part, self.xs.at[s, at], self.xr.at[s, at], to, p.f)

    def relay(self, s):
        for i in range(1, NZ):
            self.zcopy(s, i).wait_recv()
            self.xcopy(s, i, 0).start()
            self.xcopy(s, i, 1).start()

    def turn(self, s):
        for i in range(1, NZ):
            self.xcopy(s, i, 0).wait_recv()
            self.xcopy(s, i, 2).start()
            self.xcopy(s, i, 1).wait_recv()
            self.xcopy(s, i, 3).start()

    def dcopy(self, s):
        p = self.p
        mine = self.W.at[s // 3, lax.rem(s, 3), :, p.c]
        return remote(mine, mine, self.ds.at[s], self.dr.at[s], p.b, p.sib)

    def across(self, s):
        for i in range(1, NZ):
            self.xcopy(s, i, 2).wait_recv()
            self.xcopy(s, i, 3).wait_recv()
        self.dcopy(s).start()

    def arrive(self, s):
        self.dcopy(s).wait_recv()

    def drain(self, s):
        for i in range(1, NZ):
            self.zcopy(s, i).wait_send()
            for d in range(4):
                self.xcopy(s, i, d).wait_send()
        self.dcopy(s).wait_send()


class Scatter:
    def __init__(self, p, W, RX, RZ, G, Q, GF, sems):
        self.p, self.W, self.RX, self.RZ, self.G, self.Q, self.GF = p, W, RX, RZ, G, Q, GF
        (self.bs, self.br, self.cs, self.cr, self.es, self.er) = sems

    def held(self, e, q, half):
        return self.G.at[e % 3, :, pl.ds(pl.multiple_of(q * 64 + 32 * half, 32), 32), :]

    def room(self, e, i):
        at = pl.ds(128 * (i % 2), 128)
        if e < 3:
            ref = self.RX.at[e, i // 2, at, :]
        else:
            ref = self.W.at[1, e % 3, i // 4, (i // 2) % 2, at, :]
        return ref

    def hop(self, e, i):
        p = self.p
        q, half, to = (
            (p.dn, 0, p.xn), (p.dn, 1, p.yn), (p.xn, 0, p.xn), (p.yn, 1, p.yn), (p.yn, 0, p.yn), (p.xn, 1, p.xn),
        )[i]
        return remote(
            self.held(e, q, half), self.room(e, i).reshape(NZ, 32, C), self.bs.at[e, i], self.br.at[e, i], to, p.f
        )

    def begin(self, e):
        for i in range(4):
            self.hop(e, i).start()

    def mid(self, e):
        p = self.p
        for i, q, half in ((0, p.yn, 0), (1, p.xn, 1)):
            self.hop(e, i).wait_recv()
            mine = self.held(e, q, half)
            got = self.room(e, i)[...].reshape(NZ, 32, C).astype(f32)
            mine[...] = (mine[...].astype(f32) + got).astype(bf16)
            self.hop(e, 4 + i).start()

    def out3(self, e, i):
        p = self.p
        to = lax.rem(p.z + i, NZ)
        return remote(
            self.Q.at[e % 3, to], self.RZ.at[e, i - 1], self.cs.at[e, i - 1], self.cr.at[e, i - 1], p.b, 2 * to + p.c
        )

    def out4(self, e, d):
        p = self.p
        to = (p.xn, p.yn, p.dn)[d]
        mine = self.GF.at[1 - e // 3, e % 3, pl.ds(pl.multiple_of(p.b * 64, 64), 64), :]
        return remote(mine, mine, self.es.at[e, d], self.er.at[e, d], to, p.f)

    def along(self, e):
        p = self.p
        for i in range(2, 6):
            self.hop(e, i).wait_recv()
        for half, ways in ((0, (2, 4)), (1, (3, 5))):
            acc = self.held(e, p.b, half)[...].astype(f32)
            for i in ways:
                acc = acc + self.room(e, i)[...].reshape(NZ, 32, C).astype(f32)
            self.Q[e % 3, :, 32 * half : 32 * half + 32, :] = acc.astype(self.Q.dtype)
        for i in (2, 1, 3):
            self.out3(e, i).start()

    def final(self, e, lost):
        p = self.p
        for i in range(1, NZ):
            self.out3(e, i).wait_recv()
        acc = self.Q[e % 3, p.z].astype(f32)
        for i in range(1, NZ):
            acc = acc + self.RZ[e, i - 1].astype(f32)
        acc = acc + lost
        low = acc.astype(bf16)
        self.GF[1 - e // 3, e % 3, pl.ds(pl.multiple_of(p.b * 64, 64), 64), :] = low
        for d in (2, 0, 1):
            self.out4(e, d).start()
        low = low.astype(f32)
        return jnp.sum((low * low).reshape(8, 8, C), axis=0)

    def clear(self, e):
        for i in range(6):
            self.hop(e, i).wait_send()

    def clear_line(self, e):
        for i in range(1, NZ):
            self.out3(e, i).wait_send()

    def end(self, e):
        for d in range(3):
            self.out4(e, d).wait()


class RowSum:
    def __init__(self, p, ref, ssem, rsem):
        self.p, self.ref, self.ssem, self.rsem = p, ref, ssem, rsem

    def eight(self, t, row, i):
        return self.ref.at[t, pl.ds(pl.multiple_of(row + 8 * i, 8), 8), :]

    def hop(self, t, n, src, dst, b, f):
        return remote(src, dst, self.ssem.at[t, n], self.rsem.at[t, n], b, f)

    def three(self, t, n, row):
        rest = self.ref.at[t, row : row + 24, :]
        return self.hop(t, n, rest, rest, self.p.b, self.p.sib)

    def give(self, t):
        p = self.p
        return self.hop(t, 0, self.eight(t, 0, 1 - p.c), self.eight(t, 16, 1 - p.c), p.b, p.sib)

    def along(self, t):
        p = self.p
        self.give(t).wait_recv()
        mine = self.eight(t, 32, p.b)
        mine[...] = self.eight(t, 0, p.c)[...] + self.eight(t, 16, p.c)[...]
        for to in (p.dn, p.xn, p.yn):
            self.hop(t, 1, mine, mine, to, p.f).start()

    def square(self, t):
        p = self.p
        self.three(t, 1, 32).wait_recv()
        mine = self.eight(t, 64, p.z)
        mine[...] = jnp.sum(self.ref[t, 32:64, :].reshape(NB, 8, C), axis=0)
        for i in (2, 1, 3):
            self.hop(t, 2, mine, mine, p.b, 2 * lax.rem(p.z + i, NZ) + p.c).start()

    def back(self, t):
        p = self.p
        mine = self.eight(t, 96, p.c)
        return self.hop(t, 3, mine, mine, p.b, p.sib)

    def close(self, t):
        self.three(t, 2, 64).wait_recv()
        self.eight(t, 96, self.p.c)[...] = jnp.sum(self.ref[t, 64:96, :].reshape(NZ, 8, C), axis=0)
        self.back(t).start()

    def result(self, t):
        self.back(t).wait_recv()
        return self.ref[t, 96:112, :]

    def drain(self, t):
        self.give(t).wait_send()
        self.three(t, 1, 32).wait_send()
        self.three(t, 2, 64).wait_send()
        self.back(t).wait_send()


def conv_back_rows(S, W, k, r0, M):
    acc = None
    for u in range(3):
        lhs = jnp.concatenate([S[2 - u][pl.ds(r0 + (2 - v) * BLK, M), :] for v in range(3)], axis=1)
        rhs = jnp.concatenate(
            [
                W[k, u, z, c, v * 80 : v * 80 + 80, :]
                for v in range(3)
                for z in range(NZ)
                for c in range(2)
            ],
            axis=0,
        )
        d = jnp.dot(lhs, rhs, preferred_element_type=f32)
        acc = d if acc is None else acc + d
    return acc


def own_rows(p, dyT):
    return jnp.concatenate([dyT[z, p.c] for z in range(NZ)], axis=0)


def sib_rows(dyS):
    return jnp.concatenate([dyS[z] for z in range(NZ)], axis=0)


def first_grad(p, S, dyT, acc):
    def tap(v, carry):
        at = pl.ds(pl.multiple_of(v * BLK, BLK), ROWS)
        acc[pl.ds(pl.multiple_of(v * 320, 320), 320), :] = jnp.dot(
            own_rows(p, dyT), S[0][at, :], preferred_element_type=f32
        )
        return carry

    lax.fori_loop(0, 3, tap, 0)


def filter_grad(p, S, S2, dyT, dyS, DS, mu, G, e, acc):
    u = e % 3
    if u == 0:
        ones = jnp.ones((ROWS, 128), bf16)
        DS[...] = jnp.dot(own_rows(p, dyT), ones, preferred_element_type=f32) + jnp.dot(
            sib_rows(dyS), ones, preferred_element_type=f32
        )

    def tap(v, carry):
        at = pl.ds(pl.multiple_of(v * BLK, BLK), ROWS)
        d = jnp.dot(sib_rows(dyS), S2[u, at, :], preferred_element_type=f32)
        if u == 0:
            d = d + acc[pl.ds(pl.multiple_of(v * 320, 320), 320), :]
        else:
            d = d + jnp.dot(own_rows(p, dyT), S[u][at, :], preferred_element_type=f32)
        d = d - jnp.concatenate([DS[...]] * 5, axis=1) * mu
        for z in range(NZ):
            G[u, z, pl.ds(pl.multiple_of(v * 80, 16), 80), :] = d[80 * z : 80 * z + 80].astype(bf16)
        return carry

    lax.fori_loop(0, 3, tap, 0)


def step_kernel(
    images, labels, partner, valid, sizes, stem_w, bridge_t, conv_w, norm, head, bias,
    GF_o, own_o, stem_o, misc_o,
    GF, W, S, S2, S3, dyT, dyS, DS, inner, block, dfl, RX, RZ, G, Q, slots, sibs, lab, few, gath, gathn, par, mask, AB, stem, dstem, pad, pad32,
    xs_, xr_, ps_, pr_, lbs, lbr, gs, gr, zs, zr, xs, xr, ds, dr, ls,
    bs, br, cs, cr, es, er, ts, tr, us, ur, free, fs, fr, os_,
):
    p = Place()
    ex = Exchange(p, slots, sibs, xs_, xr_, ps_, pr_)
    ga = Gather(p, W, zs, zr, xs, xr, ds, dr)
    sc = Scatter(p, W, RX, RZ, G, Q, GF, (bs, br, cs, cr, es, er))
    rs = RowSum(p, few, fs, fr)
    greet(p)
    SA = [S.at[u] for u in range(3)]
    SB = [S.at[0], S.at[1], S3]
    def load(s):
        at = pl.ds(240 * s, 240)
        return pltpu.make_async_copy(conv_w.reshape(1440, C).at[at], block.at[at], ls.at[s])

    for s in range(6):
        load(s).start()
    pad32[...] = jnp.zeros((32, 128), f32)
    pad32[0:16, 0:80] = bridge_t[...]
    pad32[16:26, 0:80] = head[...]
    gath[p.z, p.c] = pad32[...].astype(bf16)
    gathn[p.z, p.c] = jnp.zeros((8, 128), f32)
    gathn[p.z, p.c, 0:6, 0:80] = norm[...]

    def cast(s):
        load(s).wait()
        k, u = s // 3, s % 3
        for v in range(3):
            t = 9 * k + 3 * u + v
            W[k, u, p.z, p.c, 80 * v : 80 * v + 80, :] = block[80 * t : 80 * t + 80, :].astype(bf16)
        W[k, u, p.z, p.c, 240:256, :] = jnp.zeros((16, C), bf16)

    cast(0)
    met()
    for i in (2, 1, 3):
        to = lax.rem(p.z + i, NZ)
        for n, ref in enumerate((gath, gathn)):
            mine = ref.at[p.z, p.c]
            remote(mine, mine, gs.at[n], gr.at[n], p.b, 2 * to + p.c).start()
    ga.zsend(0)
    for s in range(1, 6):
        cast(s)
        if s < 2:
            ga.zsend(s)
    img = pltpu.roll(images[...].astype(f32), 32, 1)
    lane = iota((IMG, 128), 1)
    for c in range(3):
        for i in range(8):
            a = img[:, 1024 * c + 128 * i : 1024 * c + 128 * i + 128]
            if i == 0:
                a = jnp.where(lane < 32, 0.0, a)
            AB[IMG * i : IMG * i + IMG, 128 * c : 128 * c + 128] = a
    tile_c = jnp.bitwise_and(iota((16, 128), 1), 15) == iota((16, 128), 0)
    wc = lax.dot_general(
        stem_w[...].astype(bf16), tile_c.astype(bf16), CC, preferred_element_type=f32
    )
    fold_r = (jnp.bitwise_and(iota((256, 27), 0), 31) == iota((256, 27), 1)).astype(bf16)
    own_j = iota((256, 128), 0) // 32 == iota((256, 128), 1) // 16
    bd = jnp.dot(fold_r, wc.astype(bf16), preferred_element_type=f32)
    bd = jnp.where(own_j, bd, 0.0).astype(bf16)
    l, r = iota((128, 256), 0), iota((128, 256), 1)
    v = jnp.bitwise_and(l, 31) - 4 * (r // 32) + 1

    def hits(c):
        want = 9 * c + 3 * (l // 32) + v
        hit = (l < 96) & (v >= 0) & (v < 3) & (want == jnp.bitwise_and(r, 31))
        return hit.astype(f32)

    acc = None
    for c in range(3):
        t = jnp.dot(hits(c).astype(bf16), bd, preferred_element_type=f32).astype(bf16)
        d = jnp.dot(
            AB[:, 128 * c : 128 * c + 128].astype(bf16), t, preferred_element_type=f32
        )
        acc = d if acc is None else acc + d
    stem[...] = acc.astype(bf16).astype(f32)
    ok = column(valid[...].astype(f32), IMG)
    q = p.f * IMG + iota((IMG, 1), 0)
    member = jnp.zeros((IMG, 1), jnp.int32)
    end = jnp.int32(0)
    for g in range(8):
        end = end + sizes[p.b, g]
        member = member + (q >= end).astype(jnp.int32)
    member = jnp.minimum(member, 7)
    size = jnp.zeros((IMG, 1), f32)
    for g in range(8):
        size = size + jnp.where(member == g, sizes[p.b, g].astype(f32), 0.0)
    weight = ok / size
    mask[...] = jnp.concatenate([jnp.broadcast_to(ok, (IMG, 128))] * 8, axis=0)
    count = 64.0 * jnp.sum(ok)
    own_row = labels[...].astype(f32)
    slot = ex.mine(0)
    slot[5:6, :] = jnp.full((1, 128), count, f32)
    slot[6:7, :] = jnp.concatenate([own_row, jnp.zeros((1, 104), f32)], axis=1)
    slot[7:8, :] = jnp.full((1, 128), jnp.sum(weight), f32)
    edge = jnp.zeros((BLK, C), bf16)
    S3[0:BLK, :] = edge
    S3[9 * BLK : 10 * BLK, :] = edge
    for u in range(3):
        S[u, 0:BLK, :] = edge
        S[u, 9 * BLK : 10 * BLK, :] = edge
        for z in range(NZ):
            G[u, z, 240:256, :] = jnp.zeros((16, C), bf16)
    pairs = []
    for n, ref in enumerate((gath, gathn)):
        rest = ref.at[0 : NZ - 1, 0]
        remote(rest, rest, gs.at[n], gr.at[n], p.b, p.sib).wait()
        side = ref.at[:, p.c]
        pairs.append(remote(side, side, gs.at[2 + n], gr.at[2 + n], p.b, p.sib))
        pairs[n].start()
    for pair in pairs:
        pair.wait()
    lane = iota((40, 128), 1)
    for k in range(5):
        acc = jnp.zeros((40, 128), f32)
        for f in range(NF):
            lo, hi = max(80 * f, 128 * k), min(80 * f + 80, 128 * k + 128)
            if lo < hi:
                low = gath[f // 2, f % 2].astype(f32)
                all_rows = jnp.concatenate([low[0:16], gathn[f // 2, f % 2], low[16:32]], axis=0)
                turned = pltpu.roll(all_rows, (80 * f - 128 * k) % 128, 1)
                acc = jnp.where((lane >= lo - 128 * k) & (lane < hi - 128 * k), turned, acc)
        par[:, 128 * k : 128 * k + 128] = acc
    bridge8 = jnp.concatenate([par[0:16, :].astype(bf16)] * 8, axis=0)

    def rows(j):
        return pl.ds(pl.multiple_of(j * BLK, BLK), BLK)

    def base_rows(j):
        pick = iota((BLK, 128), 1) // 16 == j
        x = jnp.where(pick, stem[...], 0.0).astype(bf16)
        return jnp.dot(x, bridge8, preferred_element_type=f32)

    def base_block(j, carry):
        inner[rows(j), :] = base_rows(j)
        return carry

    lax.fori_loop(0, 8, base_block, 0)
    local_stats(inner, mask, count, ex.mine(0))
    ex.send(0)
    ga.zsend(2)
    ga.relay(0)
    ga.turn(0)
    ga.relay(1)

    def inner_rows(j):
        return inner[rows(j), :]

    def block_rows(j):
        return block[rows(j), :]

    def dfl_rows(j):
        return dfl[rows(j), :]

    def gain(k):
        return par[16 + 2 * k : 17 + 2 * k, :]

    def shift(k):
        return par[17 + 2 * k : 18 + 2 * k, :]

    def normed(src, stats, k, S):
        mean, scale = stats[:2]

        def one(j, acc):
            hat = (src(j) - mean) * scale
            out = jnp.maximum(gain(k) * hat + shift(k), 0.0)
            spread_rows(S, j, out)
            m = jnp.concatenate([mask[...]] * 5, axis=1)
            return acc + jnp.sum((out * m).reshape(BLK // 8, 8, C), axis=0)

        acc = lax.fori_loop(0, 8, one, jnp.zeros((8, C), f32))
        return jnp.sum(acc, axis=0, keepdims=True)

    stats0 = joint_stats(ex, 0)
    labs = remote(lab.at[0], lab.at[1], lbs, lbr, p.b, p.sib)
    lab[0] = slots[0, :, 6, :]
    labs.start()
    put_spare(ex.mine(1), normed(inner_rows, stats0, 0, SA))
    for s in range(3, 6):
        ga.zsend(s)

    def conv(k, u, dst, start, acts):
        def one(it, carry):
            r0 = pl.multiple_of(it * 384, 384)
            at = pl.ds(r0, 384)
            d = conv_part(SB if k else SA, W, k, u, r0, 384)
            dst[at, :] = (dst[at, :] if start is None else start(it)) + d if start != 0 else d
            for when, act in acts.items():
                pl.when(it == when)(act)
            return carry

        lax.fori_loop(0, 4, one, 0)

    def share(u, S=SA):
        return remote(S[u], S2.at[u], ts.at[u], tr.at[u], p.b, p.sib)

    def doing(f, *a):
        return lambda: f(*a)

    ga.relay(2)
    ga.turn(1)
    ga.across(0)
    ga.arrive(0)
    conv(0, 0, inner, 0, {1: doing(ga.turn, 2), 2: doing(ga.relay, 3)})
    ga.across(1)
    ga.across(2)
    ga.arrive(1)
    conv(0, 1, inner, None, {1: doing(ga.relay, 4)})
    ga.arrive(2)
    conv(0, 2, inner, None, {0: doing(ga.turn, 3), 2: doing(ga.relay, 5)})
    ga.turn(4)
    local_stats(inner, mask, count, ex.mine(1))
    ex.send(1)
    ga.across(3)
    ga.turn(5)
    stats1 = joint_stats(ex, 1)
    put_spare(ex.mine(2), normed(inner_rows, stats1, 1, SB))
    ga.arrive(3)
    conv(1, 0, block, lambda it: jnp.concatenate([base_rows(2 * it), base_rows(2 * it + 1)], axis=0),
         {1: doing(ga.across, 4), 3: doing(ga.across, 5)})
    ga.arrive(4)
    for u in range(3):
        share(u, SB).start()
    conv(1, 1, block, None, {})
    ga.arrive(5)
    conv(1, 2, block, None, {})
    local_stats(block, mask, count, ex.mine(2))
    ex.send(2)
    for s in range(6):
        ga.drain(s)
    lane = iota((IMG, 16), 1)
    label = column(own_row, IMG)
    mate = column(partner[...].astype(f32), IMG)
    home = jnp.floor((mate + 0.5) / 24.0)
    chip = jnp.floor((home + 0.5) / 2.0)
    at_chip = (iota((IMG, NCHIP), 1).astype(f32) == chip).astype(bf16)
    labs.wait()
    own_side = jnp.dot(at_chip, lab[0].astype(bf16), preferred_element_type=f32)
    sib_side = jnp.dot(at_chip, lab[1].astype(bf16), preferred_element_type=f32)
    there = jnp.where(home - 2.0 * chip == p.c.astype(f32), own_side, sib_side)
    spot = iota((IMG, 128), 1).astype(f32) == mate - 24.0 * home
    mate_label = jnp.sum(jnp.where(spot, there, 0.0), axis=1, keepdims=True)
    lane_f = lane.astype(f32)
    target = own_share * (lane_f == label).astype(f32) + (1.0 - own_share) * (
        lane_f == mate_label
    ).astype(f32)
    live = lane < 10
    head16 = par[24:40, :].astype(bf16)
    pad[...] = jnp.zeros((8, 128), f32)
    pad[0:1, 0:10] = bias[...]
    sides = sibs[0, 0] + sibs[0, 1]
    total = jnp.sum(sides[7:8, 0:1])
    valid_count = jnp.sum(sides[5:6, 0:1])
    stats2 = joint_stats(ex, 2)
    mu0, mu1 = stats1[2] / valid_count, stats2[2] / valid_count

    def pool(j, acc):
        hat = (block_rows(j) - stats2[0]) * stats2[1]
        out = jnp.maximum(gain(2) * hat + shift(2), 0.0)
        return acc + jnp.sum(out.reshape(8, IMG, C), axis=0)

    pooled = lax.fori_loop(0, 8, pool, jnp.zeros((IMG, C), f32)) / 64.0
    pooled = pooled.astype(bf16)
    logits = lax.dot_general(pooled, head16, AC, preferred_element_type=f32) + pad[0:1, 0:16]
    top = jnp.max(jnp.where(live, logits, -3e38), axis=1, keepdims=True)
    moved = jnp.where(live, logits - top, 0.0)
    size_sum = jnp.sum(jnp.where(live, jnp.exp(moved), 0.0), axis=1, keepdims=True)
    logp = moved - jnp.log(size_sum)
    loss_part = -jnp.sum(
        weight * jnp.sum(jnp.where(live, target * logp, 0.0), axis=1, keepdims=True)
    )
    d_logits = jnp.where(live, (jnp.exp(logp) - target) * (weight / total), 0.0).astype(bf16)
    g_bias = jnp.sum(d_logits.astype(f32), axis=0, keepdims=True)
    few[0, 0:16, :] = lax.dot_general(d_logits, pooled, CC, preferred_element_type=f32)
    rs.give(0).start()
    d_pooled = jnp.dot(d_logits, head16, preferred_element_type=f32)
    d_out24 = d_pooled / 64.0

    def zhat(src, j, stats):
        return (src(j) - stats[0]) * stats[1]

    def passed(hat, k, d_out):
        return jnp.where(gain(k) * hat + shift(k) > 0.0, d_out, 0.0)

    def grad_sums(src, stats, k, d_of, e):
        def one(j, acc):
            hat = zhat(src, j, stats)
            got = passed(hat, k, d_of(j))
            return (
                acc[0] + jnp.sum(got.reshape(BLK // 8, 8, C), axis=0),
                acc[1] + jnp.sum((got * hat).reshape(BLK // 8, 8, C), axis=0),
            )

        zero = jnp.zeros((8, C), f32)
        acc = lax.fori_loop(0, 8, one, (zero, zero))
        put_row(ex.mine(e), 0, jnp.sum(acc[0], axis=0, keepdims=True))
        put_row(ex.mine(e), 8, jnp.sum(acc[1], axis=0, keepdims=True))

    def grad_rows(src, stats, k, d_of, sums, j):
        hat = zhat(src, j, stats)
        m = jnp.concatenate([mask[...]] * 5, axis=1)
        got = passed(hat, k, d_of(j))
        return (gain(k) * stats[1]) * (got - m * (sums[0] + hat * sums[1]) / valid_count)

    def head_rows(j):
        return jnp.concatenate([d_out24] * 8, axis=0)

    def turn(src):
        for it in range(4):
            x = src[384 * it : 384 * it + 384, :].T.astype(bf16)
            for f in range(NF):
                dyT[f // 2, f % 2, :, 384 * it : 384 * it + 384] = x[80 * f : 80 * f + 80]

    trade = remote(dyT.at[:, 1 - p.c], dyS, us, ur, p.b, p.sib)

    grad_sums(block_rows, stats2, 2, head_rows, 3)
    slot = ex.mine(3)
    slot[5:6, :] = jnp.full((1, 128), loss_part, f32)
    slot[6:7, :] = jnp.concatenate([g_bias, jnp.zeros((1, 112), f32)], axis=1)
    ex.send(3)
    tot3 = ex.total(3)
    sums2 = wide(tot3[0:5]), wide(tot3[8:13])

    def low_sums(dst, src, stats, k, d_of, sums):
        def one(j, acc):
            d = grad_rows(src, stats, k, d_of, sums, j)
            dst[rows(j), :] = d
            return acc + jnp.sum(d.astype(bf16).astype(f32).reshape(BLK // 8, 8, C), axis=0)

        acc = lax.fori_loop(0, 8, one, jnp.zeros((8, C), f32))
        return jnp.sum(acc, axis=0, keepdims=True)

    def lost(dy_sums, mu):
        at = 64 * p.b + iota((64, C), 0)
        o = at - 80 * ((at >= 80).astype(jnp.int32) + (at >= 160).astype(jnp.int32))
        hit = (iota((64, C), 1) == 80 * p.f + o) & (at < 240)
        return jnp.sum(jnp.where(hit, dy_sums, 0.0), axis=1, keepdims=True) * mu

    put_spare(ex.mine(4), low_sums(block, block_rows, stats2, 2, head_rows, sums2))
    turn(block)
    trade.start()
    first_grad(p, SB, dyT, dfl)
    for u in range(3):
        share(u, SB).wait()
    trade.wait()
    filter_grad(p, SB, S2, dyT, dyS, DS, mu1, G, 0, dfl)
    sc.begin(0)
    filter_grad(p, SB, S2, dyT, dyS, DS, mu1, G, 1, dfl)
    sc.begin(1)
    rs.along(0)
    def spread(src):
        def one(j, carry):
            spread_rows(SA, j, src[rows(j), :])
            return carry

        lax.fori_loop(0, 8, one, 0)

    spread(block)

    def back_conv1(it, carry):
        r0 = pl.multiple_of(it * 384, 384)
        dfl[pl.ds(r0, 384), :] = conv_back_rows(SA, W, 1, r0, 384)

        @pl.when(it == 0)
        def _():
            sc.mid(0)

        @pl.when(it == 2)
        def _():
            sc.mid(1)

        return carry

    lax.fori_loop(0, 4, back_conv1, 0)
    grad_sums(inner_rows, stats1, 1, dfl_rows, 4)
    ex.send(4)
    sc.along(0)
    filter_grad(p, SB, S2, dyT, dyS, DS, mu1, G, 2, None)
    sc.begin(2)
    rs.square(0)
    pl.semaphore_signal(free, inc=1, device_id=(p.b, p.sib), device_id_type=MESH)
    normed(base_rows, stats0, 0, SA)
    sc.along(1)
    tot4 = ex.total(4)
    pl.semaphore_wait(free, 1)
    share(0).start()
    sums1 = wide(tot4[0:5]), wide(tot4[8:13])
    lost1 = lost(spare(tot4), mu1)
    put_spare(ex.mine(5), low_sums(dfl, inner_rows, stats1, 1, dfl_rows, sums1))
    turn(dfl)
    trade.start()
    for u in range(1, 3):
        share(u).start()
    first_grad(p, SA, dyT, inner)
    sc.mid(2)
    squares = sc.final(0, lost1)
    sc.clear(0)
    share(0).wait()
    trade.wait()
    filter_grad(p, SA, S2, dyT, dyS, DS, mu0, G, 3, inner)
    sc.begin(3)
    rs.close(0)
    sc.clear(1)
    share(1).wait()
    filter_grad(p, SA, S2, dyT, dyS, DS, mu0, G, 4, inner)
    sc.begin(4)
    sc.along(2)
    sc.clear(2)
    share(2).wait()
    filter_grad(p, SA, S2, dyT, dyS, DS, mu0, G, 5, inner)
    sc.mid(3)
    sc.begin(5)
    spread(dfl)

    def back_conv0(it, carry):
        r0 = pl.multiple_of(it * 384, 384)
        inner[pl.ds(r0, 384), :] = conv_back_rows(SA, W, 0, r0, 384)

        @pl.when(it == 1)
        def _():
            sc.mid(4)

        @pl.when(it == 2)
        def _():
            sc.clear_line(0)
            sc.along(3)

        return carry

    lax.fori_loop(0, 4, back_conv0, 0)

    sc.mid(5)
    grad_sums(base_rows, stats0, 0, inner_rows, 5)
    ex.send(5)
    squares = squares + sc.final(1, lost1) + sc.final(2, lost1)
    sc.clear_line(1)
    sc.along(4)
    tot5 = ex.total(5)
    lost0 = lost(spare(tot5), mu0)
    sc.clear_line(2)
    sc.along(5)
    squares = squares + sc.final(3, lost0)
    sums0 = wide(tot5[0:5]), wide(tot5[8:13])
    grid16 = dfl.at[512:640]
    grid16[...] = jnp.zeros((128, C), f32)
    dstem[...] = jnp.zeros((BLK, 128), f32)

    def back0(i, carry):
        total_g, total_s = None, None
        for h in range(4):
            j = 4 * i + h
            d = block[rows(j), :] + grad_rows(base_rows, stats0, 0, inner_rows, sums0, j)
            d = d.astype(bf16)
            pick = iota((BLK, 128), 1) // 16 == j
            x = jnp.where(pick, stem[...], 0.0).astype(bf16)
            g = lax.dot_general(x, d, CC, preferred_element_type=f32)
            y = jnp.where(pick, lax.dot_general(d, bridge8, AC, preferred_element_type=f32), 0.0)
            total_g = g if total_g is None else total_g + g
            total_s = y if total_s is None else total_s + y
        grid16[...] += total_g
        dstem[...] += total_s
        return carry

    lax.fori_loop(0, 2, back0, 0)
    acc = grid16[0:16, :]
    for j in range(1, 8):
        acc = acc + grid16[16 * j : 16 * j + 16, :]
    few[1, 0:16, :] = acc
    rs.give(1).start()
    low = dstem[...].astype(bf16)
    high = lax.Precision.HIGHEST
    acc = None
    for c in range(3):
        t = lax.dot_general(
            AB[:, 128 * c : 128 * c + 128].astype(bf16), low, CC, preferred_element_type=f32
        )
        d = lax.dot_general(hits(c), t, CC, precision=high, preferred_element_type=f32)
        acc = d if acc is None else acc + d
    acc = jnp.where(own_j, acc, 0.0)
    fold = (jnp.bitwise_and(iota((256, 128), 0), 31) == iota((256, 128), 1)).astype(f32)
    acc = lax.dot_general(acc, fold, CC, precision=high, preferred_element_type=f32)
    slots[6, p.chip] = jnp.dot(
        tile_c.astype(f32), acc, precision=high, preferred_element_type=f32
    )
    ex.send(6)
    rs.along(1)
    squares = squares + sc.final(4, lost0)
    rs.square(1)
    g_stem = ex.total(6)
    squares = squares + sc.final(5, lost0)
    slots[7, p.chip] = jnp.full((16, 128), jnp.sum(squares), f32)
    ex.send(7)

    def leave(e):
        at = 1 - e // 3, e % 3
        return pltpu.make_async_copy(GF.at[at], GF_o.at[at], os_.at[e])

    for e in range(4):
        sc.end(e)
        leave(e).start()
    rs.close(1)
    both = jnp.concatenate([rs.result(1), rs.result(0)], axis=0)
    bias_all = tot3[6:7, :]
    stem_o[...] = g_stem
    ng = [row for sums in (sums0, sums1, sums2) for row in (sums[1], sums[0])]
    ng = jnp.concatenate(ng + [jnp.zeros((2, C), f32)], axis=0)
    every = jnp.concatenate([both, ng], axis=0)
    pick = (iota((C, 128), 0) == 80 * p.f + iota((C, 128), 1)) & (iota((C, 128), 1) < 80)
    own_o[...] = jnp.dot(every, pick.astype(f32), precision=high, preferred_element_type=f32)
    other = jnp.sum(every * every) + jnp.sum(g_stem * g_stem) + jnp.sum(bias_all * bias_all)
    conv_sq = ex.total(7)[0:1, :]
    misc_o[...] = jnp.zeros((8, 128), f32)
    misc_o[0:1, :] = jnp.sqrt(conv_sq + other)
    misc_o[1:2, :] = tot3[5:6, :] / total
    misc_o[2:3, :] = bias_all
    for e in range(4, 6):
        sc.end(e)
        leave(e).start()
    for e in range(3, 6):
        sc.clear(e)
        sc.clear_line(e)
    for e in range(8):
        ex.drain(e)
    rs.drain(0)
    rs.drain(1)
    for e in range(6):
        leave(e).wait()


def step_call(images, labels, partner, valid, sizes, stem_w, bridge_t, conv_w, norm, head, bias):
    V, A, SM = pltpu.VMEM, pl.ANY, pltpu.SMEM
    spec = lambda m: pl.BlockSpec(memory_space=m)
    D = pltpu.SemaphoreType.DMA
    sh = jax.ShapeDtypeStruct
    return pl.pallas_call(
        step_kernel,
        out_shape=(
            sh((2, 3, 256, C), bf16), sh((40, 128), f32), sh((16, 128), f32), sh((8, 128), f32),
        ),
        in_specs=[
            spec(V), spec(V), spec(V), spec(V), spec(SM), spec(V), spec(V), spec(A), spec(V), spec(V), spec(V),
        ],
        out_specs=(spec(A),) + (spec(V),) * 3,
        scratch_shapes=[
            V((2, 3, 256, C), bf16), V((2, 3, NZ, 2, 256, C), bf16), V((3, 10 * BLK, C), bf16), V((3, 10 * BLK, C), bf16), V((10 * BLK, C), bf16),
            V((NZ, 2, 80, ROWS), bf16), V((NZ, 80, ROWS), bf16), V((NZ * 80, 128), f32),
            V((ROWS, C), f32), V((ROWS, C), f32), V((ROWS, C), f32),
            V((3, 3, 256, C), bf16), V((6, 3, 64, C), LINE), V((3, NZ, 256, C), bf16), V((3, NZ, 64, C), LINE),
            V((8, NCHIP, 16, 128), f32), V((8, 2, 16, 128), f32), V((2, NCHIP, 128), f32), V((2, 112, C), f32), V((NZ, 2, 32, 128), bf16), V((NZ, 2, 8, 128), f32), V((40, C), f32),
            V((BLK, 128), f32), V((BLK, 384), f32), V((BLK, 128), f32), V((BLK, 128), f32), V((8, 128), f32), V((32, 128), f32),
            D((8,)), D((8,)), D((8,)), D((8,)), D, D, D((4,)), D((4,)), D((6, 4)), D((6, 4)), D((6, 12)), D((6, 12)), D((6,)), D((6,)), D((6,)),
            D((6, 6)), D((6, 6)), D((6, 3)), D((6, 3)), D((6, 3)), D((6, 3)), D((3,)), D((3,)), D, D,
            pltpu.SemaphoreType.REGULAR, D((2, 4)), D((2, 4)), D((6,)),
        ],
        compiler_params=pltpu.CompilerParams(
            collective_id=0, has_side_effects=True, vmem_limit_bytes=63 << 20
        ),
    )(images, labels, partner, valid, sizes, stem_w, bridge_t, conv_w, norm, head, bias)


def adam_rule(g, w, m, v, rate, shrink, factor):
    clipped = g * factor
    m = beta_one * m + (1.0 - beta_one) * clipped
    v = beta_two * v + (1.0 - beta_two) * clipped * clipped
    ahead = m / (1.0 - beta_one**STEP)
    behind = v / (1.0 - beta_two**STEP)
    return w - rate * (ahead / (jnp.sqrt(behind) + adam_eps) + shrink * w), m, v


def adam_kernel(G, misc, own, stem_g, *refs):
    ins, outs, (norm_o, loss_o, held, GV, lsem, osem, gsem) = refs[:18], refs[18:36], refs[36:]
    norm_o[...] = misc[0:1, 0:1]
    loss_o[...] = misc[1:2, 0:1]
    factor = clip_norm / jnp.maximum(misc[0:1, :], clip_norm)
    wide_factor = jnp.concatenate([factor] * 5, axis=1)

    def load(s, i):
        return pltpu.make_async_copy(ins[i].at[s // 3, s % 3], held.at[i, s], lsem.at[i, s])

    def store(s, i):
        return pltpu.make_async_copy(held.at[i, s], outs[i].at[s // 3, s % 3], osem.at[i, s])

    def grad(s):
        return pltpu.make_async_copy(G.at[s // 3, s % 3], GV.at[s], gsem.at[s])

    for s in range(6):
        grad(s).start()
        for i in range(3):
            load(s, i).start()

    def write(i, g, rate, shrink, f):
        w, m, v = (r[...] for r in ins[3 * i : 3 * i + 3])
        for o, x in zip(outs[3 * i : 3 * i + 3], adam_rule(g, w, m, v, rate, shrink, f)):
            o[...] = x

    write(1, stem_g[:, 0:27], 0.5, 0.05, factor[:, 0:27])
    write(2, own[0:16, 0:80], 0.6, 0.05, factor[:, 0:80])
    write(3, own[32:38, 0:80], 0.5, 0.0, factor[:, 0:80])
    write(4, own[16:26, 0:80], 0.1, 0.05, factor[:, 0:80])
    write(5, misc[2:3, 0:10], 0.5, 0.0, factor[:, 0:10])
    for s in range(6):
        for i in range(3):
            load(s, i).wait()
        grad(s).wait()

        def part(j, carry):
            at = pl.ds(pl.multiple_of(j * 48, 16), 48)
            new = adam_rule(
                GV[s, at, :].astype(f32), held[0, s, at, :], held[1, s, at, :], held[2, s, at, :],
                0.033, 0.05, wide_factor,
            )
            for i in range(3):
                held[i, s, at, :] = new[i]
            return carry

        lax.fori_loop(0, 5, part, 0)
        for i in range(3):
            store(s, i).start()
    for s in range(6):
        for i in range(3):
            store(s, i).wait()


def adam_call(G, misc, own, stem_g, *state):
    V, A, D = pltpu.VMEM, pl.ANY, pltpu.SemaphoreType.DMA
    spec = lambda m: pl.BlockSpec(memory_space=m)
    return pl.pallas_call(
        adam_kernel,
        out_shape=tuple(jax.ShapeDtypeStruct(s, f32) for s in [x.shape for x in state] + [(1, 1)] * 2),
        in_specs=[spec(A)] + [spec(V)] * 3 + [spec(A)] * 3 + [spec(V)] * 15,
        out_specs=tuple([spec(A)] * 3 + [spec(V)] * 17),
        scratch_shapes=[V((3, 6, 240, C), f32), V((6, 256, C), bf16), D((3, 6)), D((3, 6)), D((6,))],
        compiler_params=pltpu.CompilerParams(vmem_limit_bytes=62 << 20),
    )(G, misc, own, stem_g, *state)


def make_patches(images):
    number = images.shape[0]
    grid = images.reshape(number, 3, 32, 32)
    padded = jnp.pad(grid, ((0, 0), (0, 0), (1, 1), (1, 1)))
    pieces = [
        padded[:, :, row_off : row_off + 29 : 4, col_off : col_off + 29 : 4]
        for row_off in range(3)
        for col_off in range(3)
    ]
    stacked = jnp.stack(pieces, axis=2)
    return jnp.transpose(stacked, (1, 2, 0, 3, 4)).reshape(27, number * 64)


def shifted(feature_field):
    width, rows = feature_field.shape
    grid = feature_field.reshape(width, rows // 64, 8, 8)
    padded = jnp.pad(grid, ((0, 0), (0, 0), (1, 1), (1, 1)))
    pieces = [
        padded[:, :, row_off : row_off + 8, col_off : col_off + 8]
        for row_off in range(3)
        for col_off in range(3)
    ]
    return jnp.stack(pieces, axis=0).reshape(9 * width, rows)


def unshifted(parts, width):
    rows = parts.shape[1]
    grid = parts.reshape(9, width, rows // 64, 8, 8)
    summed = jnp.zeros((width, rows // 64, 10, 10), jnp.float32)
    for row_off in range(3):
        for col_off in range(3):
            summed = summed + jnp.pad(
                grid[3 * row_off + col_off],
                ((0, 0), (0, 0), (row_off, 2 - row_off), (col_off, 2 - col_off)),
            )
    return summed[:, :, 1:9, 1:9].reshape(width, rows)


def image_weights(valid_mask, group_sizes):
    shards, groups = group_sizes.shape
    capacity = valid_mask.shape[0] // shards
    group_ends = jnp.cumsum(group_sizes, axis=1)
    slot_index = jnp.arange(capacity, dtype=jnp.int32)
    member = jnp.sum(
        (slot_index[None, :, None] >= group_ends[:, None, :]).astype(jnp.int32), axis=2
    )
    member = jnp.minimum(member, groups - 1)
    chosen = (member[:, :, None] == jnp.arange(groups, dtype=jnp.int32)[None, None, :]).astype(
        jnp.float32
    )
    sizes_each = jnp.sum(chosen * group_sizes[:, None, :].astype(jnp.float32), axis=2)
    return valid_mask.astype(jnp.float32) / sizes_each.reshape(-1)


def norm_forward(feature_field, norm_gain, norm_shift, row_validity_mask, valid_count):
    batch_mean = (
        lax.psum(jnp.sum(feature_field * row_validity_mask, axis=1), ("batch", "filt"))
        / valid_count
    )
    centered_input = feature_field - batch_mean[:, None]
    batch_variance = (
        lax.psum(
            jnp.sum(centered_input * centered_input * row_validity_mask, axis=1), ("batch", "filt")
        )
        / valid_count
    )
    inverse_scale = lax.rsqrt(batch_variance + norm_epsilon)
    normalized_input = (feature_field - batch_mean[:, None]) * inverse_scale[:, None]
    norm_output = jnp.maximum(norm_gain[:, None] * normalized_input + norm_shift[:, None], 0.0)
    return (norm_output, normalized_input, inverse_scale)


def masked_norm_backward(
    output_gradient,
    norm_output,
    normalized_input,
    inverse_scale,
    norm_gain,
    row_validity_mask,
    valid_count,
):
    passed_rows = jnp.where(norm_output > 0.0, output_gradient, 0.0)
    shift_gradient, gain_gradient = lax.psum(
        (jnp.sum(passed_rows, axis=1), jnp.sum(passed_rows * normalized_input, axis=1)),
        ("batch", "filt"),
    )
    input_gradient = (
        passed_rows
        - row_validity_mask[None, :]
        * (shift_gradient[:, None] + normalized_input * gain_gradient[:, None])
        / valid_count
    )
    return ((norm_gain * inverse_scale)[:, None] * input_gradient, gain_gradient, shift_gradient)


def conv_forward(feature_field, weight_shard):
    stacked = shifted(feature_field)
    low_shard = weight_shard.astype(jnp.bfloat16)
    piece = lax.all_gather(low_shard, "filt", axis=0, tiled=True)
    norm_output = jnp.dot(
        piece.reshape(piece.shape[0], -1), stacked, preferred_element_type=jnp.float32
    )
    return (norm_output, None)


def conv_backward(feature_field, weight_shard, output_gradient):
    width = feature_field.shape[0]
    stacked = shifted(feature_field)
    rows_grad = output_gradient
    term = lax.dot_general(
        rows_grad, stacked, (((1,), (1,)), ((), ())), preferred_element_type=jnp.float32
    )
    weight_grad = lax.psum_scatter(
        term.reshape(lax.axis_size("filt") * weight_shard.shape[0], 9, width),
        "filt",
        scatter_dimension=0,
        tiled=True,
    )
    piece = lax.all_gather(weight_shard.astype(jnp.bfloat16), "filt", axis=0, tiled=True)
    rows_grad = output_gradient
    back = lax.dot_general(
        piece.reshape(piece.shape[0], -1),
        rows_grad,
        (((0,), (0,)), ((), ())),
        preferred_element_type=jnp.float32,
    )
    return (unshifted(back, width), weight_grad)


def adam_step(weight, output_gradient, first, second, rate, shrink, factor):
    clipped = output_gradient * factor
    first = beta_one * first + (1.0 - beta_one) * clipped
    second = beta_two * second + (1.0 - beta_two) * clipped * clipped
    ahead = first / (1.0 - beta_one**STEP)
    behind = second / (1.0 - beta_two**STEP)
    return (
        weight - rate * (ahead / (jnp.sqrt(behind) + adam_eps) + shrink * weight),
        first,
        second,
    )


def body(
    images,
    labels,
    partner,
    valid_mask,
    group_sizes,
    stem_weight,
    bridge_weight,
    conv_weight,
    norm_params,
    head_weight,
    head_bias,
    stem_first,
    stem_second,
    bridge_first,
    bridge_second,
    conv_first,
    conv_second,
    norm_first,
    norm_second,
    head_first,
    head_second,
    bias_first,
    bias_second,
):
    width = bridge_weight.shape[0]
    bridge_all, norm_all, head_all = (
        lax.all_gather(bridge_weight, "filt", axis=0, tiled=True),
        lax.all_gather(norm_params, "filt", axis=1, tiled=True),
        lax.all_gather(head_weight, "filt", axis=1, tiled=True),
    )
    labels_all, valid_all = (
        lax.all_gather(labels, ("batch", "filt"), axis=0, tiled=True),
        lax.all_gather(valid_mask, ("batch", "filt"), axis=0, tiled=True),
    )
    weight_all = image_weights(valid_all, group_sizes)
    total = jnp.sum(weight_all)
    valid_count = 64.0 * jnp.sum(valid_all.astype(jnp.float32))
    local = images.shape[0]
    image_weight = lax.dynamic_slice_in_dim(
        weight_all, lax.axis_index(("batch", "filt")) * local, local
    )
    row_validity_mask = jnp.repeat(valid_mask.astype(jnp.float32), 64)
    patch = make_patches(images)
    stem = jnp.dot(
        stem_weight.astype(jnp.bfloat16), patch, preferred_element_type=jnp.float32
    ).astype(jnp.bfloat16)
    base = jnp.dot(bridge_all.astype(jnp.bfloat16), stem, preferred_element_type=jnp.float32)
    first, first_hat, first_scale = norm_forward(
        base, norm_all[0], norm_all[1], row_validity_mask, valid_count
    )
    first_low = first.astype(jnp.bfloat16)
    inner, kept_zero = conv_forward(first_low, conv_weight[0])
    second, second_hat, second_scale = norm_forward(
        inner, norm_all[2], norm_all[3], row_validity_mask, valid_count
    )
    second_low = second.astype(jnp.bfloat16)
    branch, kept_one = conv_forward(second_low, conv_weight[1])
    final, final_hat, final_scale = norm_forward(
        base + branch, norm_all[4], norm_all[5], row_validity_mask, valid_count
    )
    pooled = jnp.mean(final.reshape(final.shape[0], local, 64), axis=2).astype(jnp.bfloat16)
    logits = (
        jnp.dot(head_all.astype(jnp.bfloat16), pooled, preferred_element_type=jnp.float32)
        + head_bias[:, None]
    )
    moved = logits - jnp.max(logits, axis=0, keepdims=True)
    logp = moved - jnp.log(jnp.sum(jnp.exp(moved), axis=0, keepdims=True))
    classes = jnp.arange(logits.shape[0], dtype=jnp.int32)
    partner_labels = jnp.take(labels_all, partner)
    target = own_share * (labels[None, :] == classes[:, None]).astype(jnp.float32) + (
        1.0 - own_share
    ) * (partner_labels[None, :] == classes[:, None]).astype(jnp.float32)
    loss_part = -jnp.sum(image_weight * jnp.sum(target * logp, axis=0))
    d_logits = ((jnp.exp(logp) - target) * (image_weight / total)[None, :]).astype(jnp.bfloat16)
    bias_grad = jnp.sum(d_logits.astype(jnp.float32), axis=1)
    head_grad = lax.dot_general(
        d_logits, pooled, (((1,), (1,)), ((), ())), preferred_element_type=jnp.float32
    )
    d_pooled = lax.dot_general(
        head_all.astype(jnp.bfloat16),
        d_logits,
        (((0,), (0,)), ((), ())),
        preferred_element_type=jnp.float32,
    )
    d_final = jnp.repeat(d_pooled / 64.0, 64, axis=1)
    d_block, gain_two, shift_two = masked_norm_backward(
        d_final, final, final_hat, final_scale, norm_all[4], row_validity_mask, valid_count
    )
    d_second, conv_grad_one = conv_backward(
        second_low, conv_weight[1], d_block.astype(jnp.bfloat16)
    )
    d_inner, gain_one, shift_one = masked_norm_backward(
        d_second, second, second_hat, second_scale, norm_all[2], row_validity_mask, valid_count
    )
    d_first, conv_grad_zero = conv_backward(first_low, conv_weight[0], d_inner.astype(jnp.bfloat16))
    d_lower, gain_zero, shift_zero = masked_norm_backward(
        d_first, first, first_hat, first_scale, norm_all[0], row_validity_mask, valid_count
    )
    d_base = (d_block + d_lower).astype(jnp.bfloat16)
    bridge_grad = lax.dot_general(
        d_base, stem, (((1,), (1,)), ((), ())), preferred_element_type=jnp.float32
    )
    d_stem = lax.dot_general(
        bridge_all.astype(jnp.bfloat16),
        d_base,
        (((0,), (0,)), ((), ())),
        preferred_element_type=jnp.float32,
    ).astype(jnp.bfloat16)
    stem_grad = lax.dot_general(
        d_stem, patch, (((1,), (1,)), ((), ())), preferred_element_type=jnp.float32
    )
    bridge_part, head_part = (
        lax.psum_scatter(bridge_grad, "filt", scatter_dimension=0, tiled=True),
        lax.psum_scatter(head_grad, "filt", scatter_dimension=1, tiled=True),
    )
    conv_grad, bridge_sum, head_sum = lax.psum(
        (jnp.stack([conv_grad_zero, conv_grad_one]), bridge_part, head_part), "batch"
    )
    stem_sum, bias_sum, loss_sum = lax.psum((stem_grad, bias_grad, loss_part), ("batch", "filt"))
    norm_full = jnp.stack([gain_zero, shift_zero, gain_one, shift_one, gain_two, shift_two])
    norm_grad = lax.dynamic_slice_in_dim(norm_full, lax.axis_index("filt") * width, width, 1)
    owned_square = (
        jnp.sum(conv_grad * conv_grad)
        + jnp.sum(bridge_sum * bridge_sum)
        + jnp.sum(norm_grad * norm_grad)
        + jnp.sum(head_sum * head_sum)
    )
    squares_all = (
        lax.psum(owned_square, "filt") + jnp.sum(stem_sum * stem_sum) + jnp.sum(bias_sum * bias_sum)
    )
    grad_norm = jnp.sqrt(squares_all)
    factor = clip_norm / jnp.maximum(grad_norm, clip_norm)
    stem_new = adam_step(stem_weight, stem_sum, stem_first, stem_second, 0.5, 0.05, factor)
    bridge_new = adam_step(
        bridge_weight, bridge_sum, bridge_first, bridge_second, 0.6, 0.05, factor
    )
    conv_new = adam_step(conv_weight, conv_grad, conv_first, conv_second, 0.033, 0.05, factor)
    norm_new = adam_step(norm_params, norm_grad, norm_first, norm_second, 0.5, 0.0, factor)
    head_new = adam_step(head_weight, head_sum, head_first, head_second, 0.1, 0.05, factor)
    bias_new = adam_step(head_bias, bias_sum, bias_first, bias_second, 0.5, 0.0, factor)
    return (
        stem_new[0],
        stem_new[1],
        stem_new[2],
        bridge_new[0],
        bridge_new[1],
        bridge_new[2],
        conv_new[0],
        conv_new[1],
        conv_new[2],
        norm_new[0],
        norm_new[1],
        norm_new[2],
        head_new[0],
        head_new[1],
        head_new[2],
        bias_new[0],
        bias_new[1],
        bias_new[2],
        grad_norm,
        loss_sum / total,
    )


def fast_body(
    images, labels, partner, valid_mask, group_sizes, stem_weight, bridge_weight, conv_weight, norm_params,
    head_weight, head_bias, stem_first, stem_second, bridge_first, bridge_second, conv_first, conv_second,
    norm_first, norm_second, head_first, head_second, bias_first, bias_second,
):
    width = bridge_weight.shape[0]
    def rows(x):
        return x.transpose(0, 2, 1, 3).reshape(2, 3, 3 * width, C)

    def back(x):
        return x.reshape(2, 9, width, C).transpose(0, 2, 1, 3)

    G, own, stem_g, misc = step_call(
        images, labels[None], partner[None], valid_mask[None], group_sizes, stem_weight, bridge_weight.T,
        conv_weight.transpose(0, 2, 1, 3), norm_params, head_weight, head_bias[None],
    )
    new = adam_call(
        G, misc, own, stem_g,
        rows(conv_weight), rows(conv_first), rows(conv_second),
        stem_weight, stem_first, stem_second,
        bridge_weight.T, bridge_first.T, bridge_second.T,
        norm_params, norm_first, norm_second,
        head_weight, head_first, head_second,
        head_bias[None], bias_first[None], bias_second[None],
    )
    conv, stem, bridge, norm, head, bias = (new[i : i + 3] for i in range(0, 18, 3))
    return (
        *stem,
        *(x.T for x in bridge),
        *(back(x) for x in conv),
        *norm,
        *head,
        *(x[0] for x in bias),
        new[18].reshape(()),
        new[19].reshape(()),
    )


def solution(mesh):
    in_specs = (
        P(("batch", "filt"), None),
        P(("batch", "filt")),
        P(("batch", "filt")),
        P(("batch", "filt")),
        P(),
        P(),
        P("filt", None),
        P(None, "filt", None, None),
        P(None, "filt"),
        P(None, "filt"),
        P(),
        P(),
        P(),
        P("filt", None),
        P("filt", None),
        P(None, "filt", None, None),
        P(None, "filt", None, None),
        P(None, "filt"),
        P(None, "filt"),
        P(None, "filt"),
        P(None, "filt"),
        P(),
        P(),
    )
    out_specs = (
        P(),
        P(),
        P(),
        P("filt", None),
        P("filt", None),
        P("filt", None),
        P(None, "filt", None, None),
        P(None, "filt", None, None),
        P(None, "filt", None, None),
        P(None, "filt"),
        P(None, "filt"),
        P(None, "filt"),
        P(None, "filt"),
        P(None, "filt"),
        P(None, "filt"),
        P(),
        P(),
        P(),
        P(),
        P(),
    )
    fits = mesh.shape["batch"] == NB and mesh.shape["filt"] == NF
    return jax.shard_map(fast_body if fits else body, mesh=mesh, in_specs=in_specs, out_specs=out_specs, check_vma=False)
```
